32 devices in a mesh: ctx: 8 (over z, y), wsh: 4 (over x, core).
Axes of the slice: x: 2, y: 2, z: 4, core: 2. Of those that a mesh axis runs over, the one named last changes fastest.
Arguments:
- tokens: bfloat16 [8, 1024, 1024], P('wsh', 'ctx'), may hold values from -6 to 6
- routes: int32 [8, 1024, 8], P('wsh', 'ctx'), may hold values from 0 to 31, all different within a row; in each aligned block of 128 rows (0 to 127, 128 to 255, ..., all dimensions but the last counted through in order) at most 48 rows name the same one
- in_weight: bfloat16 [1024, 2048], replicated, may hold values from -0.1875 to 0.1875
- out_weight: bfloat16 [1024, 1024], replicated, may hold values from -0.75 to 0.75
- first_gain: float32 [1024], replicated, may hold values from 0.5 to 1.5
- second_gain: float32 [1024], replicated, may hold values from 0.5 to 1.5
- router_weight: bfloat16 [1024, 32], replicated, may hold values from -0.1875 to 0.1875
- gate_weight: bfloat16 [32, 1024, 512], P('ctx', None, 'wsh'), may hold values from -0.1875 to 0.1875
- up_weight: bfloat16 [32, 1024, 512], P('ctx', None, 'wsh'), may hold values from -0.1875 to 0.1875
- down_weight: bfloat16 [32, 512, 1024], P('ctx', 'wsh'), may hold values from -0.75 to 0.75
- cotangent: bfloat16 [8, 1024, 1024], P('wsh', 'ctx'), may hold values from -6 to 6
Outputs:
- layer_out: bfloat16 [8, 1024, 1024], P('wsh', 'ctx')
- tokens_grad: bfloat16 [8, 1024, 1024], P('wsh', 'ctx')
- in_grad: float32 [1024, 2048], P(('ctx', 'wsh'))
- out_grad: float32 [1024, 1024], P(('ctx', 'wsh'))
- first_gain_grad: float32 [1024], P(('ctx', 'wsh'))
- second_gain_grad: float32 [1024], P(('ctx', 'wsh'))
- router_grad: float32 [1024, 32], P(('ctx', 'wsh'))
- gate_grad: float32 [32, 1024, 512], P('ctx', None, 'wsh')
- up_grad: float32 [32, 1024, 512], P('ctx', None, 'wsh')
- down_grad: float32 [32, 512, 1024], P('ctx', 'wsh')
The draws below stay inside these ranges and needn't reach their ends.
Inputs may be any that keep to these rules, and one draw needn't show every extreme that they name: `routes`: in each aligned block of 128 rows (one sequence's rows on one index of ctx) the 8 experts of a row differ, and no expert is named by more than 48 rows of the block; some block reaches 48.
All inputs are finite; a program needn't handle non-finite values.
Results may differ from the reference program's by a relative error of at most 0.018.
Values may be sent and summed in bfloat16 or wider, within the bound.
No kernel may reach another device: no remote copies, remote signals or barrier semaphores. Data moves between devices by JAX's collectives and lax.ppermute only.
A program may use at most 256 MiB of HBM per device.

```python
import math
import jax
import jax.numpy as jnp
import numpy as np
from jax import lax

D = 1024
HEADS = 16
KV_HEADS = 8
HEAD_DIM = 64
EXPERTS = 32
FF = 512
TOP = 8
SEQ_TOK = 128
LEN = 1024
SEQS = 8
HALF = 64
MOST = 48
QKV = 2048
N_CTX = 8


def levels(own_key, shape, split, smallest, high):
    level, own = 1.0, jax.random.fold_in(own_key, 6)
    for dim, shards_of in split:
        draws = jnp.exp(jax.random.uniform(jax.random.fold_in(own, dim), (shards_of,), jnp.float32, smallest / len(split), high / len(split)))
        level = level * jnp.repeat(draws, shape[dim] // shards_of).reshape([-1 if axis == dim else 1 for axis in range(len(shape))])
    return level


def deal_out(rng, own, number, rows, amount, top, reach, skew):
    sequence = jax.random.permutation(rng, amount)
    packed, common = load_shares(amount, rows * top, reach, skew, True), load_shares(amount, rows * top, reach, skew, False)
    places = jnp.arange(amount)

    def named(sizes, rotation):
        used = int((sizes > 0).sum())
        fixed = max(1, used // 4)
        passed = fixed + (places - fixed + rotation * (used - fixed)) % max(1, amount - fixed)
        return jnp.zeros((amount,), jnp.int32).at[sequence[jnp.where(places < fixed, places, passed)]].set(jnp.asarray(sizes, jnp.int32))

    sizes = jnp.where(number % 4 == 0, named(packed, number // 4), named(common, number - number // 4 - 1))
    mixed = jax.random.permutation(jax.random.fold_in(own, 3), amount)
    source_of, taker = mixed[0:amount // 2 * 2:2], mixed[1:amount // 2 * 2:2]
    room = jnp.minimum(sizes[source_of] - 1, reach - sizes[taker]) // 2
    room = jnp.where((source_of == sequence[0]) | (taker == sequence[0]) | (sizes[taker] == 0), 0, jnp.maximum(room, 0))
    passed = jax.random.randint(jax.random.fold_in(own, 4), (amount // 2,), 0, 1 << 20) % (room + 1)
    sizes = sizes.at[source_of].add(-passed).at[taker].add(passed)
    members = jnp.searchsorted(jnp.cumsum(sizes), jnp.arange(rows * top), side="right").astype(jnp.int32)
    grid = members.reshape(top, rows).T
    grid = grid[jax.random.permutation(jax.random.fold_in(own, 1), rows)]
    rotation = jax.random.randint(jax.random.fold_in(own, 2), (rows, 1), 0, top)
    return jnp.take_along_axis(grid, (jnp.arange(top)[None, :] + rotation) % top, axis=1)


def load_shares(count, total, bound, lean, full):
    loads = [(1 << 20) // math.isqrt(rank ** lean) + 1 for rank in range(1, count + 1)]
    largest = bound if full else min(bound, max(-(-total // count), total * loads[0] // sum(loads)))
    least = 1 if total - largest >= count - 1 else 0
    given, spare = [largest] + [least] * (count - 1), total - largest - least * (count - 1)
    while spare > 0:
        candidates = [i for i in range(1, count) if given[i] < largest] or [i for i in range(1, count) if given[i] < bound]
        mass, remaining = sum([loads[i] for i in candidates]), spare
        for i in candidates:
            more = min(bound - given[i], max(1, remaining * loads[i] // mass), spare)
            given[i] = given[i] + more
            spare = spare - more
    return np.array(given)


def bell_draw(rng, shape, width, limit, cuts=(), kind=jnp.bfloat16):
    result = jax.random.normal(rng, shape, jnp.float32) * width
    if len(cuts) > 0:
        result = levels(rng, shape, cuts, -0.22, 0.18) * result
    return jnp.clip(result, min=-limit, max=limit).astype(kind)


def setup_inputs(seed: int = 0) -> dict:
    arg_keys = jax.random.split(jax.random.key(seed), 12)
    tokens = bell_draw(arg_keys[0], (SEQS, LEN, D), 1.0, 6.0, ((0, 4), (1, 8)))
    routes_keys = jax.random.split(jax.random.fold_in(arg_keys[1], 1), SEQS * LEN // SEQ_TOK)
    routes_turns = jax.random.permutation(jax.random.fold_in(arg_keys[1], 3), SEQS * LEN // SEQ_TOK)
    routes = jax.vmap(lambda own, number: deal_out(jax.random.fold_in(arg_keys[1], 2), own, number, SEQ_TOK, EXPERTS, TOP, MOST, 1))(routes_keys, routes_turns).reshape((SEQS, LEN, TOP))
    in_weight = bell_draw(arg_keys[2], (D, QKV), D ** -0.5, 0.1875)
    out_weight = bell_draw(arg_keys[3], (HEADS * HEAD_DIM, D), (HEADS * HEAD_DIM // 16) ** -0.5, 0.75)
    first_gain = jnp.clip(jax.random.uniform(arg_keys[4], (D,), jnp.float32, 0.5, 1.5), 0.5, 1.5)
    second_gain = jnp.clip(jax.random.uniform(arg_keys[5], (D,), jnp.float32, 0.5, 1.5), 0.5, 1.5)
    router_weight = bell_draw(arg_keys[6], (D, EXPERTS), D ** -0.5, 0.1875)
    gate_weight = bell_draw(arg_keys[7], (EXPERTS, D, FF), D ** -0.5, 0.1875, ((0, 8), (2, 4)))
    up_weight = bell_draw(arg_keys[8], (EXPERTS, D, FF), D ** -0.5, 0.1875, ((0, 8), (2, 4)))
    down_weight = bell_draw(arg_keys[9], (EXPERTS, FF, D), (FF // 8) ** -0.5, 0.75, ((0, 8), (1, 4)))
    cotangent = bell_draw(arg_keys[10], (SEQS, LEN, D), 1.0, 6.0, ((0, 4), (1, 8)))
    return {"tokens": tokens, "routes": routes, "in_weight": in_weight, "out_weight": out_weight, "first_gain": first_gain, "second_gain": second_gain, "router_weight": router_weight, "gate_weight": gate_weight, "up_weight": up_weight, "down_weight": down_weight, "cotangent": cotangent}


EPS = 1e-05
THETA = 10000.0
NEG = -1e+30

@jax.custom_vjp
def low(v):
    return lax.optimization_barrier(v.astype(jnp.bfloat16)).astype(jnp.float32)

@jax.custom_vjp
def low_back(v):
    return v

def low_keep(v):
    return (low(v), None)

def low_pass(kept, grad):
    return (grad,)

def back_keep(v):
    return (v, None)

def back_low(kept, grad):
    return (low(grad),)
low.defvjp(low_keep, low_pass)
low_back.defvjp(back_keep, back_low)

def dealt(rows, length):
    owner = rows // SEQ_TOK
    offset = rows % SEQ_TOK
    early = owner * HALF + offset
    late = length - (owner + 1) * HALF + offset - HALF
    return jnp.where(offset < HALF, early, late).astype(jnp.int32)

def rotate(values, place, sign):
    half_dim = values.shape[-1] // 2
    freq = THETA ** (-2.0 * jnp.arange(half_dim, dtype=jnp.float32) / values.shape[-1])
    angle = place.astype(jnp.float32)[:, None] * freq[None, :]
    cosine = jnp.cos(angle)[:, None, :]
    sine = sign * jnp.sin(angle)[:, None, :]
    front = values[..., :half_dim]
    back = values[..., half_dim:]
    return jnp.concatenate([front * cosine - back * sine, back * cosine + front * sine], -1)

def rms_norm(values, gain):
    return values * lax.rsqrt(lax.optimization_barrier(jnp.mean(values * values, -1, keepdims=True)) + EPS) * gain

def highest(form, left, right):
    return jnp.einsum(form, left, right, precision=lax.Precision.HIGHEST)

def sequence_layer(params, tokens, routes):
    in_weight, out_weight, first_gain, second_gain, router_weight, gate_weight, up_weight, down_weight = params
    place = dealt(jnp.arange(LEN, dtype=jnp.int32), LEN)
    width_q = HEADS * HEAD_DIM
    width_k = KV_HEADS * HEAD_DIM
    group = HEADS // KV_HEADS
    normed = low(rms_norm(tokens, first_gain))
    mixed = jnp.dot(normed, in_weight, precision=lax.Precision.HIGHEST)
    query = low(rotate(low_back(mixed[:, :width_q]).reshape(LEN, HEADS, HEAD_DIM), place, 1.0))
    key = low(rotate(low_back(mixed[:, width_q:width_q + width_k]).reshape(LEN, KV_HEADS, HEAD_DIM), place, 1.0))
    value = low_back(low(mixed[:, width_q + width_k:])).reshape(LEN, KV_HEADS, HEAD_DIM)
    query = query.reshape(LEN, KV_HEADS, group, HEAD_DIM)
    scores = low_back(highest('qngd,knd->ngqk', query, key) * HEAD_DIM ** (-0.5))
    allowed = place[None, :] <= place[:, None]
    probs = low(jax.nn.softmax(jnp.where(allowed, scores, NEG), -1))
    attended = low_back(low(highest('ngqk,knd->qngd', probs, value).reshape(LEN, width_q)))
    resid = tokens + low_back(jnp.dot(attended, out_weight, precision=lax.Precision.HIGHEST))
    normed_two = low(rms_norm(resid, second_gain))
    logits = low_back(jnp.dot(normed_two, router_weight, precision=lax.Precision.HIGHEST))
    gates = low(jax.nn.softmax(jnp.take_along_axis(logits, routes, axis=1), -1))
    counts = (routes.reshape(N_CTX, SEQ_TOK * TOP)[..., None] == jnp.arange(EXPERTS, dtype=jnp.int32)).astype(jnp.int32)
    ranks = lax.optimization_barrier(jnp.sum((jnp.cumsum(counts, 1) - 1) * counts, -1)).reshape(LEN, TOP)
    owner = (jnp.arange(LEN, dtype=jnp.int32) // SEQ_TOK)[:, None]
    slots = ((owner * MOST + ranks) * EXPERTS + routes).reshape(-1).astype(jnp.int32)
    total_slots = N_CTX * MOST * EXPERTS
    sources = jnp.repeat(jnp.arange(LEN, dtype=jnp.int32), TOP)
    table = jnp.full((total_slots,), LEN, jnp.int32).at[slots].set(sources)
    padded = jnp.concatenate([normed_two, jnp.zeros((1, D), normed_two.dtype)], 0)
    sent = low_back(jnp.take(padded, table, axis=0)).reshape(N_CTX * MOST, EXPERTS, D)
    gate_act = low_back(highest('red,edf->ref', sent, gate_weight))
    up_act = low_back(highest('red,edf->ref', sent, up_weight))
    hidden = low_back(low(jax.nn.silu(gate_act) * up_act))
    produced = low_back(low(highest('ref,efd->red', hidden, down_weight))).reshape(total_slots, D)
    routed = jnp.take(produced, slots, axis=0).reshape(LEN, TOP, D)
    return resid + highest('tkd,tk->td', routed, gates)

def reference(tokens, routes, in_weight, out_weight, first_gain, second_gain, router_weight, gate_weight, up_weight, down_weight, cotangent):
    arrays = (in_weight, out_weight, first_gain, second_gain, router_weight, gate_weight, up_weight, down_weight)
    params = tuple((array.astype(jnp.float32) for array in arrays))

    def forward(inputs, *weights):

        def per_sequence(pair):
            return jax.checkpoint(sequence_layer)(weights, pair[0], pair[1])
        return lax.map(per_sequence, (inputs, routes))
    outputs, pullback = jax.vjp(forward, tokens.astype(jnp.float32), *params)
    grads = pullback(cotangent.astype(jnp.float32))
    return (outputs.astype(jnp.bfloat16), grads[0].astype(jnp.bfloat16), grads[1], grads[2], grads[3], grads[4], grads[5], grads[6], grads[7], grads[8])
```

```python
import math

import jax
import jax.numpy as jnp
from jax import lax
from jax.sharding import PartitionSpec as P

D = 1024
HEADS = 16
KV_HEADS = 8
HEAD_DIM = 64
EXPERTS = 32
TOP = 8
SEQ_TOK = 128
SEQ_GRP = 2
HALF = 64
MOST = 48


EPS = 1e-05
THETA = 10000.0
NEG = -1e30


def dealt(rows, length):
    owner = rows // SEQ_TOK
    offset = rows % SEQ_TOK
    early = owner * HALF + offset
    late = length - (owner + 1) * HALF + offset - HALF
    return jnp.where(offset < HALF, early, late)


def rotate(values, place, sign):
    half_dim = values.shape[-1] // 2
    freq = THETA ** (-2.0 * jnp.arange(half_dim, dtype=jnp.float32) / values.shape[-1])
    angle = place.astype(jnp.float32)[:, None] * freq[None, :]
    cosine = jnp.cos(angle)[:, None, :]
    sine = sign * jnp.sin(angle)[:, None, :]
    front = values[..., :half_dim]
    back = values[..., half_dim:]
    return jnp.concatenate([front * cosine - back * sine, back * cosine + front * sine], -1)


def norm_back(values, scale, gain, grad_out):
    weighted = grad_out * gain
    grad_in = scale * weighted - values * scale**3 * jnp.mean(weighted * values, -1, keepdims=True)
    return (grad_in, jnp.sum(grad_out * values * scale, 0))


def split_block(block):
    width_k = KV_HEADS * HEAD_DIM
    size = block.shape[0]
    keys = block[..., :width_k].reshape(size, SEQ_GRP, KV_HEADS, HEAD_DIM)
    values = block[..., width_k:].reshape(size, SEQ_GRP, KV_HEADS, HEAD_DIM)
    return (keys, values)


def block_scores(query, keys, query_place, key_place):
    scores = jnp.einsum(
        "sqngd,ksnd->sngqk", query, keys, preferred_element_type=jnp.float32
    ) * HEAD_DIM ** (-0.5)
    allowed = key_place[None, :] <= query_place[:, None]
    return (scores, allowed)


def stack_blocks(whole, places):
    size = math.gcd(whole.shape[0], 512)
    count = whole.shape[0] // size
    return (whole.reshape(count, size, SEQ_GRP, whole.shape[-1]), places.reshape(count, size))


def attend(query, whole, query_place, places):
    group = HEADS // KV_HEADS
    stacked, block_places = stack_blocks(whole, places)
    shape = (SEQ_GRP, KV_HEADS, group, SEQ_TOK)

    def max_step(carry, item):
        peak, total = carry
        keys, values = split_block(item[0])
        scores, allowed = block_scores(query, keys, query_place, item[1])
        masked = jnp.where(allowed, scores, NEG)
        new_peak = jnp.maximum(peak, jnp.max(masked, -1))
        weights = jnp.where(allowed, jnp.exp(masked - new_peak[..., None]), 0.0)
        total = total * jnp.exp(peak - new_peak) + jnp.sum(weights, -1)
        return ((new_peak, total), None)

    start = (jnp.full(shape, NEG, jnp.float32), jnp.zeros(shape, jnp.float32))
    (peak, total), unused = lax.scan(max_step, start, (stacked, block_places))
    log_total = peak + jnp.log(total)

    def value_step(accum, item):
        keys, values = split_block(item[0])
        scores, allowed = block_scores(query, keys, query_place, item[1])
        probs = jnp.where(allowed, jnp.exp(scores - log_total[..., None]), 0.0).astype(jnp.bfloat16)
        return (
            accum
            + jnp.einsum("sngqk,ksnd->sqngd", probs, values, preferred_element_type=jnp.float32),
            None,
        )

    empty = jnp.zeros((SEQ_GRP, SEQ_TOK, KV_HEADS, group, HEAD_DIM), jnp.float32)
    attended, unused = lax.scan(value_step, empty, (stacked, block_places))
    return (attended, log_total)


def score_grads(query, grad_out, log_total, delta, keys, values, query_place, key_place):
    scores, allowed = block_scores(query, keys, query_place, key_place)
    probs = jnp.where(allowed, jnp.exp(scores - log_total[..., None]), 0.0)
    grad_probs = jnp.einsum(
        "sqngd,ksnd->sngqk", grad_out, values, preferred_element_type=jnp.float32
    )
    grad_scores = (probs * (grad_probs - delta[..., None])).astype(jnp.bfloat16)
    return (probs, grad_scores)


def query_grads(query, grad_out, log_total, delta, whole, query_place, places):
    stacked, block_places = stack_blocks(whole, places)

    def query_step(accum, item):
        keys, values = split_block(item[0])
        probs, grad_scores = score_grads(
            query, grad_out, log_total, delta, keys, values, query_place, item[1]
        )
        return (
            accum
            + jnp.einsum(
                "sngqk,ksnd->sqngd", grad_scores, keys, preferred_element_type=jnp.float32
            ),
            None,
        )

    accum, unused = lax.scan(
        query_step, jnp.zeros(query.shape, jnp.float32), (stacked, block_places)
    )
    return accum * HEAD_DIM ** (-0.5)


def key_value_block(query, grad_out, log_total, delta, query_place, block, key_place):
    keys, values = split_block(block)
    probs, grad_scores = score_grads(
        query, grad_out, log_total, delta, keys, values, query_place, key_place
    )
    grad_keys = jnp.einsum(
        "sngqk,sqngd->ksnd", grad_scores, query, preferred_element_type=jnp.float32
    ) * HEAD_DIM ** (-0.5)
    grad_values = jnp.einsum(
        "sngqk,sqngd->ksnd",
        probs.astype(jnp.bfloat16),
        grad_out,
        preferred_element_type=jnp.float32,
    )
    size = block.shape[0]
    return jnp.concatenate(
        [grad_keys.reshape(size, SEQ_GRP, -1), grad_values.reshape(size, SEQ_GRP, -1)], -1
    )


def spread(local):
    once = lax.psum_scatter(local, "ctx", scatter_dimension=0, tiled=True)
    return lax.psum_scatter(once, "wsh", scatter_dimension=0, tiled=True).astype(jnp.float32)


def shards(
    tokens,
    routes,
    in_weight,
    out_weight,
    first_gain,
    second_gain,
    router_weight,
    gate_weight,
    up_weight,
    down_weight,
    cotangent,
):
    ctx_count = lax.axis_size("ctx")
    length = SEQ_TOK * ctx_count
    rows = SEQ_GRP * SEQ_TOK
    group = HEADS // KV_HEADS
    width_q = HEADS * HEAD_DIM
    width_k = KV_HEADS * HEAD_DIM
    my_index = lax.axis_index("ctx")
    local_place = dealt(my_index * SEQ_TOK + jnp.arange(SEQ_TOK, dtype=jnp.int32), length)
    all_place = dealt(jnp.arange(length, dtype=jnp.int32), length)
    inputs = tokens.astype(jnp.float32).reshape(rows, D)
    scale_one = lax.rsqrt(jnp.mean(inputs * inputs, -1, keepdims=True) + EPS)
    normed = (inputs * scale_one * first_gain).astype(jnp.bfloat16)
    mixed = jnp.dot(normed, in_weight, preferred_element_type=jnp.float32).reshape(
        SEQ_GRP, SEQ_TOK, -1
    )
    query = rotate(
        mixed[..., :width_q].reshape(SEQ_GRP, SEQ_TOK, HEADS, HEAD_DIM), local_place, 1.0
    ).astype(jnp.bfloat16)
    query = query.reshape(SEQ_GRP, SEQ_TOK, KV_HEADS, group, HEAD_DIM)
    key = rotate(
        mixed[..., width_q : width_q + width_k].reshape(SEQ_GRP, SEQ_TOK, KV_HEADS, HEAD_DIM),
        local_place,
        1.0,
    ).astype(jnp.bfloat16)
    value = mixed[..., width_q + width_k :].astype(jnp.bfloat16)
    key_value = jnp.swapaxes(
        jnp.concatenate([key.reshape(SEQ_GRP, SEQ_TOK, width_k), value], -1), 0, 1
    )
    whole = lax.all_gather(key_value, "ctx", axis=0, tiled=True)
    attended_full, log_total = attend(query, whole, local_place, all_place)
    attended = attended_full.reshape(rows, width_q).astype(jnp.bfloat16)
    resid = inputs + jnp.dot(attended, out_weight, preferred_element_type=jnp.float32)
    scale_two = lax.rsqrt(jnp.mean(resid * resid, -1, keepdims=True) + EPS)
    normed_two = (resid * scale_two * second_gain).astype(jnp.bfloat16)
    blocks = SEQ_GRP * ctx_count
    mine = gate_weight.shape[0]
    upstream = cotangent.reshape(rows, D)
    cot_all = lax.all_gather(upstream, "ctx", axis=0, tiled=True)
    chosen = jnp.any(
        routes.reshape(rows, TOP).T[:, None, :] == jnp.arange(EXPERTS, dtype=jnp.int32)[:, None], 0
    )
    chosen_all = jnp.swapaxes(
        lax.all_gather(chosen.astype(jnp.bfloat16), "ctx", axis=0, tiled=False), 0, 1
    ).reshape(EXPERTS, blocks, SEQ_TOK)
    gate_full, up_full, down_full = (
        lax.all_gather(gate_weight, "wsh", axis=2, tiled=True),
        lax.all_gather(up_weight, "wsh", axis=2, tiled=True),
        lax.all_gather(down_weight, "wsh", axis=1, tiled=True),
    )
    chosen_my = lax.dynamic_slice_in_dim(chosen_all, my_index * mine, mine, 0)
    before = (
        jnp.arange(SEQ_TOK, dtype=jnp.int32)[:, None] < jnp.arange(SEQ_TOK, dtype=jnp.int32)[None, :]
    ).astype(jnp.bfloat16)
    ranks = jnp.dot(
        chosen_my.reshape(mine * blocks, SEQ_TOK), before, preferred_element_type=jnp.float32
    ).reshape(mine, blocks, SEQ_TOK)
    ranks = jnp.where(chosen_my > 0, ranks, -1.0)
    normed_all = lax.all_gather(normed_two, "ctx", axis=0, tiled=True)
    logits = lax.dot_general(
        router_weight, normed_all, (((0,), (1,)), ((), ())), preferred_element_type=jnp.float32
    )
    taken = chosen_all.reshape(EXPERTS, blocks * SEQ_TOK) > 0
    picked = jnp.where(taken, logits, NEG)
    weights = jnp.where(taken, jnp.exp(picked - jnp.max(picked, 0, keepdims=True)), 0.0)
    gates_all = weights / jnp.sum(weights, 0, keepdims=True)
    gates = lax.dynamic_slice_in_dim(gates_all, my_index * rows, rows, 1)
    gates_my = lax.dynamic_slice_in_dim(gates_all, my_index * mine, mine, 0).reshape(
        mine, blocks, SEQ_TOK
    )
    slot_ids = jnp.arange(MOST, dtype=jnp.int32).astype(jnp.float32)
    match = ranks[:, :, None, :] == slot_ids[:, None]
    dispatch = match.astype(jnp.bfloat16)
    combine = jnp.where(match, gates_my[:, :, None, :], 0.0).astype(jnp.bfloat16)
    slot_gates = jnp.sum(jnp.where(match, gates_my[:, :, None, :], 0.0), -1).astype(jnp.bfloat16)
    normed_blocks = normed_all.reshape(blocks, SEQ_TOK, D)
    cot_blocks = cot_all.reshape(blocks, SEQ_TOK, D)
    arrived = jnp.einsum(
        "ebmt,btd->ebmd", dispatch, normed_blocks, preferred_element_type=jnp.float32
    ).astype(jnp.bfloat16)
    cot_slots = jnp.einsum(
        "ebmt,btd->ebmd", dispatch, cot_blocks, preferred_element_type=jnp.float32
    ).astype(jnp.bfloat16)
    slots = blocks * MOST
    arrived = arrived.reshape(mine, slots, D)
    cot_slots = cot_slots.reshape(mine, slots, D)
    grad_produced = cot_slots * slot_gates.reshape(mine, slots, 1)
    gate_act = jnp.einsum("erd,edf->erf", arrived, gate_full, preferred_element_type=jnp.float32)
    up_act = jnp.einsum("erd,edf->erf", arrived, up_full, preferred_element_type=jnp.float32)
    sigma = jax.nn.sigmoid(gate_act)
    swish = gate_act * sigma
    hidden = (swish * up_act).astype(jnp.bfloat16)
    produced = jnp.einsum(
        "erf,efd->erd", hidden, down_full, preferred_element_type=jnp.float32
    ).astype(jnp.bfloat16)
    mixture = lax.psum_scatter(
        jnp.einsum(
            "ebmt,ebmd->btd",
            combine,
            produced.reshape(mine, blocks, MOST, D),
            preferred_element_type=jnp.float32,
        )
        .astype(jnp.bfloat16)
        .reshape(blocks * SEQ_TOK, D),
        "ctx",
        scatter_dimension=0,
        tiled=True,
    )
    layer_out = (
        (resid + mixture.astype(jnp.float32)).astype(jnp.bfloat16).reshape(SEQ_GRP, SEQ_TOK, D)
    )
    slot_dots = jnp.sum(
        produced.astype(jnp.float32) * cot_slots.astype(jnp.float32), -1
    ).reshape(mine, blocks, MOST)
    gate_dots = jnp.sum(jnp.where(match, slot_dots[..., None], 0.0), 2)
    gate_dots = jnp.swapaxes(gate_dots.reshape(mine, ctx_count, rows), 0, 1)
    grad_gates = lax.all_to_all(gate_dots, "ctx", split_axis=0, concat_axis=0, tiled=True).reshape(
        EXPERTS, rows
    )
    down_local = jnp.einsum(
        "erf,erd->efd", hidden, grad_produced, preferred_element_type=jnp.float32
    )
    grad_hidden = jnp.einsum(
        "erd,efd->erf", grad_produced, down_full, preferred_element_type=jnp.float32
    ).astype(jnp.bfloat16)
    slope = sigma * (1.0 + gate_act * (1.0 - sigma))
    grad_gate = (grad_hidden * up_act * slope).astype(jnp.bfloat16)
    grad_up = (grad_hidden * swish).astype(jnp.bfloat16)
    gate_local = jnp.einsum(
        "erd,erf->edf", arrived, grad_gate, preferred_element_type=jnp.float32
    )
    up_local = jnp.einsum("erd,erf->edf", arrived, grad_up, preferred_element_type=jnp.float32)
    grad_arrived = jnp.einsum(
        "erf,edf->erd", grad_gate, gate_full, preferred_element_type=jnp.float32
    )
    grad_arrived = (
        grad_arrived
        + jnp.einsum("erf,edf->erd", grad_up, up_full, preferred_element_type=jnp.float32)
    ).astype(jnp.bfloat16)
    grad_sent = lax.psum_scatter(
        jnp.einsum(
            "ebmt,ebmd->btd",
            dispatch,
            grad_arrived.reshape(mine, blocks, MOST, D),
            preferred_element_type=jnp.float32,
        )
        .astype(jnp.bfloat16)
        .reshape(blocks * SEQ_TOK, D),
        "ctx",
        scatter_dimension=0,
        tiled=True,
    )
    gate_grad, up_grad, down_grad = (
        lax.psum_scatter(
            gate_local.astype(jnp.bfloat16), "wsh", scatter_dimension=2, tiled=True
        ).astype(jnp.float32),
        lax.psum_scatter(
            up_local.astype(jnp.bfloat16), "wsh", scatter_dimension=2, tiled=True
        ).astype(jnp.float32),
        lax.psum_scatter(
            down_local.astype(jnp.bfloat16), "wsh", scatter_dimension=1, tiled=True
        ).astype(jnp.float32),
    )
    grad_logits = (gates * (grad_gates - jnp.sum(gates * grad_gates, 0, keepdims=True))).astype(
        jnp.bfloat16
    )
    router_local = lax.dot_general(
        normed_two, grad_logits, (((0,), (1,)), ((), ())), preferred_element_type=jnp.float32
    )
    grad_normed_two = grad_sent.astype(jnp.float32) + lax.dot_general(
        grad_logits, router_weight, (((0,), (1,)), ((), ())), preferred_element_type=jnp.float32
    )
    grad_resid_norm, second_local = norm_back(resid, scale_two, second_gain, grad_normed_two)
    grad_resid = upstream.astype(jnp.float32) + grad_resid_norm
    grad_branch = grad_resid.astype(jnp.bfloat16)
    out_local = lax.dot_general(
        attended, grad_branch, (((0,), (0,)), ((), ())), preferred_element_type=jnp.float32
    )
    grad_attended = lax.dot_general(
        grad_branch, out_weight, (((1,), (1,)), ((), ())), preferred_element_type=jnp.float32
    ).astype(jnp.bfloat16)
    grad_out = grad_attended.reshape(SEQ_GRP, SEQ_TOK, KV_HEADS, group, HEAD_DIM)
    delta = jnp.einsum("sqngd,sqngd->sngq", grad_out.astype(jnp.float32), attended_full)
    grad_query = query_grads(query, grad_out, log_total, delta, whole, local_place, all_place)
    size = math.gcd(SEQ_TOK * lax.axis_size("ctx"), 512)
    pieces = SEQ_TOK * lax.axis_size("ctx") // size

    def block_term(item):
        return key_value_block(query, grad_out, log_total, delta, local_place, item[0], item[1])

    terms = lax.map(
        block_term,
        (whole.reshape(pieces, size, SEQ_GRP, whole.shape[-1]), all_place.reshape(pieces, size)),
    )
    kv_grad = jnp.swapaxes(
        lax.psum_scatter(
            terms.reshape(SEQ_TOK * lax.axis_size("ctx"), SEQ_GRP, terms.shape[-1]).astype(
                jnp.bfloat16
            ),
            "ctx",
            scatter_dimension=0,
            tiled=True,
        ).astype(jnp.float32),
        0,
        1,
    )
    grad_query = rotate(grad_query.reshape(SEQ_GRP, SEQ_TOK, HEADS, HEAD_DIM), local_place, -1.0)
    grad_key = rotate(
        kv_grad[..., :width_k].reshape(SEQ_GRP, SEQ_TOK, KV_HEADS, HEAD_DIM), local_place, -1.0
    )
    grad_mixed = jnp.concatenate(
        [
            grad_query.reshape(SEQ_GRP, SEQ_TOK, width_q),
            grad_key.reshape(SEQ_GRP, SEQ_TOK, width_k),
            kv_grad[..., width_k:],
        ],
        -1,
    )
    grad_mixed = grad_mixed.astype(jnp.bfloat16).reshape(rows, -1)
    in_local = lax.dot_general(
        normed, grad_mixed, (((0,), (0,)), ((), ())), preferred_element_type=jnp.float32
    )
    grad_normed = lax.dot_general(
        grad_mixed, in_weight, (((1,), (1,)), ((), ())), preferred_element_type=jnp.float32
    )
    grad_inputs_norm, first_local = norm_back(inputs, scale_one, first_gain, grad_normed)
    tokens_grad = (grad_resid + grad_inputs_norm).astype(jnp.bfloat16).reshape(SEQ_GRP, SEQ_TOK, D)
    in_grad, out_grad = spread(in_local.astype(jnp.bfloat16)), spread(out_local.astype(jnp.bfloat16))
    small = spread(
        jnp.concatenate([router_local, first_local[:, None], second_local[:, None]], -1)
    )
    router_grad = small[:, :EXPERTS]
    first_gain_grad, second_gain_grad = small[:, EXPERTS], small[:, EXPERTS + 1]
    return (
        layer_out,
        tokens_grad,
        in_grad,
        out_grad,
        first_gain_grad,
        second_gain_grad,
        router_grad,
        gate_grad,
        up_grad,
        down_grad,
    )


def solution(mesh):
    placed = (
        P("wsh", "ctx", None),
        P("wsh", "ctx", None),
        P(),
        P(),
        P(),
        P(),
        P(),
        P("ctx", None, "wsh"),
        P("ctx", None, "wsh"),
        P("ctx", "wsh", None),
        P("wsh", "ctx", None),
    )
    return jax.shard_map(
        shards,
        mesh=mesh,
        in_specs=placed,
        out_specs=(
            P("wsh", "ctx", None),
            P("wsh", "ctx", None),
            P(("ctx", "wsh"), None),
            P(("ctx", "wsh"), None),
            P(("ctx", "wsh")),
            P(("ctx", "wsh")),
            P(("ctx", "wsh"), None),
            P("ctx", None, "wsh"),
            P("ctx", None, "wsh"),
            P("ctx", "wsh", None),
        ),
        check_vma=False,
    )
```

```python
import jax
import jax.numpy as jnp
from jax import lax
from jax.experimental import pallas as pl
from jax.experimental.pallas import tpu as pltpu
from jax.sharding import PartitionSpec as P

D = 1024
HEADS = 16
KV_HEADS = 8
HEAD_DIM = 64
EXPERTS = 32
TOP = 8
SEQ_TOK = 128
SEQ_GRP = 2
HALF = 64
MOST = 48


EPS = 1e-05
THETA = 10000.0
NEG = -1e30


def dealt(rows, length):
    owner = rows // SEQ_TOK
    offset = rows % SEQ_TOK
    early = owner * HALF + offset
    late = length - (owner + 1) * HALF + offset - HALF
    return jnp.where(offset < HALF, early, late)


def rotate(values, place, sign):
    half_dim = values.shape[-1] // 2
    freq = THETA ** (-2.0 * jnp.arange(half_dim, dtype=jnp.float32) / values.shape[-1])
    angle = place.astype(jnp.float32)[:, None] * freq[None, :]
    cosine = jnp.cos(angle)[:, None, :]
    sine = sign * jnp.sin(angle)[:, None, :]
    front = values[..., :half_dim]
    back = values[..., half_dim:]
    return jnp.concatenate([front * cosine - back * sine, back * cosine + front * sine], -1)


def norm_back(values, scale, gain, grad_out):
    weighted = grad_out * gain
    grad_in = scale * weighted - values * scale**3 * jnp.mean(weighted * values, -1, keepdims=True)
    return (grad_in, jnp.sum(grad_out * values * scale, 0))


def ring_order(count):
    return list(range(0, count, 2)) + list(reversed(range(1, count, 2)))


def ring_shift(count, step):
    order = ring_order(count)
    return [(order[i], order[(i + step) % count]) for i in range(count)]


def ring_gather(parts):
    count = lax.axis_size("ctx")
    ahead, behind = ring_shift(count, 1), ring_shift(count, -1)
    held = [list(parts)] + [[None] * len(parts) for _ in range(count - 1)]
    far = count // 2
    for p, part in enumerate(parts):
        up, down = part, part
        ups = far if p % 2 == 0 else count - 1 - far
        for step in range(1, far + 1):
            if step <= ups:
                up = lax.ppermute(up, "ctx", ahead)
                held[step][p] = up
            if step <= count - 1 - ups:
                down = lax.ppermute(down, "ctx", behind)
                held[count - step][p] = down
    return held


def add_low(left, right):
    return (left.astype(jnp.float32) + right.astype(jnp.float32)).astype(left.dtype)


def ring_sum(block, parts):
    count = lax.axis_size("ctx")
    ahead, behind = ring_shift(count, 1), ring_shift(count, -1)
    far = count // 2
    sums = []
    for p in range(parts):
        ups = far if p % 2 == 0 else count - 1 - far
        downs = count - 1 - ups
        up = block(count - ups, p)
        for step in range(ups - 1, 0, -1):
            up = add_low(lax.ppermute(up, "ctx", ahead), block(count - step, p))
        up = lax.ppermute(up, "ctx", ahead)
        down = block(downs, p)
        for step in range(downs - 1, 0, -1):
            down = add_low(lax.ppermute(down, "ctx", behind), block(step, p))
        down = lax.ppermute(down, "ctx", behind)
        own = block(0, p).astype(jnp.float32)
        sums.append(up.astype(jnp.float32) + down.astype(jnp.float32) + own)
    return sums


OTHER_CORE = [(0, 1), (1, 0), (2, 3), (3, 2)]
OTHER_CHIP = [(0, 2), (2, 0), (1, 3), (3, 1)]


def pair_gather(piece):
    other = lax.ppermute(piece, "wsh", OTHER_CHIP)
    near, near_other = (lax.ppermute(one, "wsh", OTHER_CORE) for one in (piece, other))
    return [piece, other, near, near_other]


def pair_sum(pieces):
    own = add_low(pieces[0], lax.ppermute(pieces[2], "wsh", OTHER_CORE))
    other = add_low(pieces[1], lax.ppermute(pieces[3], "wsh", OTHER_CORE))
    return own.astype(jnp.float32) + lax.ppermute(other, "wsh", OTHER_CHIP).astype(jnp.float32)


def spread(local, behind):
    count = lax.axis_size("ctx")
    me = lax.axis_index("wsh")
    split = local.reshape(count, 4, local.shape[0] // (4 * count), -1)

    def take(flip):
        return lax.dynamic_index_in_dim(split, me ^ flip, 1, False)

    once = pair_sum([take(0), take(2), take(1), take(3)]).astype(local.dtype)

    def block(k, p):
        return lax.dynamic_index_in_dim(once, behind[k], 0, False)

    return ring_sum(block, 1)[0]


PAIR = 2 * HEAD_DIM
def nt(left, right):
    return lax.dot_general(left, right, (((1,), (1,)), ((), ())), preferred_element_type=jnp.float32)
def tn(left, right):
    return lax.dot_general(left, right, (((0,), (0,)), ((), ())), preferred_element_type=jnp.float32)
def nn(left, right):
    return jnp.dot(left, right, preferred_element_type=jnp.float32)

def halves(ref, head):
    start = head * PAIR
    block = ref[0, :, start : start + PAIR]
    both = [block[:, :HEAD_DIM], block[:, HEAD_DIM:]]
    return (
        jnp.concatenate([one[:HALF] for one in both], 0),
        jnp.concatenate([one[HALF:] for one in both], 0),
    )

def key_parts(ref):
    whole = ref[:, 0]
    count = whole.shape[0]
    early = whole[:, :HALF].reshape(count * HALF, -1)
    late = whole[:, HALF:].reshape(count * HALF, -1)
    return early, late

def weigh(scores):
    peak = jnp.max(scores[0], 0, keepdims=True)
    for more in scores[1:]:
        peak = jnp.maximum(peak, jnp.max(more, 0, keepdims=True))
    powers = [jnp.exp(part - peak) for part in scores]
    total = sum(jnp.sum(part, 0, keepdims=True) for part in powers)
    inverse = 1.0 / total
    return [part * inverse for part in powers]

def split_heads(stacked_early, stacked_late):
    return jnp.concatenate(
        [
            jnp.concatenate([stacked_early[:HALF], stacked_early[HALF:]], 1),
            jnp.concatenate([stacked_late[:HALF], stacked_late[HALF:]], 1),
        ],
        0,
    )

def attend_kernel(bias_early, bias_late, query, keys, out):
    early, late = key_parts(keys)
    for head in range(2):
        at = head * HEAD_DIM
        k_e, k_l = early[:, at : at + HEAD_DIM], late[:, at : at + HEAD_DIM]
        v_e, v_l = early[:, PAIR + at : PAIR + at + HEAD_DIM], late[:, PAIR + at : PAIR + at + HEAD_DIM]
        q_e, q_l = halves(query, head)
        (p_ee,) = weigh([nt(k_e, q_e) + bias_early[...]])
        p_el, p_ll = weigh([nt(k_e, q_l), nt(k_l, q_l) + bias_late[...]])
        o_e = tn(p_ee.astype(jnp.bfloat16), v_e)
        o_l = tn(p_el.astype(jnp.bfloat16), v_e) + tn(p_ll.astype(jnp.bfloat16), v_l)
        out[0, :, head * PAIR : (head + 1) * PAIR] = split_heads(o_e, o_l).astype(jnp.bfloat16)

def attend_back_kernel(bias_early, bias_late, query, keys, grad, grad_query, grad_keys):
    early, late = key_parts(keys)
    scale = HEAD_DIM ** (-0.5)
    count = keys.shape[0]
    parts_e, parts_l = [], []
    for head in range(2):
        at = head * HEAD_DIM
        k_e, k_l = early[:, at : at + HEAD_DIM], late[:, at : at + HEAD_DIM]
        v_e, v_l = early[:, PAIR + at : PAIR + at + HEAD_DIM], late[:, PAIR + at : PAIR + at + HEAD_DIM]
        q_e, q_l = halves(query, head)
        d_e, d_l = halves(grad, head)
        (p_ee,) = weigh([nt(k_e, q_e) + bias_early[...]])
        p_el, p_ll = weigh([nt(k_e, q_l), nt(k_l, q_l) + bias_late[...]])
        g_ee, g_el, g_ll = nt(v_e, d_e), nt(v_e, d_l), nt(v_l, d_l)
        delta_e = jnp.sum(p_ee * g_ee, 0, keepdims=True)
        delta_l = jnp.sum(p_el * g_el, 0, keepdims=True) + jnp.sum(p_ll * g_ll, 0, keepdims=True)
        s_ee = (p_ee * (g_ee - delta_e)).astype(jnp.bfloat16)
        s_el = (p_el * (g_el - delta_l)).astype(jnp.bfloat16)
        s_ll = (p_ll * (g_ll - delta_l)).astype(jnp.bfloat16)
        gq_e = tn(s_ee, k_e) * scale
        gq_l = (tn(s_el, k_e) + tn(s_ll, k_l)) * scale
        grad_query[0, :, head * PAIR : (head + 1) * PAIR] = split_heads(gq_e, gq_l)
        gk_e = nn(s_ee, q_e) + nn(s_el, q_l)
        gk_l = nn(s_ll, q_l)
        gv_e = nn(p_ee.astype(jnp.bfloat16), d_e) + nn(p_el.astype(jnp.bfloat16), d_l)
        gv_l = nn(p_ll.astype(jnp.bfloat16), d_l)
        parts_e.append((gk_e, gv_e))
        parts_l.append((gk_l, gv_l))
    for parts, start in ((parts_e, 0), (parts_l, HALF)):
        for kind in range(2):
            joined = jnp.concatenate([parts[0][kind], parts[1][kind]], 1)
            grad_keys[:, 0, start : start + HALF, kind * PAIR : (kind + 1) * PAIR] = (
                joined.astype(jnp.bfloat16).reshape(count, HALF, PAIR)
            )

def attend_specs(count):
    bias = pl.BlockSpec((count * HALF, SEQ_TOK), lambda s, j: (0, 0))
    rows = pl.BlockSpec((1, SEQ_TOK, 2 * PAIR), lambda s, j: (s, 0, j))
    keys = pl.BlockSpec((count, 1, SEQ_TOK, 2 * PAIR), lambda s, j: (0, s, 0, j))
    return bias, rows, keys

def attend(bias_early, bias_late, query, keys):
    count = keys.shape[0]
    bias, rows, key_rows = attend_specs(count)
    return pl.pallas_call(
        attend_kernel,
        out_shape=jax.ShapeDtypeStruct(query.shape, jnp.bfloat16),
        grid=(SEQ_GRP, KV_HEADS // 2),
        in_specs=[bias, bias, rows, key_rows],
        out_specs=rows,
        cost_estimate=pl.CostEstimate(flops=4 * query.size * count * SEQ_TOK, bytes_accessed=2 * keys.size + 4 * query.size, transcendentals=0),
    )(bias_early, bias_late, query, keys)

def attend_back(bias_early, bias_late, query, keys, grad):
    count = keys.shape[0]
    bias, rows, key_rows = attend_specs(count)
    return pl.pallas_call(
        attend_back_kernel,
        out_shape=(jax.ShapeDtypeStruct(query.shape, jnp.float32), jax.ShapeDtypeStruct(keys.shape, jnp.bfloat16)),
        grid=(SEQ_GRP, KV_HEADS // 2),
        in_specs=[bias, bias, rows, key_rows, rows],
        out_specs=(rows, key_rows),
        cost_estimate=pl.CostEstimate(flops=10 * query.size * count * SEQ_TOK, bytes_accessed=4 * keys.size + 8 * query.size, transcendentals=0),
    )(bias_early, bias_late, query, keys, grad)


def shards(
    tokens,
    routes,
    in_weight,
    out_weight,
    first_gain,
    second_gain,
    router_weight,
    gate_weight,
    up_weight,
    down_weight,
    cotangent,
):
    ctx_count = lax.axis_size("ctx")
    length = SEQ_TOK * ctx_count
    rows = SEQ_GRP * SEQ_TOK
    width_q = HEADS * HEAD_DIM
    width_k = KV_HEADS * HEAD_DIM
    my_index = lax.axis_index("ctx")
    order = ring_order(ctx_count)
    place_of = jnp.array([order.index(c) for c in range(ctx_count)], jnp.int32)
    my_place = place_of[my_index]
    order = jnp.array(order, jnp.int32)
    owner = order[(my_place - jnp.arange(ctx_count, dtype=jnp.int32)) % ctx_count]
    local_place = dealt(my_index * SEQ_TOK + jnp.arange(SEQ_TOK, dtype=jnp.int32), length)
    key_place = dealt(owner[:, None] * SEQ_TOK + jnp.arange(SEQ_TOK, dtype=jnp.int32), length)
    bias_early, bias_late = (
        jnp.where(
            key_place[:, part].reshape(-1, 1) <= jnp.tile(local_place[part], 2)[None, :], 0.0, NEG
        ).astype(jnp.float32)
        for part in (slice(0, HALF), slice(HALF, None))
    )
    upstream = cotangent.reshape(rows, D)
    chosen = jnp.any(
        routes.reshape(rows, TOP).T[:, None, :] == jnp.arange(EXPERTS, dtype=jnp.int32)[:, None], 0
    )
    chosen_all = jnp.stack(
        [held[0] for held in ring_gather([chosen.astype(jnp.bfloat16)])], 1
    )
    gate_full, up_full, down_full = (
        jnp.concatenate(pair_gather(gate_weight), 2),
        jnp.concatenate(pair_gather(up_weight), 2),
        jnp.concatenate(pair_gather(down_weight), 1),
    )
    inputs = tokens.astype(jnp.float32).reshape(rows, D)
    scale_one = lax.rsqrt(jnp.mean(inputs * inputs, -1, keepdims=True) + EPS)
    normed = (inputs * scale_one * first_gain).astype(jnp.bfloat16)
    mixed = jnp.dot(normed, in_weight, preferred_element_type=jnp.float32).reshape(
        SEQ_GRP, SEQ_TOK, -1
    )
    query = rotate(
        mixed[..., :width_q].reshape(SEQ_GRP, SEQ_TOK, HEADS, HEAD_DIM), local_place, 1.0
    ).astype(jnp.bfloat16)
    query = (query * jnp.bfloat16(HEAD_DIM ** (-0.5))).reshape(SEQ_GRP, SEQ_TOK, width_q)
    key = rotate(
        mixed[..., width_q : width_q + width_k].reshape(SEQ_GRP, SEQ_TOK, KV_HEADS, HEAD_DIM),
        local_place,
        1.0,
    ).astype(jnp.bfloat16)
    value = mixed[..., width_q + width_k :].astype(jnp.bfloat16)
    pairs = (SEQ_GRP, SEQ_TOK, KV_HEADS // 2, PAIR)
    key_value = jnp.concatenate([key.reshape(pairs), value.reshape(pairs)], -1).reshape(
        SEQ_GRP, SEQ_TOK, 2 * width_k
    )
    whole = jnp.stack(
        [jnp.stack(held) for held in ring_gather([key_value[s] for s in range(SEQ_GRP)])]
    )
    attended = attend(bias_early, bias_late, query, whole).reshape(rows, width_q)
    resid = inputs + jnp.dot(attended, out_weight, preferred_element_type=jnp.float32)
    scale_two = lax.rsqrt(jnp.mean(resid * resid, -1, keepdims=True) + EPS)
    normed_two = (resid * scale_two * second_gain).astype(jnp.bfloat16)
    blocks = SEQ_GRP * ctx_count
    mine = gate_weight.shape[0]
    chosen_all = chosen_all.reshape(EXPERTS, blocks, SEQ_TOK)
    chosen_my = lax.dynamic_slice_in_dim(chosen_all, my_index * mine, mine, 0)
    before = (
        jnp.arange(SEQ_TOK, dtype=jnp.int32)[:, None] < jnp.arange(SEQ_TOK, dtype=jnp.int32)[None, :]
    ).astype(jnp.bfloat16)
    ranks = jnp.dot(
        chosen_my.reshape(mine * blocks, SEQ_TOK), before, preferred_element_type=jnp.float32
    ).reshape(mine, blocks, SEQ_TOK)
    ranks = jnp.where(chosen_my > 0, ranks, -1.0)
    normed_all = jnp.concatenate(
        [part for held in ring_gather([normed_two[:SEQ_TOK], normed_two[SEQ_TOK:]]) for part in held]
    )
    cot_late = lax.optimization_barrier((upstream[SEQ_TOK:], attended[:1, :1]))[0]
    cot_all = jnp.concatenate(
        [part for held in ring_gather([upstream[:SEQ_TOK], cot_late]) for part in held]
    )
    logits = lax.dot_general(
        router_weight, normed_all, (((0,), (1,)), ((), ())), preferred_element_type=jnp.float32
    )
    taken = chosen_all.reshape(EXPERTS, blocks * SEQ_TOK) > 0
    picked = jnp.where(taken, logits, NEG)
    weights = jnp.where(taken, jnp.exp(picked - jnp.max(picked, 0, keepdims=True)), 0.0)
    gates_all = weights / jnp.sum(weights, 0, keepdims=True)
    gates = gates_all[:, :rows]
    gates_my = lax.dynamic_slice_in_dim(gates_all, my_index * mine, mine, 0).reshape(
        mine, blocks, SEQ_TOK
    )
    slot_ids = jnp.arange(MOST, dtype=jnp.int32).astype(jnp.float32)
    match = ranks[:, :, None, :] == slot_ids[:, None]
    dispatch = match.astype(jnp.bfloat16)
    combine = jnp.where(match, gates_my[:, :, None, :], 0.0).astype(jnp.bfloat16)
    slot_gates = jnp.sum(jnp.where(match, gates_my[:, :, None, :], 0.0), -1).astype(jnp.bfloat16)
    normed_blocks = normed_all.reshape(blocks, SEQ_TOK, D)
    cot_blocks = cot_all.reshape(blocks, SEQ_TOK, D)
    arrived = jnp.einsum(
        "ebmt,btd->ebmd", dispatch, normed_blocks, preferred_element_type=jnp.float32
    ).astype(jnp.bfloat16)
    cot_slots = jnp.einsum(
        "ebmt,btd->ebmd", dispatch, cot_blocks, preferred_element_type=jnp.float32
    ).astype(jnp.bfloat16)
    slots = blocks * MOST
    arrived = arrived.reshape(mine, slots, D)
    cot_slots = cot_slots.reshape(mine, slots, D)
    grad_produced = cot_slots * slot_gates.reshape(mine, slots, 1)
    gate_act = jnp.einsum("erd,edf->erf", arrived, gate_full, preferred_element_type=jnp.float32)
    up_act = jnp.einsum("erd,edf->erf", arrived, up_full, preferred_element_type=jnp.float32)
    sigma = jax.nn.sigmoid(gate_act)
    swish = gate_act * sigma
    hidden = (swish * up_act).astype(jnp.bfloat16)
    produced = jnp.einsum(
        "erf,efd->erd", hidden, down_full, preferred_element_type=jnp.float32
    ).astype(jnp.bfloat16)
    mixed_part = (
        jnp.einsum(
            "ebmt,ebmd->btd",
            combine,
            produced.reshape(mine, blocks, MOST, D),
            preferred_element_type=jnp.float32,
        )
        .astype(jnp.bfloat16)
        .reshape(ctx_count, SEQ_GRP, SEQ_TOK, D)
    )
    mixture = jnp.concatenate(ring_sum(lambda k, p: mixed_part[k, p], SEQ_GRP))
    layer_out = (resid + mixture).astype(jnp.bfloat16).reshape(SEQ_GRP, SEQ_TOK, D)
    slot_dots = jnp.sum(
        produced.astype(jnp.float32) * cot_slots.astype(jnp.float32), -1
    ).reshape(mine, blocks, MOST)
    gate_dots = jnp.sum(jnp.where(match, slot_dots[..., None], 0.0), 2)
    gate_dots = jnp.swapaxes(gate_dots.reshape(mine, ctx_count, rows), 0, 1)
    arrived_dots = [gate_dots[0]] + [
        lax.ppermute(gate_dots[ctx_count - k], "ctx", ring_shift(ctx_count, k))
        for k in range(1, ctx_count)
    ]
    behind_of = (my_place - place_of) % ctx_count
    grad_gates = jnp.take(jnp.stack(arrived_dots), behind_of, axis=0).reshape(EXPERTS, rows)
    down_local = jnp.einsum(
        "erf,erd->efd", hidden, grad_produced, preferred_element_type=jnp.float32
    )
    grad_hidden = jnp.einsum(
        "erd,efd->erf", grad_produced, down_full, preferred_element_type=jnp.float32
    ).astype(jnp.bfloat16)
    slope = sigma * (1.0 + gate_act * (1.0 - sigma))
    grad_gate = (grad_hidden * up_act * slope).astype(jnp.bfloat16)
    grad_up = (grad_hidden * swish).astype(jnp.bfloat16)
    gate_local = jnp.einsum(
        "erd,erf->edf", arrived, grad_gate, preferred_element_type=jnp.float32
    )
    up_local = jnp.einsum("erd,erf->edf", arrived, grad_up, preferred_element_type=jnp.float32)
    grad_arrived = jnp.einsum(
        "erf,edf->erd", grad_gate, gate_full, preferred_element_type=jnp.float32
    )
    grad_arrived = (
        grad_arrived
        + jnp.einsum("erf,edf->erd", grad_up, up_full, preferred_element_type=jnp.float32)
    ).astype(jnp.bfloat16)
    sent_part = (
        jnp.einsum(
            "ebmt,ebmd->btd",
            dispatch,
            grad_arrived.reshape(mine, blocks, MOST, D),
            preferred_element_type=jnp.float32,
        )
        .astype(jnp.bfloat16)
        .reshape(ctx_count, SEQ_GRP, SEQ_TOK, D)
    )
    grad_sent = jnp.concatenate(ring_sum(lambda k, p: sent_part[k, p], SEQ_GRP))
    gate_grad, up_grad, down_grad = (
        pair_sum(jnp.split(gate_local.astype(jnp.bfloat16), 4, 2)),
        pair_sum(jnp.split(up_local.astype(jnp.bfloat16), 4, 2)),
        pair_sum(jnp.split(down_local.astype(jnp.bfloat16), 4, 1)),
    )
    grad_logits = (gates * (grad_gates - jnp.sum(gates * grad_gates, 0, keepdims=True))).astype(
        jnp.bfloat16
    )
    router_local = lax.dot_general(
        normed_two, grad_logits, (((0,), (1,)), ((), ())), preferred_element_type=jnp.float32
    )
    grad_normed_two = grad_sent + lax.dot_general(
        grad_logits, router_weight, (((0,), (1,)), ((), ())), preferred_element_type=jnp.float32
    )
    grad_resid_norm, second_local = norm_back(resid, scale_two, second_gain, grad_normed_two)
    grad_resid = upstream.astype(jnp.float32) + grad_resid_norm
    grad_branch = grad_resid.astype(jnp.bfloat16)
    out_local = lax.dot_general(
        attended, grad_branch, (((0,), (0,)), ((), ())), preferred_element_type=jnp.float32
    )
    grad_attended = lax.dot_general(
        grad_branch, out_weight, (((1,), (1,)), ((), ())), preferred_element_type=jnp.float32
    ).astype(jnp.bfloat16)
    grad_query, grad_whole = attend_back(
        bias_early,
        bias_late,
        query,
        whole,
        grad_attended.reshape(SEQ_GRP, SEQ_TOK, width_q),
    )
    kv_grad = jnp.stack(ring_sum(lambda k, p: grad_whole[k, p], SEQ_GRP)).reshape(
        SEQ_GRP, SEQ_TOK, KV_HEADS // 2, 2, PAIR
    )
    grad_query = rotate(grad_query.reshape(SEQ_GRP, SEQ_TOK, HEADS, HEAD_DIM), local_place, -1.0)
    grad_query = grad_query.astype(jnp.bfloat16).reshape(rows, width_q)
    grad_key = rotate(
        kv_grad[:, :, :, 0].reshape(SEQ_GRP, SEQ_TOK, KV_HEADS, HEAD_DIM), local_place, -1.0
    )
    grad_pair = jnp.concatenate(
        [grad_key.reshape(rows, width_k), kv_grad[:, :, :, 1].reshape(rows, width_k)], -1
    ).astype(jnp.bfloat16)
    in_first = lax.dot_general(
        normed, grad_query, (((0,), (0,)), ((), ())), preferred_element_type=jnp.float32
    )
    in_second = lax.dot_general(
        normed, grad_pair, (((0,), (0,)), ((), ())), preferred_element_type=jnp.float32
    )
    grad_normed = lax.dot_general(
        grad_query, in_weight[:, :width_q], (((1,), (1,)), ((), ())), preferred_element_type=jnp.float32
    ) + lax.dot_general(
        grad_pair, in_weight[:, width_q:], (((1,), (1,)), ((), ())), preferred_element_type=jnp.float32
    )
    grad_inputs_norm, first_local = norm_back(inputs, scale_one, first_gain, grad_normed)
    tokens_grad = (grad_resid + grad_inputs_norm).astype(jnp.bfloat16).reshape(SEQ_GRP, SEQ_TOK, D)
    in_grad = jnp.concatenate(
        [spread(in_first.astype(jnp.bfloat16), owner), spread(in_second.astype(jnp.bfloat16), owner)],
        -1,
    )
    out_grad = spread(out_local.astype(jnp.bfloat16), owner)
    small = spread(jnp.concatenate([router_local, second_local[:, None]], -1), owner)
    router_grad = small[:, :EXPERTS]
    second_gain_grad = small[:, EXPERTS]
    first_gain_grad = spread(first_local[:, None], owner)[:, 0]
    return (
        layer_out,
        tokens_grad,
        in_grad,
        out_grad,
        first_gain_grad,
        second_gain_grad,
        router_grad,
        gate_grad,
        up_grad,
        down_grad,
    )


def solution(mesh):
    placed = (
        P("wsh", "ctx", None),
        P("wsh", "ctx", None),
        P(),
        P(),
        P(),
        P(),
        P(),
        P("ctx", None, "wsh"),
        P("ctx", None, "wsh"),
        P("ctx", "wsh", None),
        P("wsh", "ctx", None),
    )
    return jax.shard_map(
        shards,
        mesh=mesh,
        in_specs=placed,
        out_specs=(
            P("wsh", "ctx", None),
            P("wsh", "ctx", None),
            P(("ctx", "wsh"), None),
            P(("ctx", "wsh"), None),
            P(("ctx", "wsh")),
            P(("ctx", "wsh")),
            P(("ctx", "wsh"), None),
            P("ctx", None, "wsh"),
            P("ctx", None, "wsh"),
            P("ctx", "wsh", None),
        ),
        check_vma=False,
    )
```

```python
import jax
import jax.numpy as jnp
from jax import lax
from jax.experimental import pallas as pl
from jax.experimental.pallas import tpu as pltpu
from jax.sharding import PartitionSpec as P

D = 1024
HEADS = 16
KV_HEADS = 8
HEAD_DIM = 64
EXPERTS = 32
TOP = 8
SEQ_TOK = 128
SEQ_GRP = 2
HALF = 64
MOST = 48


EPS = 1e-05
THETA = 10000.0
NEG = -1e30


def dealt(rows, length):
    owner = rows // SEQ_TOK
    offset = rows % SEQ_TOK
    early = owner * HALF + offset
    late = length - (owner + 1) * HALF + offset - HALF
    return jnp.where(offset < HALF, early, late)


def rotate(values, place, sign):
    half_dim = values.shape[-1] // 2
    freq = THETA ** (-2.0 * jnp.arange(half_dim, dtype=jnp.float32) / values.shape[-1])
    angle = place.astype(jnp.float32)[:, None] * freq[None, :]
    cosine = jnp.cos(angle)[:, None, :]
    sine = sign * jnp.sin(angle)[:, None, :]
    front = values[..., :half_dim]
    back = values[..., half_dim:]
    return jnp.concatenate([front * cosine - back * sine, back * cosine + front * sine], -1)


def norm_back(values, scale, gain, grad_out):
    weighted = grad_out * gain
    grad_in = scale * weighted - values * scale**3 * jnp.mean(weighted * values, -1, keepdims=True)
    return (grad_in, jnp.sum(grad_out * values * scale, 0))


def ring_order(count):
    return list(range(0, count, 2)) + list(reversed(range(1, count, 2)))


def ring_shift(count, step):
    order = ring_order(count)
    return [(order[i], order[(i + step) % count]) for i in range(count)]


def ring_gather(parts):
    count = lax.axis_size("ctx")
    ahead, behind = ring_shift(count, 1), ring_shift(count, -1)
    held = [list(parts)] + [[None] * len(parts) for _ in range(count - 1)]
    far = count // 2
    for p, part in enumerate(parts):
        up, down = part, part
        ups = far if p % 2 == 0 else count - 1 - far
        for step in range(1, far + 1):
            if step <= ups:
                up = lax.ppermute(up, "ctx", ahead)
                held[step][p] = up
            if step <= count - 1 - ups:
                down = lax.ppermute(down, "ctx", behind)
                held[count - step][p] = down
    return held


def add_low(left, right):
    return (left.astype(jnp.float32) + right.astype(jnp.float32)).astype(left.dtype)


def ring_sum(block, parts):
    count = lax.axis_size("ctx")
    ahead, behind = ring_shift(count, 1), ring_shift(count, -1)
    far = count // 2
    sums = []
    for p in range(parts):
        ups = far if p % 2 == 0 else count - 1 - far
        downs = count - 1 - ups
        up = block(count - ups, p)
        for step in range(ups - 1, 0, -1):
            up = add_low(lax.ppermute(up, "ctx", ahead), block(count - step, p))
        up = lax.ppermute(up, "ctx", ahead)
        down = block(downs, p)
        for step in range(downs - 1, 0, -1):
            down = add_low(lax.ppermute(down, "ctx", behind), block(step, p))
        down = lax.ppermute(down, "ctx", behind)
        own = block(0, p).astype(jnp.float32)
        sums.append(up.astype(jnp.float32) + down.astype(jnp.float32) + own)
    return sums


OTHER_CORE = [(0, 1), (1, 0), (2, 3), (3, 2)]
OTHER_CHIP = [(0, 2), (2, 0), (1, 3), (3, 1)]


def pair_sum(pieces):
    own = add_low(pieces[0], lax.ppermute(pieces[2], "wsh", OTHER_CORE))
    other = add_low(pieces[1], lax.ppermute(pieces[3], "wsh", OTHER_CORE))
    return own.astype(jnp.float32) + lax.ppermute(other, "wsh", OTHER_CHIP).astype(jnp.float32)


def scatter(local):
    once = lax.psum_scatter(local, "ctx", scatter_dimension=0, tiled=True)
    return lax.psum_scatter(once, "wsh", scatter_dimension=0, tiled=True).astype(jnp.float32)


def spread(local, behind):
    count = lax.axis_size("ctx")
    me = lax.axis_index("wsh")
    split = local.reshape(count, 4, local.shape[0] // (4 * count), -1)

    def take(flip):
        return lax.dynamic_index_in_dim(split, me ^ flip, 1, False)

    once = pair_sum([take(0), take(2), take(1), take(3)]).astype(local.dtype)

    def block(k, p):
        return lax.dynamic_index_in_dim(once, behind[k], 0, False)

    return ring_sum(block, 1)[0]


PAIR = 2 * HEAD_DIM
def nt(left, right):
    return lax.dot_general(left, right, (((1,), (1,)), ((), ())), preferred_element_type=jnp.float32)
def tn(left, right):
    return lax.dot_general(left, right, (((0,), (0,)), ((), ())), preferred_element_type=jnp.float32)
def nn(left, right):
    return jnp.dot(left, right, preferred_element_type=jnp.float32)

def halves(ref, head):
    start = head * PAIR
    block = ref[0, :, start : start + PAIR]
    both = [block[:, :HEAD_DIM], block[:, HEAD_DIM:]]
    return (
        jnp.concatenate([one[:HALF] for one in both], 0),
        jnp.concatenate([one[HALF:] for one in both], 0),
    )

def key_parts(ref):
    whole = ref[:, 0]
    count = whole.shape[0]
    early = whole[:, :HALF].reshape(count * HALF, -1)
    late = whole[:, HALF:].reshape(count * HALF, -1)
    return early, late

def weigh(scores):
    peak = jnp.max(scores[0], 0, keepdims=True)
    for more in scores[1:]:
        peak = jnp.maximum(peak, jnp.max(more, 0, keepdims=True))
    powers = [jnp.exp(part - peak) for part in scores]
    total = sum(jnp.sum(part, 0, keepdims=True) for part in powers)
    inverse = 1.0 / total
    return [part * inverse for part in powers]

def split_heads(stacked_early, stacked_late):
    return jnp.concatenate(
        [
            jnp.concatenate([stacked_early[:HALF], stacked_early[HALF:]], 1),
            jnp.concatenate([stacked_late[:HALF], stacked_late[HALF:]], 1),
        ],
        0,
    )

def fill_bias(owner, bias_early, bias_late):
    count = owner.shape[0] - 1

    @pl.when((pl.program_id(0) == 0) & (pl.program_id(1) == 0))
    def fill():
        lead = lax.broadcasted_iota(jnp.int32, (HALF, SEQ_TOK), 0) - (
            lax.broadcasted_iota(jnp.int32, (HALF, SEQ_TOK), 1) % HALF
        )
        for k in range(count):
            gap = (owner[count] - owner[k]) * HALF
            span = slice(k * HALF, (k + 1) * HALF)
            bias_early[span] = jnp.where(lead <= gap, 0.0, NEG)
            bias_late[span] = jnp.where(lead <= -gap, 0.0, NEG)


def attend_kernel(owner, query, keys, out, bias_early, bias_late):
    fill_bias(owner, bias_early, bias_late)
    early, late = key_parts(keys)
    for head in range(2):
        at = head * HEAD_DIM
        k_e, k_l = early[:, at : at + HEAD_DIM], late[:, at : at + HEAD_DIM]
        v_e, v_l = early[:, PAIR + at : PAIR + at + HEAD_DIM], late[:, PAIR + at : PAIR + at + HEAD_DIM]
        q_e, q_l = halves(query, head)
        (p_ee,) = weigh([nt(k_e, q_e) + bias_early[...]])
        p_el, p_ll = weigh([nt(k_e, q_l), nt(k_l, q_l) + bias_late[...]])
        o_e = tn(p_ee.astype(jnp.bfloat16), v_e)
        o_l = tn(p_el.astype(jnp.bfloat16), v_e) + tn(p_ll.astype(jnp.bfloat16), v_l)
        out[0, :, head * PAIR : (head + 1) * PAIR] = split_heads(o_e, o_l).astype(jnp.bfloat16)

def attend_back_kernel(
    owner, query, keys, grad, grad_query, grad_keys, bias_early, bias_late
):
    fill_bias(owner, bias_early, bias_late)
    early, late = key_parts(keys)
    scale = HEAD_DIM ** (-0.5)
    count = keys.shape[0]
    parts_e, parts_l = [], []
    for head in range(2):
        at = head * HEAD_DIM
        k_e, k_l = early[:, at : at + HEAD_DIM], late[:, at : at + HEAD_DIM]
        v_e, v_l = early[:, PAIR + at : PAIR + at + HEAD_DIM], late[:, PAIR + at : PAIR + at + HEAD_DIM]
        q_e, q_l = halves(query, head)
        d_e, d_l = halves(grad, head)
        (p_ee,) = weigh([nt(k_e, q_e) + bias_early[...]])
        p_el, p_ll = weigh([nt(k_e, q_l), nt(k_l, q_l) + bias_late[...]])
        g_ee, g_el, g_ll = nt(v_e, d_e), nt(v_e, d_l), nt(v_l, d_l)
        delta_e = jnp.sum(p_ee * g_ee, 0, keepdims=True)
        delta_l = jnp.sum(p_el * g_el, 0, keepdims=True) + jnp.sum(p_ll * g_ll, 0, keepdims=True)
        s_ee = (p_ee * (g_ee - delta_e)).astype(jnp.bfloat16)
        s_el = (p_el * (g_el - delta_l)).astype(jnp.bfloat16)
        s_ll = (p_ll * (g_ll - delta_l)).astype(jnp.bfloat16)
        gq_e = tn(s_ee, k_e) * scale
        gq_l = (tn(s_el, k_e) + tn(s_ll, k_l)) * scale
        grad_query[0, :, head * PAIR : (head + 1) * PAIR] = split_heads(gq_e, gq_l)
        gk_e = nn(s_ee, q_e) + nn(s_el, q_l)
        gk_l = nn(s_ll, q_l)
        gv_e = nn(p_ee.astype(jnp.bfloat16), d_e) + nn(p_el.astype(jnp.bfloat16), d_l)
        gv_l = nn(p_ll.astype(jnp.bfloat16), d_l)
        parts_e.append((gk_e, gv_e))
        parts_l.append((gk_l, gv_l))
    for parts, start in ((parts_e, 0), (parts_l, HALF)):
        for kind in range(2):
            joined = jnp.concatenate([parts[0][kind], parts[1][kind]], 1)
            grad_keys[:, 0, start : start + HALF, kind * PAIR : (kind + 1) * PAIR] = (
                joined.astype(jnp.bfloat16).reshape(count, HALF, PAIR)
            )

def attend_specs(count):
    scalars = pl.BlockSpec(memory_space=pltpu.SMEM)
    rows = pl.BlockSpec((1, SEQ_TOK, 2 * PAIR), lambda s, j: (s, 0, j))
    keys = pl.BlockSpec((count, 1, SEQ_TOK, 2 * PAIR), lambda s, j: (0, s, 0, j))
    scratch = [pltpu.VMEM((count * HALF, SEQ_TOK), jnp.float32)] * 2
    return scalars, rows, keys, scratch


def attend(owner, query, keys):
    count = keys.shape[0]
    scalars, rows, key_rows, scratch = attend_specs(count)
    return pl.pallas_call(
        attend_kernel,
        out_shape=jax.ShapeDtypeStruct(query.shape, jnp.bfloat16),
        grid=(SEQ_GRP, KV_HEADS // 2),
        in_specs=[scalars, rows, key_rows],
        out_specs=rows,
        scratch_shapes=scratch,
        cost_estimate=pl.CostEstimate(
            flops=20 * query.size * count * SEQ_TOK,
            bytes_accessed=2 * keys.size + 4 * query.size,
            transcendentals=0,
        ),
    )(owner, query, keys)


def attend_back(owner, query, keys, grad):
    count = keys.shape[0]
    scalars, rows, key_rows, scratch = attend_specs(count)
    return pl.pallas_call(
        attend_back_kernel,
        out_shape=(
            jax.ShapeDtypeStruct(query.shape, jnp.float32),
            jax.ShapeDtypeStruct(keys.shape, jnp.bfloat16),
        ),
        grid=(SEQ_GRP, KV_HEADS // 2),
        in_specs=[scalars, rows, key_rows, rows],
        out_specs=(rows, key_rows),
        scratch_shapes=scratch,
        cost_estimate=pl.CostEstimate(
            flops=30 * query.size * count * SEQ_TOK,
            bytes_accessed=4 * keys.size + 8 * query.size,
            transcendentals=0,
        ),
    )(owner, query, keys, grad)


def shards(
    tokens,
    routes,
    in_weight,
    out_weight,
    first_gain,
    second_gain,
    router_weight,
    gate_weight,
    up_weight,
    down_weight,
    cotangent,
):
    ctx_count = lax.axis_size("ctx")
    length = SEQ_TOK * ctx_count
    rows = SEQ_GRP * SEQ_TOK
    width_q = HEADS * HEAD_DIM
    width_k = KV_HEADS * HEAD_DIM
    my_index = lax.axis_index("ctx")
    order = ring_order(ctx_count)
    table = [
        [order[(order.index(c) - k) % ctx_count] for k in range(ctx_count)] + [c]
        for c in range(ctx_count)
    ]
    owner = lax.dynamic_index_in_dim(jnp.array(table, jnp.int32), my_index, 0, False)
    local_place = dealt(my_index * SEQ_TOK + jnp.arange(SEQ_TOK, dtype=jnp.int32), length)
    upstream = cotangent.reshape(rows, D)
    chosen = jnp.any(
        routes.reshape(rows, TOP).T[:, None, :] == jnp.arange(EXPERTS, dtype=jnp.int32)[:, None], 0
    )
    chosen_all = lax.all_gather(chosen.astype(jnp.bfloat16), "ctx", axis=0, tiled=False)
    gate_full, up_full, down_full = (
        lax.all_gather(gate_weight, "wsh", axis=2, tiled=True),
        lax.all_gather(up_weight, "wsh", axis=2, tiled=True),
        lax.all_gather(down_weight, "wsh", axis=1, tiled=True),
    )
    inputs = tokens.astype(jnp.float32).reshape(rows, D)
    scale_one = lax.rsqrt(jnp.mean(inputs * inputs, -1, keepdims=True) + EPS)
    normed = (inputs * scale_one * first_gain).astype(jnp.bfloat16)
    mixed = jnp.dot(normed, in_weight, preferred_element_type=jnp.float32).reshape(
        SEQ_GRP, SEQ_TOK, -1
    )
    query = rotate(
        mixed[..., :width_q].reshape(SEQ_GRP, SEQ_TOK, HEADS, HEAD_DIM), local_place, 1.0
    ).astype(jnp.bfloat16)
    query = (query * jnp.bfloat16(HEAD_DIM ** (-0.5))).reshape(SEQ_GRP, SEQ_TOK, width_q)
    key = rotate(
        mixed[..., width_q : width_q + width_k].reshape(SEQ_GRP, SEQ_TOK, KV_HEADS, HEAD_DIM),
        local_place,
        1.0,
    ).astype(jnp.bfloat16)
    value = mixed[..., width_q + width_k :].astype(jnp.bfloat16)
    pairs = (SEQ_GRP, SEQ_TOK, KV_HEADS // 2, PAIR)
    key_value = jnp.concatenate([key.reshape(pairs), value.reshape(pairs)], -1).reshape(
        SEQ_GRP, SEQ_TOK, 2 * width_k
    )
    whole = jnp.stack([held[0] for held in ring_gather([key_value])])
    attended = attend(owner, query, whole).reshape(rows, width_q)
    resid = inputs + jnp.dot(attended, out_weight, preferred_element_type=jnp.float32)
    scale_two = lax.rsqrt(jnp.mean(resid * resid, -1, keepdims=True) + EPS)
    normed_two = (resid * scale_two * second_gain).astype(jnp.bfloat16)
    blocks = SEQ_GRP * ctx_count
    mine = gate_weight.shape[0]
    chosen_all = jnp.swapaxes(
        jnp.stack(
            [
                lax.dynamic_index_in_dim(chosen_all, owner[k], 0, False)
                for k in range(ctx_count)
            ]
        ),
        0,
        1,
    ).reshape(EXPERTS, blocks, SEQ_TOK)
    chosen_my = lax.dynamic_slice_in_dim(chosen_all, my_index * mine, mine, 0)
    before = (
        jnp.arange(SEQ_TOK, dtype=jnp.int32)[:, None] < jnp.arange(SEQ_TOK, dtype=jnp.int32)[None, :]
    ).astype(jnp.bfloat16)
    ranks = jnp.dot(
        chosen_my.reshape(mine * blocks, SEQ_TOK), before, preferred_element_type=jnp.float32
    ).reshape(mine, blocks, SEQ_TOK)
    ranks = jnp.where(chosen_my > 0, ranks, -1.0)
    normed_all = jnp.concatenate([held[0] for held in ring_gather([normed_two])])
    cot_all = jnp.concatenate(
        [held[0] for held in ring_gather([lax.optimization_barrier((upstream, whole[:1, :1, :16, :128]))[0]])]
    )
    logits = lax.dot_general(
        router_weight, normed_all, (((0,), (1,)), ((), ())), preferred_element_type=jnp.float32
    )
    taken = chosen_all.reshape(EXPERTS, blocks * SEQ_TOK) > 0
    picked = jnp.where(taken, logits, NEG)
    weights = jnp.where(taken, jnp.exp(picked - jnp.max(picked, 0, keepdims=True)), 0.0)
    gates_all = weights / jnp.sum(weights, 0, keepdims=True)
    gates = gates_all[:, :rows]
    gates_my = lax.dynamic_slice_in_dim(gates_all, my_index * mine, mine, 0).reshape(
        mine, blocks, SEQ_TOK
    )
    slot_ids = jnp.arange(MOST, dtype=jnp.int32).astype(jnp.float32)
    match = ranks[:, :, None, :] == slot_ids[:, None]
    dispatch = match.astype(jnp.bfloat16)
    combine = jnp.where(match, gates_my[:, :, None, :], 0.0).astype(jnp.bfloat16)
    slot_gates = jnp.sum(jnp.where(match, gates_my[:, :, None, :], 0.0), -1).astype(jnp.bfloat16)
    normed_blocks = normed_all.reshape(blocks, SEQ_TOK, D)
    cot_blocks = cot_all.reshape(blocks, SEQ_TOK, D)
    arrived = jnp.einsum(
        "ebmt,btd->ebmd", dispatch, normed_blocks, preferred_element_type=jnp.float32
    ).astype(jnp.bfloat16)
    cot_slots = jnp.einsum(
        "ebmt,btd->ebmd", dispatch, cot_blocks, preferred_element_type=jnp.float32
    ).astype(jnp.bfloat16)
    slots = blocks * MOST
    arrived = arrived.reshape(mine, slots, D)
    cot_slots = cot_slots.reshape(mine, slots, D)
    grad_produced = cot_slots * slot_gates.reshape(mine, slots, 1)
    gate_act = jnp.einsum("erd,edf->erf", arrived, gate_full, preferred_element_type=jnp.float32)
    up_act = jnp.einsum("erd,edf->erf", arrived, up_full, preferred_element_type=jnp.float32)
    sigma = jax.nn.sigmoid(gate_act)
    swish = gate_act * sigma
    hidden = (swish * up_act).astype(jnp.bfloat16)
    produced = jnp.einsum(
        "erf,efd->erd", hidden, down_full, preferred_element_type=jnp.float32
    ).astype(jnp.bfloat16)
    mixed_part = (
        jnp.einsum(
            "ebmt,ebmd->btd",
            combine,
            produced.reshape(mine, blocks, MOST, D),
            preferred_element_type=jnp.float32,
        )
        .astype(jnp.bfloat16)
        .reshape(ctx_count, rows, D)
    )
    mixture = ring_sum(lambda k, p: mixed_part[k], 1)[0]
    layer_out = (resid + mixture).astype(jnp.bfloat16).reshape(SEQ_GRP, SEQ_TOK, D)
    slot_dots = jnp.sum(
        produced.astype(jnp.float32) * cot_slots.astype(jnp.float32), -1
    ).reshape(mine, blocks, MOST)
    gate_dots = jnp.sum(jnp.where(match, slot_dots[..., None], 0.0), 2)
    gate_dots = jnp.swapaxes(gate_dots.reshape(mine, ctx_count, rows), 0, 1)
    dots_all = lax.all_gather(gate_dots, "ctx", axis=0, tiled=False)
    behind = [lax.dynamic_index_in_dim(dots_all, owner[k], 0, False)[-k % ctx_count] for k in range(ctx_count)]
    steps = [jnp.argmax(owner[:ctx_count] == c) for c in range(ctx_count)]
    behind = jnp.stack(behind)
    grad_gates = jnp.concatenate(
        [lax.dynamic_index_in_dim(behind, steps[c], 0, False) for c in range(ctx_count)]
    )
    down_local = jnp.einsum(
        "erf,erd->efd", hidden, grad_produced, preferred_element_type=jnp.float32
    )
    grad_hidden = jnp.einsum(
        "erd,efd->erf", grad_produced, down_full, preferred_element_type=jnp.float32
    ).astype(jnp.bfloat16)
    slope = sigma * (1.0 + gate_act * (1.0 - sigma))
    grad_gate = (grad_hidden * up_act * slope).astype(jnp.bfloat16)
    grad_up = (grad_hidden * swish).astype(jnp.bfloat16)
    gate_local = jnp.einsum(
        "erd,erf->edf", arrived, grad_gate, preferred_element_type=jnp.float32
    )
    up_local = jnp.einsum("erd,erf->edf", arrived, grad_up, preferred_element_type=jnp.float32)
    grad_arrived = jnp.einsum(
        "erf,edf->erd", grad_gate, gate_full, preferred_element_type=jnp.float32
    )
    grad_arrived = (
        grad_arrived
        + jnp.einsum("erf,edf->erd", grad_up, up_full, preferred_element_type=jnp.float32)
    ).astype(jnp.bfloat16)
    sent_part = (
        jnp.einsum(
            "ebmt,ebmd->btd",
            dispatch,
            grad_arrived.reshape(mine, blocks, MOST, D),
            preferred_element_type=jnp.float32,
        )
        .astype(jnp.bfloat16)
        .reshape(ctx_count, rows, D)
    )
    grad_sent = ring_sum(lambda k, p: sent_part[k], 1)[0]
    gate_grad, up_grad, down_grad = (
        lax.psum_scatter(
            gate_local.astype(jnp.bfloat16), "wsh", scatter_dimension=2, tiled=True
        ).astype(jnp.float32),
        lax.psum_scatter(
            up_local.astype(jnp.bfloat16), "wsh", scatter_dimension=2, tiled=True
        ).astype(jnp.float32),
        lax.psum_scatter(
            down_local.astype(jnp.bfloat16), "wsh", scatter_dimension=1, tiled=True
        ).astype(jnp.float32),
    )
    grad_logits = (gates * (grad_gates - jnp.sum(gates * grad_gates, 0, keepdims=True))).astype(
        jnp.bfloat16
    )
    router_local = lax.dot_general(
        normed_two, grad_logits, (((0,), (1,)), ((), ())), preferred_element_type=jnp.float32
    )
    grad_normed_two = grad_sent + lax.dot_general(
        grad_logits, router_weight, (((0,), (1,)), ((), ())), preferred_element_type=jnp.float32
    )
    grad_resid_norm, second_local = norm_back(resid, scale_two, second_gain, grad_normed_two)
    grad_resid = upstream.astype(jnp.float32) + grad_resid_norm
    grad_branch = grad_resid.astype(jnp.bfloat16)
    out_local = lax.dot_general(
        attended, grad_branch, (((0,), (0,)), ((), ())), preferred_element_type=jnp.float32
    )
    grad_attended = lax.dot_general(
        grad_branch, out_weight, (((1,), (1,)), ((), ())), preferred_element_type=jnp.float32
    ).astype(jnp.bfloat16)
    grad_query, grad_whole = attend_back(
        owner,
        query,
        whole,
        grad_attended.reshape(SEQ_GRP, SEQ_TOK, width_q),
    )
    kv_grad = ring_sum(lambda k, p: grad_whole[k], 1)[0].reshape(
        SEQ_GRP, SEQ_TOK, KV_HEADS // 2, 2, PAIR
    )
    grad_query = rotate(grad_query.reshape(SEQ_GRP, SEQ_TOK, HEADS, HEAD_DIM), local_place, -1.0)
    grad_query = grad_query.astype(jnp.bfloat16).reshape(rows, width_q)
    grad_key = rotate(
        kv_grad[:, :, :, 0].reshape(SEQ_GRP, SEQ_TOK, KV_HEADS, HEAD_DIM), local_place, -1.0
    )
    grad_pair = jnp.concatenate(
        [grad_key.reshape(rows, width_k), kv_grad[:, :, :, 1].reshape(rows, width_k)], -1
    ).astype(jnp.bfloat16)
    in_first = lax.dot_general(
        normed, grad_query, (((0,), (0,)), ((), ())), preferred_element_type=jnp.float32
    )
    in_second = lax.dot_general(
        normed, grad_pair, (((0,), (0,)), ((), ())), preferred_element_type=jnp.float32
    )
    grad_normed = lax.dot_general(
        grad_query, in_weight[:, :width_q], (((1,), (1,)), ((), ())), preferred_element_type=jnp.float32
    ) + lax.dot_general(
        grad_pair, in_weight[:, width_q:], (((1,), (1,)), ((), ())), preferred_element_type=jnp.float32
    )
    grad_inputs_norm, first_local = norm_back(inputs, scale_one, first_gain, grad_normed)
    tokens_grad = (grad_resid + grad_inputs_norm).astype(jnp.bfloat16).reshape(SEQ_GRP, SEQ_TOK, D)
    in_first = spread(in_first.astype(jnp.bfloat16), owner)
    in_second = spread(
        jnp.concatenate(
            [in_second, jnp.broadcast_to(first_local[:, None], (D, SEQ_TOK))], -1
        ).astype(jnp.bfloat16),
        owner,
    )
    in_grad = jnp.concatenate([in_first, in_second[:, : 2 * width_k]], -1)
    first_gain_grad = in_second[:, 2 * width_k]
    out_grad = scatter(out_local.astype(jnp.bfloat16))
    small = scatter(jnp.concatenate([router_local, second_local[:, None]], -1))
    router_grad = small[:, :EXPERTS]
    second_gain_grad = small[:, EXPERTS]
    return (
        layer_out,
        tokens_grad,
        in_grad,
        out_grad,
        first_gain_grad,
        second_gain_grad,
        router_grad,
        gate_grad,
        up_grad,
        down_grad,
    )


def solution(mesh):
    placed = (
        P("wsh", "ctx", None),
        P("wsh", "ctx", None),
        P(),
        P(),
        P(),
        P(),
        P(),
        P("ctx", None, "wsh"),
        P("ctx", None, "wsh"),
        P("ctx", "wsh", None),
        P("wsh", "ctx", None),
    )
    return jax.shard_map(
        shards,
        mesh=mesh,
        in_specs=placed,
        out_specs=(
            P("wsh", "ctx", None),
            P("wsh", "ctx", None),
            P(("ctx", "wsh"), None),
            P(("ctx", "wsh"), None),
            P(("ctx", "wsh")),
            P(("ctx", "wsh")),
            P(("ctx", "wsh"), None),
            P("ctx", None, "wsh"),
            P("ctx", None, "wsh"),
            P("ctx", "wsh", None),
        ),
        check_vma=False,
    )
```

```python
import jax
import jax.numpy as jnp
from jax import lax
from jax.experimental import pallas as pl
from jax.experimental.pallas import tpu as pltpu
from jax.sharding import PartitionSpec as P

D = 1024
HEADS = 16
KV_HEADS = 8
HEAD_DIM = 64
EXPERTS = 32
TOP = 8
SEQ_TOK = 128
SEQ_GRP = 2
HALF = 64
MOST = 48


EPS = 1e-05
THETA = 10000.0
NEG = -1e30


def dealt(rows, length):
    owner = rows // SEQ_TOK
    offset = rows % SEQ_TOK
    early = owner * HALF + offset
    late = length - (owner + 1) * HALF + offset - HALF
    return jnp.where(offset < HALF, early, late)


def rotate(values, place, sign):
    half_dim = values.shape[-1] // 2
    freq = THETA ** (-2.0 * jnp.arange(half_dim, dtype=jnp.float32) / values.shape[-1])
    angle = place.astype(jnp.float32)[:, None] * freq[None, :]
    cosine = jnp.cos(angle)[:, None, :]
    sine = sign * jnp.sin(angle)[:, None, :]
    front = values[..., :half_dim]
    back = values[..., half_dim:]
    return jnp.concatenate([front * cosine - back * sine, back * cosine + front * sine], -1)


def norm_back(values, scale, gain, grad_out):
    weighted = grad_out * gain
    grad_in = scale * weighted - values * scale**3 * jnp.mean(weighted * values, -1, keepdims=True)
    return (grad_in, jnp.sum(grad_out * values * scale, 0))


def ring_order(count):
    return list(range(0, count, 2)) + list(reversed(range(1, count, 2)))


def ring_shift(count, step):
    order = ring_order(count)
    return [(order[i], order[(i + step) % count]) for i in range(count)]


def ring_gather(parts):
    count = lax.axis_size("ctx")
    ahead, behind = ring_shift(count, 1), ring_shift(count, -1)
    held = [list(parts)] + [[None] * len(parts) for _ in range(count - 1)]
    far = count // 2
    for p, part in enumerate(parts):
        up, down = part, part
        ups = far if p % 2 == 0 else count - 1 - far
        for step in range(1, far + 1):
            if step <= ups:
                up = lax.ppermute(up, "ctx", ahead)
                held[step][p] = up
            if step <= count - 1 - ups:
                down = lax.ppermute(down, "ctx", behind)
                held[count - step][p] = down
    return held


def add_low(left, right):
    return (left.astype(jnp.float32) + right.astype(jnp.float32)).astype(left.dtype)


def ring_sum(block, parts):
    count = lax.axis_size("ctx")
    ahead, behind = ring_shift(count, 1), ring_shift(count, -1)
    far = count // 2
    sums = []
    for p in range(parts):
        ups = far if p % 2 == 0 else count - 1 - far
        downs = count - 1 - ups
        up = block(count - ups, p)
        for step in range(ups - 1, 0, -1):
            up = add_low(lax.ppermute(up, "ctx", ahead), block(count - step, p))
        up = lax.ppermute(up, "ctx", ahead)
        down = block(downs, p)
        for step in range(downs - 1, 0, -1):
            down = add_low(lax.ppermute(down, "ctx", behind), block(step, p))
        down = lax.ppermute(down, "ctx", behind)
        own = block(0, p).astype(jnp.float32)
        sums.append(up.astype(jnp.float32) + down.astype(jnp.float32) + own)
    return sums


OTHER_CORE = [(0, 1), (1, 0), (2, 3), (3, 2)]
OTHER_CHIP = [(0, 2), (2, 0), (1, 3), (3, 1)]


def pair_sum(pieces):
    own = add_low(pieces[0], lax.ppermute(pieces[2], "wsh", OTHER_CORE))
    other = add_low(pieces[1], lax.ppermute(pieces[3], "wsh", OTHER_CORE))
    return own.astype(jnp.float32) + lax.ppermute(other, "wsh", OTHER_CHIP).astype(jnp.float32)


def spread(local, behind):
    count = lax.axis_size("ctx")
    me = lax.axis_index("wsh")
    split = local.reshape(count, 4, local.shape[0] // (4 * count), -1)

    def take(flip):
        return lax.dynamic_index_in_dim(split, me ^ flip, 1, False)

    once = pair_sum([take(0), take(2), take(1), take(3)]).astype(local.dtype)

    def block(k, p):
        return lax.dynamic_index_in_dim(once, behind[k], 0, False)

    return ring_sum(block, 1)[0]


PAIR = 2 * HEAD_DIM
def nt(left, right):
    return lax.dot_general(left, right, (((1,), (1,)), ((), ())), preferred_element_type=jnp.float32)
def tn(left, right):
    return lax.dot_general(left, right, (((0,), (0,)), ((), ())), preferred_element_type=jnp.float32)
def nn(left, right):
    return jnp.dot(left, right, preferred_element_type=jnp.float32)

def halves(ref, head):
    start = head * PAIR
    block = ref[0, :, start : start + PAIR]
    both = [block[:, :HEAD_DIM], block[:, HEAD_DIM:]]
    return (
        jnp.concatenate([one[:HALF] for one in both], 0),
        jnp.concatenate([one[HALF:] for one in both], 0),
    )

def key_parts(ref):
    whole = ref[...]
    count = whole.shape[0]
    early = whole[:, :HALF].reshape(count * HALF, -1)
    late = whole[:, HALF:].reshape(count * HALF, -1)
    return early, late

def weigh(scores):
    peak = jnp.max(scores[0], 0, keepdims=True)
    for more in scores[1:]:
        peak = jnp.maximum(peak, jnp.max(more, 0, keepdims=True))
    powers = [jnp.exp(part - peak) for part in scores]
    total = sum(jnp.sum(part, 0, keepdims=True) for part in powers)
    inverse = 1.0 / total
    return [part * inverse for part in powers]

def split_heads(stacked_early, stacked_late):
    return jnp.concatenate(
        [
            jnp.concatenate([stacked_early[:HALF], stacked_early[HALF:]], 1),
            jnp.concatenate([stacked_late[:HALF], stacked_late[HALF:]], 1),
        ],
        0,
    )

def fill_bias(owner, bias_early, bias_late):
    count = owner.shape[0] - 1

    @pl.when((pl.program_id(0) == 0) & (pl.program_id(1) == 0))
    def fill():
        lead = lax.broadcasted_iota(jnp.int32, (HALF, SEQ_TOK), 0) - (
            lax.broadcasted_iota(jnp.int32, (HALF, SEQ_TOK), 1) % HALF
        )
        for k in range(count):
            gap = (owner[count] - owner[k]) * HALF
            span = slice(k * HALF, (k + 1) * HALF)
            bias_early[span] = jnp.where(lead <= gap, 0.0, NEG)
            bias_late[span] = jnp.where(lead <= -gap, 0.0, NEG)


def attend_kernel(owner, query, keys, out, bias_early, bias_late):
    fill_bias(owner, bias_early, bias_late)
    early, late = key_parts(keys)
    for head in range(2):
        at = head * HEAD_DIM
        k_e, k_l = early[:, at : at + HEAD_DIM], late[:, at : at + HEAD_DIM]
        v_e, v_l = early[:, PAIR + at : PAIR + at + HEAD_DIM], late[:, PAIR + at : PAIR + at + HEAD_DIM]
        q_e, q_l = halves(query, head)
        (p_ee,) = weigh([nt(k_e, q_e) + bias_early[...]])
        p_el, p_ll = weigh([nt(k_e, q_l), nt(k_l, q_l) + bias_late[...]])
        o_e = tn(p_ee.astype(jnp.bfloat16), v_e)
        o_l = tn(p_el.astype(jnp.bfloat16), v_e) + tn(p_ll.astype(jnp.bfloat16), v_l)
        out[0, :, head * PAIR : (head + 1) * PAIR] = split_heads(o_e, o_l).astype(jnp.bfloat16)

def attend_back_kernel(
    owner, query, keys, grad, grad_query, grad_keys, bias_early, bias_late
):
    fill_bias(owner, bias_early, bias_late)
    early, late = key_parts(keys)
    scale = HEAD_DIM ** (-0.5)
    count = keys.shape[0]
    parts_e, parts_l = [], []
    for head in range(2):
        at = head * HEAD_DIM
        k_e, k_l = early[:, at : at + HEAD_DIM], late[:, at : at + HEAD_DIM]
        v_e, v_l = early[:, PAIR + at : PAIR + at + HEAD_DIM], late[:, PAIR + at : PAIR + at + HEAD_DIM]
        q_e, q_l = halves(query, head)
        d_e, d_l = halves(grad, head)
        (p_ee,) = weigh([nt(k_e, q_e) + bias_early[...]])
        p_el, p_ll = weigh([nt(k_e, q_l), nt(k_l, q_l) + bias_late[...]])
        g_ee, g_el, g_ll = nt(v_e, d_e), nt(v_e, d_l), nt(v_l, d_l)
        delta_e = jnp.sum(p_ee * g_ee, 0, keepdims=True)
        delta_l = jnp.sum(p_el * g_el, 0, keepdims=True) + jnp.sum(p_ll * g_ll, 0, keepdims=True)
        s_ee = (p_ee * (g_ee - delta_e)).astype(jnp.bfloat16)
        s_el = (p_el * (g_el - delta_l)).astype(jnp.bfloat16)
        s_ll = (p_ll * (g_ll - delta_l)).astype(jnp.bfloat16)
        gq_e = tn(s_ee, k_e) * scale
        gq_l = (tn(s_el, k_e) + tn(s_ll, k_l)) * scale
        grad_query[0, :, head * PAIR : (head + 1) * PAIR] = split_heads(gq_e, gq_l)
        gk_e = nn(s_ee, q_e) + nn(s_el, q_l)
        gk_l = nn(s_ll, q_l)
        gv_e = nn(p_ee.astype(jnp.bfloat16), d_e) + nn(p_el.astype(jnp.bfloat16), d_l)
        gv_l = nn(p_ll.astype(jnp.bfloat16), d_l)
        parts_e.append((gk_e, gv_e))
        parts_l.append((gk_l, gv_l))
    for parts, start in ((parts_e, 0), (parts_l, HALF)):
        for kind in range(2):
            joined = jnp.concatenate([parts[0][kind], parts[1][kind]], 1)
            grad_keys[:, start : start + HALF, kind * PAIR : (kind + 1) * PAIR] = (
                joined.astype(jnp.bfloat16).reshape(count, HALF, PAIR)
            )

def attend_specs(count):
    scalars = pl.BlockSpec(memory_space=pltpu.SMEM)
    rows = pl.BlockSpec((1, SEQ_TOK, 2 * PAIR), lambda s, j: (s, 0, j))
    keys = pl.BlockSpec((count, SEQ_TOK, 2 * PAIR), lambda s, j: (0, s, j))
    scratch = [pltpu.VMEM((count * HALF, SEQ_TOK), jnp.float32)] * 2
    return scalars, rows, keys, scratch


def attend(owner, query, keys):
    count = keys.shape[0]
    scalars, rows, key_rows, scratch = attend_specs(count)
    return pl.pallas_call(
        attend_kernel,
        out_shape=jax.ShapeDtypeStruct(query.shape, jnp.bfloat16),
        grid=(SEQ_GRP, KV_HEADS // 2),
        in_specs=[scalars, rows, key_rows],
        out_specs=rows,
        scratch_shapes=scratch,
        cost_estimate=pl.CostEstimate(
            flops=20 * query.size * count * SEQ_TOK,
            bytes_accessed=2 * keys.size + 4 * query.size,
            transcendentals=0,
        ),
    )(owner, query, keys)


def attend_back(owner, query, keys, grad):
    count = keys.shape[0]
    scalars, rows, key_rows, scratch = attend_specs(count)
    return pl.pallas_call(
        attend_back_kernel,
        out_shape=(
            jax.ShapeDtypeStruct(query.shape, jnp.float32),
            jax.ShapeDtypeStruct((count, SEQ_GRP * SEQ_TOK, keys.shape[2]), jnp.bfloat16),
        ),
        grid=(SEQ_GRP, KV_HEADS // 2),
        in_specs=[scalars, rows, key_rows, rows],
        out_specs=(rows, key_rows),
        scratch_shapes=scratch,
        cost_estimate=pl.CostEstimate(
            flops=30 * query.size * count * SEQ_TOK,
            bytes_accessed=4 * keys.size + 8 * query.size,
            transcendentals=0,
        ),
    )(owner, query, keys, grad)


STEP_BLOCKS = 16


def expert_kernel(
    arrived_ref,
    cot_ref,
    slot_gate_ref,
    gate_ref,
    up_ref,
    down_ref,
    produced_ref,
    back_ref,
    dots_ref,
    gate_grad_ref,
    up_grad_ref,
    down_grad_ref,
    *sums,
):
    rows = arrived_ref.shape[0] * MOST
    arrived = arrived_ref[:, 0].reshape(rows, D)
    cot = cot_ref[:, 0].reshape(rows, D)
    gate_w, up_w, down_w = gate_ref[0], up_ref[0], down_ref[0]
    gate_act = nn(arrived, gate_w)
    up_act = nn(arrived, up_w)
    sigma = jax.nn.sigmoid(gate_act)
    swish = gate_act * sigma
    hidden = (swish * up_act).astype(jnp.bfloat16)
    produced = nn(hidden, down_w).astype(jnp.bfloat16)
    produced_ref[:, 0] = produced.reshape(-1, MOST, D)
    wide = cot.astype(jnp.float32)
    dots = jnp.sum(produced.astype(jnp.float32) * wide, -1, keepdims=True)
    dots_ref[:, 0] = dots.reshape(-1, MOST, 1)
    grad_produced = (wide * slot_gate_ref[:, 0].reshape(rows, 1)).astype(jnp.bfloat16)
    grad_hidden = nt(grad_produced, down_w).astype(jnp.bfloat16).astype(jnp.float32)
    slope = sigma * (1.0 + gate_act * (1.0 - sigma))
    grad_gate = (grad_hidden * up_act * slope).astype(jnp.bfloat16)
    grad_up = (grad_hidden * swish).astype(jnp.bfloat16)
    back = nt(grad_gate, gate_w) + nt(grad_up, up_w)
    back_ref[:, 0] = back.astype(jnp.bfloat16).reshape(-1, MOST, D)
    grads = [tn(arrived, grad_gate), tn(arrived, grad_up), tn(hidden, grad_produced)]
    if sums:
        first = pl.program_id(1) == 0
        for held, grad in zip(sums, grads):
            held[...] = jnp.where(first, grad, held[...] + grad)
        grads = [held[...] for held in sums]
    quarter = gate_w.shape[1] // 4
    for k in range(4):
        span = slice(k * quarter, (k + 1) * quarter)
        gate_grad_ref[k, 0] = grads[0][:, span].astype(jnp.bfloat16)
        up_grad_ref[k, 0] = grads[1][:, span].astype(jnp.bfloat16)
        down_grad_ref[k, 0] = grads[2][span].astype(jnp.bfloat16)


def experts_pass(arrived, cot, slot_gates, gate_w, up_w, down_w):
    blocks, mine = arrived.shape[:2]
    steps = blocks // STEP_BLOCKS
    hidden = gate_w.shape[2]
    quarter = hidden // 4

    def slot_rows(width):
        return pl.BlockSpec((STEP_BLOCKS, 1, MOST, width), lambda e, c: (c, e, 0, 0))

    def per_expert(*shape):
        return pl.BlockSpec((1,) + shape, lambda e, c: (e, 0, 0))

    def pieces(*shape):
        return pl.BlockSpec((4, 1) + shape, lambda e, c: (0, e, 0, 0))

    low = jnp.bfloat16
    return pl.pallas_call(
        expert_kernel,
        grid=(mine, steps),
        in_specs=[
            slot_rows(D),
            slot_rows(D),
            slot_rows(1),
            per_expert(D, hidden),
            per_expert(D, hidden),
            per_expert(hidden, D),
        ],
        out_specs=(
            slot_rows(D),
            slot_rows(D),
            slot_rows(1),
            pieces(D, quarter),
            pieces(D, quarter),
            pieces(quarter, D),
        ),
        out_shape=(
            jax.ShapeDtypeStruct(arrived.shape, low),
            jax.ShapeDtypeStruct(arrived.shape, low),
            jax.ShapeDtypeStruct(slot_gates.shape, jnp.float32),
            jax.ShapeDtypeStruct((4, mine, D, quarter), low),
            jax.ShapeDtypeStruct((4, mine, D, quarter), low),
            jax.ShapeDtypeStruct((4, mine, quarter, D), low),
        ),
        scratch_shapes=[]
        if steps == 1
        else [
            pltpu.VMEM((D, hidden), jnp.float32),
            pltpu.VMEM((D, hidden), jnp.float32),
            pltpu.VMEM((hidden, D), jnp.float32),
        ],
        compiler_params=pltpu.CompilerParams(vmem_limit_bytes=63 * 1024 * 1024),
        cost_estimate=pl.CostEstimate(
            flops=18 * arrived.size * hidden,
            bytes_accessed=8 * arrived.size + 12 * mine * D * hidden,
            transcendentals=0,
        ),
    )(arrived, cot, slot_gates, gate_w, up_w, down_w)


def shards(
    tokens,
    routes,
    in_weight,
    out_weight,
    first_gain,
    second_gain,
    router_weight,
    gate_weight,
    up_weight,
    down_weight,
    cotangent,
):
    ctx_count = lax.axis_size("ctx")
    length = SEQ_TOK * ctx_count
    rows = SEQ_GRP * SEQ_TOK
    width_q = HEADS * HEAD_DIM
    width_k = KV_HEADS * HEAD_DIM
    my_index = lax.axis_index("ctx")
    order = ring_order(ctx_count)
    table = [
        [order[(order.index(c) - k) % ctx_count] for k in range(ctx_count)] + [c]
        for c in range(ctx_count)
    ]
    owner = lax.dynamic_index_in_dim(jnp.array(table, jnp.int32), my_index, 0, False)
    local_place = dealt(my_index * SEQ_TOK + jnp.arange(SEQ_TOK, dtype=jnp.int32), length)
    upstream = cotangent.reshape(rows, D)
    chosen = jnp.any(
        routes.reshape(rows, TOP).T[:, None, :] == jnp.arange(EXPERTS, dtype=jnp.int32)[:, None], 0
    )
    gate_full, up_full, down_full = (
        lax.all_gather(gate_weight, "wsh", axis=2, tiled=True),
        lax.all_gather(up_weight, "wsh", axis=2, tiled=True),
        lax.all_gather(down_weight, "wsh", axis=1, tiled=True),
    )
    inputs = tokens.astype(jnp.float32).reshape(rows, D)
    scale_one = lax.rsqrt(jnp.mean(inputs * inputs, -1, keepdims=True) + EPS)
    normed = (inputs * scale_one * first_gain).astype(jnp.bfloat16)
    mixed = jnp.dot(normed, in_weight, preferred_element_type=jnp.float32).reshape(
        SEQ_GRP, SEQ_TOK, -1
    )
    query = rotate(
        mixed[..., :width_q].reshape(SEQ_GRP, SEQ_TOK, HEADS, HEAD_DIM), local_place, 1.0
    ).astype(jnp.bfloat16)
    query = (query * jnp.bfloat16(HEAD_DIM ** (-0.5))).reshape(SEQ_GRP, SEQ_TOK, width_q)
    key = rotate(
        mixed[..., width_q : width_q + width_k].reshape(SEQ_GRP, SEQ_TOK, KV_HEADS, HEAD_DIM),
        local_place,
        1.0,
    ).astype(jnp.bfloat16)
    value = mixed[..., width_q + width_k :].astype(jnp.bfloat16)
    pairs = (SEQ_GRP, SEQ_TOK, KV_HEADS // 2, PAIR)
    key_value = jnp.concatenate([key.reshape(pairs), value.reshape(pairs)], -1).reshape(
        rows, 2 * width_k
    )
    flags = chosen.astype(jnp.bfloat16).reshape(-1, 2 * width_k)
    flag_rows = flags.shape[0]
    flags = jnp.concatenate([flags, jnp.zeros_like(flags)], 0)
    whole = jnp.stack(
        [held[0] for held in ring_gather([jnp.concatenate([key_value, flags], 0)])]
    )
    attended = attend(owner, query, whole).reshape(rows, width_q)
    resid = inputs + jnp.dot(attended, out_weight, preferred_element_type=jnp.float32)
    scale_two = lax.rsqrt(jnp.mean(resid * resid, -1, keepdims=True) + EPS)
    normed_two = (resid * scale_two * second_gain).astype(jnp.bfloat16)
    blocks = SEQ_GRP * ctx_count
    mine = gate_weight.shape[0]
    chosen_all = whole[:, rows : rows + flag_rows].reshape(ctx_count, EXPERTS, rows)
    chosen_my = lax.dynamic_slice_in_dim(chosen_all, my_index * mine, mine, 1)

    def by_block(values):
        split = values.reshape(ctx_count, mine, SEQ_GRP, SEQ_TOK)
        return jnp.swapaxes(split, 1, 2).reshape(blocks, mine, SEQ_TOK)

    chosen_my = by_block(chosen_my)
    before = (
        jnp.arange(SEQ_TOK, dtype=jnp.int32)[:, None] < jnp.arange(SEQ_TOK, dtype=jnp.int32)[None, :]
    ).astype(jnp.bfloat16)
    ranks = jnp.dot(
        chosen_my.reshape(blocks * mine, SEQ_TOK), before, preferred_element_type=jnp.float32
    ).reshape(blocks, mine, SEQ_TOK)
    ranks = jnp.where(chosen_my > 0, ranks, -1.0)
    normed_all = jnp.concatenate([held[0] for held in ring_gather([normed_two])])
    cot_late = lax.optimization_barrier((upstream[SEQ_TOK:], whole[:1, :16, :128]))[0]
    cot_rings = (ring_gather([upstream[:SEQ_TOK]]), ring_gather([cot_late]))
    cot_all = jnp.concatenate([ring[k][0] for k in range(ctx_count) for ring in cot_rings])
    logits = lax.dot_general(
        router_weight, normed_all, (((0,), (1,)), ((), ())), preferred_element_type=jnp.float32
    )
    taken = jnp.swapaxes(chosen_all, 0, 1).reshape(EXPERTS, blocks * SEQ_TOK) > 0
    picked = jnp.where(taken, logits, NEG)
    weights = jnp.where(taken, jnp.exp(picked - jnp.max(picked, 0, keepdims=True)), 0.0)
    gates_all = weights / jnp.sum(weights, 0, keepdims=True)
    gates = gates_all[:, :rows]
    gates_my = lax.dynamic_slice_in_dim(gates_all, my_index * mine, mine, 0)
    gates_my = by_block(jnp.swapaxes(gates_my.reshape(mine, ctx_count, rows), 0, 1))
    slot_ids = jnp.arange(MOST, dtype=jnp.int32).astype(jnp.float32)
    match = ranks[:, :, None, :] == slot_ids[:, None]
    chances = jnp.where(match, gates_my[:, :, None, :], 0.0)
    dispatch = match.astype(jnp.bfloat16).reshape(blocks, mine * MOST, SEQ_TOK)
    combine = chances.astype(jnp.bfloat16).reshape(blocks, mine * MOST, SEQ_TOK)
    slot_gates = jnp.sum(chances, -1, keepdims=True).astype(jnp.bfloat16).astype(jnp.float32)
    normed_blocks = normed_all.reshape(blocks, SEQ_TOK, D)
    cot_blocks = cot_all.reshape(blocks, SEQ_TOK, D)
    slot_shape = (blocks, mine, MOST, D)
    arrived, cot_slots = (
        jnp.einsum("bst,btd->bsd", dispatch, one, preferred_element_type=jnp.float32)
        .astype(jnp.bfloat16)
        .reshape(slot_shape)
        for one in (normed_blocks, cot_blocks)
    )
    produced, grad_arrived, slot_dots, gate_local, up_local, down_local = experts_pass(
        arrived, cot_slots, slot_gates, gate_full, up_full, down_full
    )
    gate_dots = jnp.sum(jnp.where(match, slot_dots, 0.0), 2)
    gate_dots = jnp.swapaxes(gate_dots.reshape(ctx_count, SEQ_GRP, mine, SEQ_TOK), 1, 2)
    ours = jnp.arange(EXPERTS, dtype=jnp.int32)[:, None] // mine == my_index
    gate_dots = jnp.where(
        ours, jnp.tile(gate_dots.reshape(ctx_count, mine, rows), (1, EXPERTS // mine, 1)), 0.0
    ).reshape(ctx_count, flag_rows, D)
    coarse = lax.reduce_precision(gate_dots, 8, 7)

    def to_tokens(matrix, slot_values):
        return jnp.einsum(
            "bst,bsd->btd",
            matrix,
            slot_values.reshape(blocks, mine * MOST, D),
            preferred_element_type=jnp.float32,
        ).astype(jnp.bfloat16).reshape(ctx_count, rows, D)

    sent_part = jnp.concatenate(
        [
            to_tokens(dispatch, grad_arrived),
            coarse.astype(jnp.bfloat16),
            (gate_dots - coarse).astype(jnp.bfloat16),
        ],
        1,
    )
    grad_sent = ring_sum(lambda k, p: sent_part[k], 1)[0]
    grad_gates = (
        grad_sent[rows : rows + flag_rows] + grad_sent[rows + flag_rows :]
    ).reshape(EXPERTS, rows)
    grad_sent = grad_sent[:rows]
    mixed_part = to_tokens(combine, produced)
    mixed_part = lax.optimization_barrier((mixed_part, grad_sent[:8, :128]))[0]
    mixture = ring_sum(lambda k, p: mixed_part[k], 1)[0]
    layer_out = (resid + mixture).astype(jnp.bfloat16).reshape(SEQ_GRP, SEQ_TOK, D)
    gate_grad, up_grad, down_grad = (
        lax.psum_scatter(local, "wsh", scatter_dimension=0).astype(jnp.float32)
        for local in (gate_local, up_local, down_local)
    )
    grad_logits = (gates * (grad_gates - jnp.sum(gates * grad_gates, 0, keepdims=True))).astype(
        jnp.bfloat16
    )
    router_local = lax.dot_general(
        normed_two, grad_logits, (((0,), (1,)), ((), ())), preferred_element_type=jnp.float32
    )
    grad_normed_two = grad_sent + lax.dot_general(
        grad_logits, router_weight, (((0,), (1,)), ((), ())), preferred_element_type=jnp.float32
    )
    grad_resid_norm, second_local = norm_back(resid, scale_two, second_gain, grad_normed_two)
    grad_resid = upstream.astype(jnp.float32) + grad_resid_norm
    grad_branch = grad_resid.astype(jnp.bfloat16)
    out_local = lax.dot_general(
        attended, grad_branch, (((0,), (0,)), ((), ())), preferred_element_type=jnp.float32
    )
    grad_attended = lax.dot_general(
        grad_branch, out_weight, (((1,), (1,)), ((), ())), preferred_element_type=jnp.float32
    ).astype(jnp.bfloat16)
    grad_query, grad_whole = attend_back(
        owner,
        query,
        whole,
        grad_attended.reshape(SEQ_GRP, SEQ_TOK, width_q),
    )
    kv_grad = ring_sum(lambda k, p: grad_whole[k], 1)[0].reshape(
        SEQ_GRP, SEQ_TOK, KV_HEADS // 2, 2, PAIR
    )
    grad_query = rotate(grad_query.reshape(SEQ_GRP, SEQ_TOK, HEADS, HEAD_DIM), local_place, -1.0)
    grad_query = grad_query.astype(jnp.bfloat16).reshape(rows, width_q)
    grad_key = rotate(
        kv_grad[:, :, :, 0].reshape(SEQ_GRP, SEQ_TOK, KV_HEADS, HEAD_DIM), local_place, -1.0
    )
    grad_pair = jnp.concatenate(
        [grad_key.reshape(rows, width_k), kv_grad[:, :, :, 1].reshape(rows, width_k)], -1
    ).astype(jnp.bfloat16)
    in_first = lax.dot_general(
        normed, grad_query, (((0,), (0,)), ((), ())), preferred_element_type=jnp.float32
    )
    in_second = lax.dot_general(
        normed, grad_pair, (((0,), (0,)), ((), ())), preferred_element_type=jnp.float32
    )
    grad_normed = lax.dot_general(
        grad_query, in_weight[:, :width_q], (((1,), (1,)), ((), ())), preferred_element_type=jnp.float32
    ) + lax.dot_general(
        grad_pair, in_weight[:, width_q:], (((1,), (1,)), ((), ())), preferred_element_type=jnp.float32
    )
    grad_inputs_norm, first_local = norm_back(inputs, scale_one, first_gain, grad_normed)
    tokens_grad = (grad_resid + grad_inputs_norm).astype(jnp.bfloat16).reshape(SEQ_GRP, SEQ_TOK, D)
    low = jnp.bfloat16
    early = spread(
        jnp.concatenate(
            [
                in_first.astype(low),
                out_local.astype(low),
                router_local.astype(low),
                second_local[:, None].astype(low),
                jnp.zeros((D, SEQ_TOK - EXPERTS - 1), low),
            ],
            -1,
        ),
        owner,
    )
    in_second = spread(
        jnp.concatenate(
            [in_second, jnp.broadcast_to(first_local[:, None], (D, SEQ_TOK))], -1
        ).astype(jnp.bfloat16),
        owner,
    )
    in_grad = jnp.concatenate([early[:, :width_q], in_second[:, : 2 * width_k]], -1)
    first_gain_grad = in_second[:, 2 * width_k]
    out_grad = early[:, width_q : width_q + D]
    small = early[:, width_q + D :]
    router_grad = small[:, :EXPERTS]
    second_gain_grad = small[:, EXPERTS]
    return (
        layer_out,
        tokens_grad,
        in_grad,
        out_grad,
        first_gain_grad,
        second_gain_grad,
        router_grad,
        gate_grad,
        up_grad,
        down_grad,
    )


def solution(mesh):
    placed = (
        P("wsh", "ctx", None),
        P("wsh", "ctx", None),
        P(),
        P(),
        P(),
        P(),
        P(),
        P("ctx", None, "wsh"),
        P("ctx", None, "wsh"),
        P("ctx", "wsh", None),
        P("wsh", "ctx", None),
    )
    return jax.shard_map(
        shards,
        mesh=mesh,
        in_specs=placed,
        out_specs=(
            P("wsh", "ctx", None),
            P("wsh", "ctx", None),
            P(("ctx", "wsh"), None),
            P(("ctx", "wsh"), None),
            P(("ctx", "wsh")),
            P(("ctx", "wsh")),
            P(("ctx", "wsh"), None),
            P("ctx", None, "wsh"),
            P("ctx", None, "wsh"),
            P("ctx", "wsh", None),
        ),
        check_vma=False,
    )
```

```python
import jax
import jax.numpy as jnp
from jax import lax
from jax.experimental import pallas as pl
from jax.experimental.pallas import tpu as pltpu
from jax.sharding import PartitionSpec as P

D = 1024
HEADS = 16
KV_HEADS = 8
HEAD_DIM = 64
EXPERTS = 32
TOP = 8
SEQ_TOK = 128
SEQ_GRP = 2
HALF = 64
MOST = 48


EPS = 1e-05
THETA = 10000.0
NEG = -1e30


def dealt(rows, length):
    owner = rows // SEQ_TOK
    offset = rows % SEQ_TOK
    early = owner * HALF + offset
    late = length - (owner + 1) * HALF + offset - HALF
    return jnp.where(offset < HALF, early, late)


def rotate(values, place, sign):
    half_dim = values.shape[-1] // 2
    freq = THETA ** (-2.0 * jnp.arange(half_dim, dtype=jnp.float32) / values.shape[-1])
    angle = place.astype(jnp.float32)[:, None] * freq[None, :]
    cosine = jnp.cos(angle)[:, None, :]
    sine = sign * jnp.sin(angle)[:, None, :]
    front = values[..., :half_dim]
    back = values[..., half_dim:]
    return jnp.concatenate([front * cosine - back * sine, back * cosine + front * sine], -1)


def norm_back(values, scale, gain, grad_out):
    weighted = grad_out * gain
    grad_in = scale * weighted - values * scale**3 * jnp.mean(weighted * values, -1, keepdims=True)
    return (grad_in, jnp.sum(grad_out * values * scale, 0))


def ring_order(count):
    return list(range(0, count, 2)) + list(reversed(range(1, count, 2)))


def ring_shift(count, step):
    order = ring_order(count)
    return [(order[i], order[(i + step) % count]) for i in range(count)]


def ring_gather(parts):
    count = lax.axis_size("ctx")
    ahead, behind = ring_shift(count, 1), ring_shift(count, -1)
    held = [list(parts)] + [[None] * len(parts) for _ in range(count - 1)]
    far = count // 2
    for p, part in enumerate(parts):
        up, down = part, part
        ups = far if p % 2 == 0 else count - 1 - far
        for step in range(1, far + 1):
            if step <= ups:
                up = lax.ppermute(up, "ctx", ahead)
                held[step][p] = up
            if step <= count - 1 - ups:
                down = lax.ppermute(down, "ctx", behind)
                held[count - step][p] = down
    return held


def add_low(left, right):
    return (left.astype(jnp.float32) + right.astype(jnp.float32)).astype(left.dtype)


def ring_sum(block, parts):
    count = lax.axis_size("ctx")
    ahead, behind = ring_shift(count, 1), ring_shift(count, -1)
    far = count // 2
    sums = []
    for p in range(parts):
        ups = far if p % 2 == 0 else count - 1 - far
        downs = count - 1 - ups
        up = block(count - ups, p)
        for step in range(ups - 1, 0, -1):
            up = add_low(lax.ppermute(up, "ctx", ahead), block(count - step, p))
        up = lax.ppermute(up, "ctx", ahead)
        down = block(downs, p)
        for step in range(downs - 1, 0, -1):
            down = add_low(lax.ppermute(down, "ctx", behind), block(step, p))
        down = lax.ppermute(down, "ctx", behind)
        own = block(0, p).astype(jnp.float32)
        sums.append(up.astype(jnp.float32) + down.astype(jnp.float32) + own)
    return sums


OTHER_CORE = [(0, 1), (1, 0), (2, 3), (3, 2)]
OTHER_CHIP = [(0, 2), (2, 0), (1, 3), (3, 1)]


def pair_sum(pieces):
    own = add_low(pieces[0], lax.ppermute(pieces[2], "wsh", OTHER_CORE))
    other = add_low(pieces[1], lax.ppermute(pieces[3], "wsh", OTHER_CORE))
    return own.astype(jnp.float32) + lax.ppermute(other, "wsh", OTHER_CHIP).astype(jnp.float32)


def spread(local, behind):
    count = lax.axis_size("ctx")
    me = lax.axis_index("wsh")
    split = local.reshape(count, 4, local.shape[0] // (4 * count), -1)

    def take(flip):
        return lax.dynamic_index_in_dim(split, me ^ flip, 1, False)

    once = pair_sum([take(0), take(2), take(1), take(3)]).astype(local.dtype)

    def block(k):
        return lax.dynamic_index_in_dim(once, behind[k], 0, False)

    total = block(0).astype(jnp.float32)
    for k in range(1, count):
        total += lax.ppermute(block(count - k), "ctx", ring_shift(count, k)).astype(jnp.float32)
    return total


PAIR = 2 * HEAD_DIM
def nt(left, right):
    return lax.dot_general(left, right, (((1,), (1,)), ((), ())), preferred_element_type=jnp.float32)
def tn(left, right):
    return lax.dot_general(left, right, (((0,), (0,)), ((), ())), preferred_element_type=jnp.float32)
def nn(left, right):
    return jnp.dot(left, right, preferred_element_type=jnp.float32)

def halves(ref, head):
    start = head * PAIR
    block = ref[0, :, start : start + PAIR]
    both = [block[:, :HEAD_DIM], block[:, HEAD_DIM:]]
    return (
        jnp.concatenate([one[:HALF] for one in both], 0),
        jnp.concatenate([one[HALF:] for one in both], 0),
    )

def key_parts(ref):
    whole = ref[...]
    count = whole.shape[0]
    early = whole[:, :HALF].reshape(count * HALF, -1)
    late = whole[:, HALF:].reshape(count * HALF, -1)
    return early, late

def weigh(scores):
    peak = jnp.max(scores[0], 0, keepdims=True)
    for more in scores[1:]:
        peak = jnp.maximum(peak, jnp.max(more, 0, keepdims=True))
    powers = [jnp.exp(part - peak) for part in scores]
    total = sum(jnp.sum(part, 0, keepdims=True) for part in powers)
    inverse = 1.0 / total
    return [part * inverse for part in powers]

def split_heads(stacked_early, stacked_late):
    return jnp.concatenate(
        [
            jnp.concatenate([stacked_early[:HALF], stacked_early[HALF:]], 1),
            jnp.concatenate([stacked_late[:HALF], stacked_late[HALF:]], 1),
        ],
        0,
    )

def fill_bias(owner, bias_early, bias_late):
    count = owner.shape[0] - 1

    @pl.when((pl.program_id(0) == 0) & (pl.program_id(1) == 0))
    def fill():
        lead = lax.broadcasted_iota(jnp.int32, (HALF, SEQ_TOK), 0) - (
            lax.broadcasted_iota(jnp.int32, (HALF, SEQ_TOK), 1) % HALF
        )
        for k in range(count):
            gap = (owner[count] - owner[k]) * HALF
            span = slice(k * HALF, (k + 1) * HALF)
            bias_early[span] = jnp.where(lead <= gap, 0.0, NEG)
            bias_late[span] = jnp.where(lead <= -gap, 0.0, NEG)


def attend_kernel(owner, query, keys, out, bias_early, bias_late):
    fill_bias(owner, bias_early, bias_late)
    early, late = key_parts(keys)
    for head in range(2):
        at = head * HEAD_DIM
        k_e, k_l = early[:, at : at + HEAD_DIM], late[:, at : at + HEAD_DIM]
        v_e, v_l = early[:, PAIR + at : PAIR + at + HEAD_DIM], late[:, PAIR + at : PAIR + at + HEAD_DIM]
        q_e, q_l = halves(query, head)
        (p_ee,) = weigh([nt(k_e, q_e) + bias_early[...]])
        p_el, p_ll = weigh([nt(k_e, q_l), nt(k_l, q_l) + bias_late[...]])
        o_e = tn(p_ee.astype(jnp.bfloat16), v_e)
        o_l = tn(p_el.astype(jnp.bfloat16), v_e) + tn(p_ll.astype(jnp.bfloat16), v_l)
        out[0, :, head * PAIR : (head + 1) * PAIR] = split_heads(o_e, o_l).astype(jnp.bfloat16)

def attend_back_kernel(
    owner, query, keys, grad, grad_query, grad_keys, bias_early, bias_late
):
    fill_bias(owner, bias_early, bias_late)
    early, late = key_parts(keys)
    scale = HEAD_DIM ** (-0.5)
    count = keys.shape[0]
    parts_e, parts_l = [], []
    for head in range(2):
        at = head * HEAD_DIM
        k_e, k_l = early[:, at : at + HEAD_DIM], late[:, at : at + HEAD_DIM]
        v_e, v_l = early[:, PAIR + at : PAIR + at + HEAD_DIM], late[:, PAIR + at : PAIR + at + HEAD_DIM]
        q_e, q_l = halves(query, head)
        d_e, d_l = halves(grad, head)
        (p_ee,) = weigh([nt(k_e, q_e) + bias_early[...]])
        p_el, p_ll = weigh([nt(k_e, q_l), nt(k_l, q_l) + bias_late[...]])
        g_ee, g_el, g_ll = nt(v_e, d_e), nt(v_e, d_l), nt(v_l, d_l)
        delta_e = jnp.sum(p_ee * g_ee, 0, keepdims=True)
        delta_l = jnp.sum(p_el * g_el, 0, keepdims=True) + jnp.sum(p_ll * g_ll, 0, keepdims=True)
        s_ee = (p_ee * (g_ee - delta_e)).astype(jnp.bfloat16)
        s_el = (p_el * (g_el - delta_l)).astype(jnp.bfloat16)
        s_ll = (p_ll * (g_ll - delta_l)).astype(jnp.bfloat16)
        gq_e = tn(s_ee, k_e) * scale
        gq_l = (tn(s_el, k_e) + tn(s_ll, k_l)) * scale
        grad_query[0, :, head * PAIR : (head + 1) * PAIR] = split_heads(gq_e, gq_l)
        gk_e = nn(s_ee, q_e) + nn(s_el, q_l)
        gk_l = nn(s_ll, q_l)
        gv_e = nn(p_ee.astype(jnp.bfloat16), d_e) + nn(p_el.astype(jnp.bfloat16), d_l)
        gv_l = nn(p_ll.astype(jnp.bfloat16), d_l)
        parts_e.append((gk_e, gv_e))
        parts_l.append((gk_l, gv_l))
    for parts, start in ((parts_e, 0), (parts_l, HALF)):
        for kind in range(2):
            joined = jnp.concatenate([parts[0][kind], parts[1][kind]], 1)
            grad_keys[:, start : start + HALF, kind * PAIR : (kind + 1) * PAIR] = (
                joined.astype(jnp.bfloat16).reshape(count, HALF, PAIR)
            )

def attend_specs(count):
    scalars = pl.BlockSpec(memory_space=pltpu.SMEM)
    rows = pl.BlockSpec((1, SEQ_TOK, 2 * PAIR), lambda s, j: (s, 0, j))
    keys = pl.BlockSpec((count, SEQ_TOK, 2 * PAIR), lambda s, j: (0, s, j))
    scratch = [pltpu.VMEM((count * HALF, SEQ_TOK), jnp.float32)] * 2
    return scalars, rows, keys, scratch


def attend(owner, query, keys):
    count = keys.shape[0]
    scalars, rows, key_rows, scratch = attend_specs(count)
    return pl.pallas_call(
        attend_kernel,
        out_shape=jax.ShapeDtypeStruct(query.shape, jnp.bfloat16),
        grid=(SEQ_GRP, KV_HEADS // 2),
        in_specs=[scalars, rows, key_rows],
        out_specs=rows,
        scratch_shapes=scratch,
        cost_estimate=pl.CostEstimate(
            flops=20 * query.size * count * SEQ_TOK,
            bytes_accessed=2 * keys.size + 4 * query.size,
            transcendentals=0,
        ),
    )(owner, query, keys)


def attend_back(owner, query, keys, grad):
    count = keys.shape[0]
    scalars, rows, key_rows, scratch = attend_specs(count)
    return pl.pallas_call(
        attend_back_kernel,
        out_shape=(
            jax.ShapeDtypeStruct(query.shape, jnp.float32),
            jax.ShapeDtypeStruct((count, SEQ_GRP * SEQ_TOK, keys.shape[2]), jnp.bfloat16),
        ),
        grid=(SEQ_GRP, KV_HEADS // 2),
        in_specs=[scalars, rows, key_rows, rows],
        out_specs=(rows, key_rows),
        scratch_shapes=scratch,
        cost_estimate=pl.CostEstimate(
            flops=30 * query.size * count * SEQ_TOK,
            bytes_accessed=4 * keys.size + 8 * query.size,
            transcendentals=0,
        ),
    )(owner, query, keys, grad)


STEP_BLOCKS = 16


def expert_kernel(
    arrived_ref,
    cot_ref,
    slot_gate_ref,
    gate_ref,
    up_ref,
    down_ref,
    produced_ref,
    back_ref,
    dots_ref,
    gate_grad_ref,
    up_grad_ref,
    down_grad_ref,
    *sums,
):
    rows = arrived_ref.shape[0] * MOST
    arrived = arrived_ref[:, 0].reshape(rows, D)
    cot = cot_ref[:, 0].reshape(rows, D)
    gate_w, up_w, down_w = gate_ref[0], up_ref[0], down_ref[0]
    gate_act = nn(arrived, gate_w)
    up_act = nn(arrived, up_w)
    sigma = jax.nn.sigmoid(gate_act)
    swish = gate_act * sigma
    hidden = (swish * up_act).astype(jnp.bfloat16)
    produced = nn(hidden, down_w).astype(jnp.bfloat16)
    produced_ref[:, 0] = produced.reshape(-1, MOST, D)
    wide = cot.astype(jnp.float32)
    dots = jnp.sum(produced.astype(jnp.float32) * wide, -1, keepdims=True)
    dots_ref[:, 0] = dots.reshape(-1, MOST, 1)
    grad_produced = (wide * slot_gate_ref[:, 0].reshape(rows, 1)).astype(jnp.bfloat16)
    grad_hidden = nt(grad_produced, down_w).astype(jnp.bfloat16).astype(jnp.float32)
    slope = sigma * (1.0 + gate_act * (1.0 - sigma))
    grad_gate = (grad_hidden * up_act * slope).astype(jnp.bfloat16)
    grad_up = (grad_hidden * swish).astype(jnp.bfloat16)
    back = nt(grad_gate, gate_w) + nt(grad_up, up_w)
    back_ref[:, 0] = back.astype(jnp.bfloat16).reshape(-1, MOST, D)
    grads = [tn(arrived, grad_gate), tn(arrived, grad_up), tn(hidden, grad_produced)]
    if sums:
        first = pl.program_id(1) == 0
        for held, grad in zip(sums, grads):
            held[...] = jnp.where(first, grad, held[...] + grad)
        grads = [held[...] for held in sums]
    quarter = gate_w.shape[1] // 4
    for k in range(4):
        span = slice(k * quarter, (k + 1) * quarter)
        gate_grad_ref[k, 0] = grads[0][:, span].astype(jnp.bfloat16)
        up_grad_ref[k, 0] = grads[1][:, span].astype(jnp.bfloat16)
        down_grad_ref[k, 0] = grads[2][span].astype(jnp.bfloat16)


def experts_pass(arrived, cot, slot_gates, gate_w, up_w, down_w):
    blocks, mine = arrived.shape[:2]
    steps = blocks // STEP_BLOCKS
    hidden = gate_w.shape[2]
    quarter = hidden // 4

    def slot_rows(width):
        return pl.BlockSpec((STEP_BLOCKS, 1, MOST, width), lambda e, c: (c, e, 0, 0))

    def per_expert(*shape):
        return pl.BlockSpec((1,) + shape, lambda e, c: (e, 0, 0))

    def pieces(*shape):
        return pl.BlockSpec((4, 1) + shape, lambda e, c: (0, e, 0, 0))

    low = jnp.bfloat16
    return pl.pallas_call(
        expert_kernel,
        grid=(mine, steps),
        in_specs=[
            slot_rows(D),
            slot_rows(D),
            slot_rows(1),
            per_expert(D, hidden),
            per_expert(D, hidden),
            per_expert(hidden, D),
        ],
        out_specs=(
            slot_rows(D),
            slot_rows(D),
            slot_rows(1),
            pieces(D, quarter),
            pieces(D, quarter),
            pieces(quarter, D),
        ),
        out_shape=(
            jax.ShapeDtypeStruct(arrived.shape, low),
            jax.ShapeDtypeStruct(arrived.shape, low),
            jax.ShapeDtypeStruct(slot_gates.shape, jnp.float32),
            jax.ShapeDtypeStruct((4, mine, D, quarter), low),
            jax.ShapeDtypeStruct((4, mine, D, quarter), low),
            jax.ShapeDtypeStruct((4, mine, quarter, D), low),
        ),
        scratch_shapes=[]
        if steps == 1
        else [
            pltpu.VMEM((D, hidden), jnp.float32),
            pltpu.VMEM((D, hidden), jnp.float32),
            pltpu.VMEM((hidden, D), jnp.float32),
        ],
        compiler_params=pltpu.CompilerParams(vmem_limit_bytes=63 * 1024 * 1024),
        cost_estimate=pl.CostEstimate(
            flops=18 * arrived.size * hidden,
            bytes_accessed=8 * arrived.size + 12 * mine * D * hidden,
            transcendentals=0,
        ),
    )(arrived, cot, slot_gates, gate_w, up_w, down_w)


def shards(
    tokens,
    routes,
    in_weight,
    out_weight,
    first_gain,
    second_gain,
    router_weight,
    gate_weight,
    up_weight,
    down_weight,
    cotangent,
):
    ctx_count = lax.axis_size("ctx")
    length = SEQ_TOK * ctx_count
    rows = SEQ_GRP * SEQ_TOK
    width_q = HEADS * HEAD_DIM
    width_k = KV_HEADS * HEAD_DIM
    my_index = lax.axis_index("ctx")
    order = ring_order(ctx_count)
    table = [
        [order[(order.index(c) - k) % ctx_count] for k in range(ctx_count)] + [c]
        for c in range(ctx_count)
    ]
    owner = lax.dynamic_index_in_dim(jnp.array(table, jnp.int32), my_index, 0, False)
    local_place = dealt(my_index * SEQ_TOK + jnp.arange(SEQ_TOK, dtype=jnp.int32), length)
    upstream = cotangent.reshape(rows, D)
    chosen = jnp.any(
        routes.reshape(rows, TOP).T[:, None, :] == jnp.arange(EXPERTS, dtype=jnp.int32)[:, None], 0
    )
    gate_full, up_full, down_full = (
        lax.all_gather(gate_weight, "wsh", axis=2, tiled=True),
        lax.all_gather(up_weight, "wsh", axis=2, tiled=True),
        lax.all_gather(down_weight, "wsh", axis=1, tiled=True),
    )
    inputs = tokens.astype(jnp.float32).reshape(rows, D)
    scale_one = lax.rsqrt(jnp.mean(inputs * inputs, -1, keepdims=True) + EPS)
    normed = (inputs * scale_one * first_gain).astype(jnp.bfloat16)
    mixed = jnp.dot(normed, in_weight, preferred_element_type=jnp.float32).reshape(
        SEQ_GRP, SEQ_TOK, -1
    )
    query = rotate(
        mixed[..., :width_q].reshape(SEQ_GRP, SEQ_TOK, HEADS, HEAD_DIM), local_place, 1.0
    ).astype(jnp.bfloat16)
    query = (query * jnp.bfloat16(HEAD_DIM ** (-0.5))).reshape(SEQ_GRP, SEQ_TOK, width_q)
    key = rotate(
        mixed[..., width_q : width_q + width_k].reshape(SEQ_GRP, SEQ_TOK, KV_HEADS, HEAD_DIM),
        local_place,
        1.0,
    ).astype(jnp.bfloat16)
    value = mixed[..., width_q + width_k :].astype(jnp.bfloat16)
    pairs = (SEQ_GRP, SEQ_TOK, KV_HEADS // 2, PAIR)
    key_value = jnp.concatenate([key.reshape(pairs), value.reshape(pairs)], -1).reshape(
        rows, 2 * width_k
    )
    flags = chosen.astype(jnp.bfloat16).reshape(-1, 2 * width_k)
    flag_rows = flags.shape[0]
    flags = jnp.concatenate([flags, jnp.zeros_like(flags)], 0)
    whole = jnp.stack(
        [held[0] for held in ring_gather([jnp.concatenate([key_value, flags], 0)])]
    )
    whole, cot_own = lax.optimization_barrier((whole, upstream))
    cot_ring = ring_gather([cot_own])
    attended = attend(owner, query, whole).reshape(rows, width_q)
    resid = inputs + jnp.dot(attended, out_weight, preferred_element_type=jnp.float32)
    scale_two = lax.rsqrt(jnp.mean(resid * resid, -1, keepdims=True) + EPS)
    normed_two = (resid * scale_two * second_gain).astype(jnp.bfloat16)
    blocks = SEQ_GRP * ctx_count
    mine = gate_weight.shape[0]
    chosen_all = whole[:, rows : rows + flag_rows].reshape(ctx_count, EXPERTS, rows)
    chosen_my = lax.dynamic_slice_in_dim(chosen_all, my_index * mine, mine, 1)

    def by_block(values):
        split = values.reshape(ctx_count, mine, SEQ_GRP, SEQ_TOK)
        return jnp.swapaxes(split, 1, 2).reshape(blocks, mine, SEQ_TOK)

    chosen_my = by_block(chosen_my)
    before = (
        jnp.arange(SEQ_TOK, dtype=jnp.int32)[:, None] < jnp.arange(SEQ_TOK, dtype=jnp.int32)[None, :]
    ).astype(jnp.bfloat16)
    ranks = jnp.dot(
        chosen_my.reshape(blocks * mine, SEQ_TOK), before, preferred_element_type=jnp.float32
    ).reshape(blocks, mine, SEQ_TOK)
    ranks = jnp.where(chosen_my > 0, ranks, -1.0)
    normed_all = jnp.concatenate([held[0] for held in ring_gather([normed_two])])
    cot_all = jnp.concatenate([held[0] for held in cot_ring])
    logits = lax.dot_general(
        router_weight, normed_all, (((0,), (1,)), ((), ())), preferred_element_type=jnp.float32
    )
    taken = jnp.swapaxes(chosen_all, 0, 1).reshape(EXPERTS, blocks * SEQ_TOK) > 0
    picked = jnp.where(taken, logits, NEG)
    weights = jnp.where(taken, jnp.exp(picked - jnp.max(picked, 0, keepdims=True)), 0.0)
    gates_all = weights / jnp.sum(weights, 0, keepdims=True)
    gates = gates_all[:, :rows]
    gates_my = lax.dynamic_slice_in_dim(gates_all, my_index * mine, mine, 0)
    gates_my = by_block(jnp.swapaxes(gates_my.reshape(mine, ctx_count, rows), 0, 1))
    slot_ids = jnp.arange(MOST, dtype=jnp.int32).astype(jnp.float32)
    match = ranks[:, :, None, :] == slot_ids[:, None]
    chances = jnp.where(match, gates_my[:, :, None, :], 0.0)
    dispatch = match.astype(jnp.bfloat16).reshape(blocks, mine * MOST, SEQ_TOK)
    combine = chances.astype(jnp.bfloat16).reshape(blocks, mine * MOST, SEQ_TOK)
    slot_gates = jnp.sum(chances, -1, keepdims=True).astype(jnp.bfloat16).astype(jnp.float32)
    normed_blocks = normed_all.reshape(blocks, SEQ_TOK, D)
    cot_blocks = cot_all.reshape(blocks, SEQ_TOK, D)
    slot_shape = (blocks, mine, MOST, D)
    arrived, cot_slots = (
        jnp.einsum("bst,btd->bsd", dispatch, one, preferred_element_type=jnp.float32)
        .astype(jnp.bfloat16)
        .reshape(slot_shape)
        for one in (normed_blocks, cot_blocks)
    )
    produced, grad_arrived, slot_dots, gate_local, up_local, down_local = experts_pass(
        arrived, cot_slots, slot_gates, gate_full, up_full, down_full
    )
    gate_dots = jnp.sum(jnp.where(match, slot_dots, 0.0), 2)
    gate_dots = jnp.swapaxes(gate_dots.reshape(ctx_count, SEQ_GRP, mine, SEQ_TOK), 1, 2)
    ours = jnp.arange(EXPERTS, dtype=jnp.int32)[:, None] // mine == my_index
    gate_dots = jnp.where(
        ours, jnp.tile(gate_dots.reshape(ctx_count, mine, rows), (1, EXPERTS // mine, 1)), 0.0
    ).reshape(ctx_count, flag_rows, D)
    coarse = lax.reduce_precision(gate_dots, 8, 7)

    def to_tokens(matrix, slot_values):
        return jnp.einsum(
            "bst,bsd->btd",
            matrix,
            slot_values.reshape(blocks, mine * MOST, D),
            preferred_element_type=jnp.float32,
        ).astype(jnp.bfloat16).reshape(ctx_count, rows, D)

    sent_part = jnp.concatenate(
        [
            to_tokens(dispatch, grad_arrived),
            coarse.astype(jnp.bfloat16),
            (gate_dots - coarse).astype(jnp.bfloat16),
        ],
        1,
    )
    grad_sent = ring_sum(lambda k, p: sent_part[k], 1)[0]
    grad_gates = (
        grad_sent[rows : rows + flag_rows] + grad_sent[rows + flag_rows :]
    ).reshape(EXPERTS, rows)
    grad_sent, mixed_part = lax.optimization_barrier(
        (grad_sent[:rows], to_tokens(combine, produced))
    )
    mixture = ring_sum(lambda k, p: mixed_part[k], 1)[0]
    layer_out = (resid + mixture).astype(jnp.bfloat16).reshape(SEQ_GRP, SEQ_TOK, D)
    gate_grad, up_grad, down_grad = (
        lax.psum_scatter(local, "wsh", scatter_dimension=0).astype(jnp.float32)
        for local in (gate_local, up_local, down_local)
    )
    grad_logits = (gates * (grad_gates - jnp.sum(gates * grad_gates, 0, keepdims=True))).astype(
        jnp.bfloat16
    )
    router_local = lax.dot_general(
        normed_two, grad_logits, (((0,), (1,)), ((), ())), preferred_element_type=jnp.float32
    )
    grad_normed_two = grad_sent + lax.dot_general(
        grad_logits, router_weight, (((0,), (1,)), ((), ())), preferred_element_type=jnp.float32
    )
    grad_resid_norm, second_local = norm_back(resid, scale_two, second_gain, grad_normed_two)
    grad_resid = upstream.astype(jnp.float32) + grad_resid_norm
    grad_branch = grad_resid.astype(jnp.bfloat16)
    out_local = lax.dot_general(
        attended, grad_branch, (((0,), (0,)), ((), ())), preferred_element_type=jnp.float32
    )
    grad_attended = lax.dot_general(
        grad_branch, out_weight, (((1,), (1,)), ((), ())), preferred_element_type=jnp.float32
    ).astype(jnp.bfloat16)
    grad_query, grad_whole = attend_back(
        owner,
        query,
        whole,
        grad_attended.reshape(SEQ_GRP, SEQ_TOK, width_q),
    )
    kv_grad = ring_sum(lambda k, p: grad_whole[k], 1)[0].reshape(
        SEQ_GRP, SEQ_TOK, KV_HEADS // 2, 2, PAIR
    )
    grad_query = rotate(grad_query.reshape(SEQ_GRP, SEQ_TOK, HEADS, HEAD_DIM), local_place, -1.0)
    grad_query = grad_query.astype(jnp.bfloat16).reshape(rows, width_q)
    grad_key = rotate(
        kv_grad[:, :, :, 0].reshape(SEQ_GRP, SEQ_TOK, KV_HEADS, HEAD_DIM), local_place, -1.0
    )
    grad_pair = jnp.concatenate(
        [grad_key.reshape(rows, width_k), kv_grad[:, :, :, 1].reshape(rows, width_k)], -1
    ).astype(jnp.bfloat16)
    in_first = lax.dot_general(
        normed, grad_query, (((0,), (0,)), ((), ())), preferred_element_type=jnp.float32
    )
    in_second = lax.dot_general(
        normed, grad_pair, (((0,), (0,)), ((), ())), preferred_element_type=jnp.float32
    )
    grad_normed = lax.dot_general(
        grad_query, in_weight[:, :width_q], (((1,), (1,)), ((), ())), preferred_element_type=jnp.float32
    ) + lax.dot_general(
        grad_pair, in_weight[:, width_q:], (((1,), (1,)), ((), ())), preferred_element_type=jnp.float32
    )
    grad_inputs_norm, first_local = norm_back(inputs, scale_one, first_gain, grad_normed)
    tokens_grad = (grad_resid + grad_inputs_norm).astype(jnp.bfloat16).reshape(SEQ_GRP, SEQ_TOK, D)
    low = jnp.bfloat16
    early = spread(
        jnp.concatenate(
            [
                in_first.astype(low),
                out_local.astype(low),
                router_local.astype(low),
                second_local[:, None].astype(low),
                jnp.zeros((D, SEQ_TOK - EXPERTS - 1), low),
            ],
            -1,
        ),
        owner,
    )
    in_second = spread(
        jnp.concatenate(
            [in_second, jnp.broadcast_to(first_local[:, None], (D, SEQ_TOK))], -1
        ).astype(jnp.bfloat16),
        owner,
    )
    in_grad = jnp.concatenate([early[:, :width_q], in_second[:, : 2 * width_k]], -1)
    first_gain_grad = in_second[:, 2 * width_k]
    out_grad = early[:, width_q : width_q + D]
    small = early[:, width_q + D :]
    router_grad = small[:, :EXPERTS]
    second_gain_grad = small[:, EXPERTS]
    return (
        layer_out,
        tokens_grad,
        in_grad,
        out_grad,
        first_gain_grad,
        second_gain_grad,
        router_grad,
        gate_grad,
        up_grad,
        down_grad,
    )


def solution(mesh):
    placed = (
        P("wsh", "ctx", None),
        P("wsh", "ctx", None),
        P(),
        P(),
        P(),
        P(),
        P(),
        P("ctx", None, "wsh"),
        P("ctx", None, "wsh"),
        P("ctx", "wsh", None),
        P("wsh", "ctx", None),
    )
    return jax.shard_map(
        shards,
        mesh=mesh,
        in_specs=placed,
        out_specs=(
            P("wsh", "ctx", None),
            P("wsh", "ctx", None),
            P(("ctx", "wsh"), None),
            P(("ctx", "wsh"), None),
            P(("ctx", "wsh")),
            P(("ctx", "wsh")),
            P(("ctx", "wsh"), None),
            P("ctx", None, "wsh"),
            P("ctx", None, "wsh"),
            P("ctx", "wsh", None),
        ),
        check_vma=False,
    )
```

```python
import jax
import jax.numpy as jnp
from jax import lax
from jax.experimental import pallas as pl
from jax.experimental.pallas import tpu as pltpu
from jax.sharding import PartitionSpec as P

D = 1024
HEADS = 16
KV_HEADS = 8
HEAD_DIM = 64
EXPERTS = 32
TOP = 8
SEQ_TOK = 128
SEQ_GRP = 2
HALF = 64
MOST = 48


EPS = 1e-05
THETA = 10000.0
NEG = -1e30


def dealt(rows, length):
    owner = rows // SEQ_TOK
    offset = rows % SEQ_TOK
    early = owner * HALF + offset
    late = length - (owner + 1) * HALF + offset - HALF
    return jnp.where(offset < HALF, early, late)


def rotate(values, place, sign):
    half_dim = values.shape[-1] // 2
    freq = THETA ** (-2.0 * jnp.arange(half_dim, dtype=jnp.float32) / values.shape[-1])
    angle = place.astype(jnp.float32)[:, None] * freq[None, :]
    cosine = jnp.cos(angle)[:, None, :]
    sine = sign * jnp.sin(angle)[:, None, :]
    front = values[..., :half_dim]
    back = values[..., half_dim:]
    return jnp.concatenate([front * cosine - back * sine, back * cosine + front * sine], -1)


def norm_back(values, scale, gain, grad_out):
    weighted = grad_out * gain
    grad_in = scale * weighted - values * scale**3 * jnp.mean(weighted * values, -1, keepdims=True)
    return (grad_in, jnp.sum(grad_out * values * scale, 0))


def ring_order(count):
    return list(range(0, count, 2)) + list(reversed(range(1, count, 2)))


def ring_shift(count, step):
    order = ring_order(count)
    return [(order[i], order[(i + step) % count]) for i in range(count)]


def ring_gather(parts):
    count = lax.axis_size("ctx")
    ahead, behind = ring_shift(count, 1), ring_shift(count, -1)
    held = [list(parts)] + [[None] * len(parts) for _ in range(count - 1)]
    far = count // 2
    for p, part in enumerate(parts):
        up, down = part, part
        ups = far if p % 2 == 0 else count - 1 - far
        for step in range(1, far + 1):
            if step <= ups:
                up = lax.ppermute(up, "ctx", ahead)
                held[step][p] = up
            if step <= count - 1 - ups:
                down = lax.ppermute(down, "ctx", behind)
                held[count - step][p] = down
    return held


def add_low(left, right):
    return (left.astype(jnp.float32) + right.astype(jnp.float32)).astype(left.dtype)


def ring_sum(block, parts):
    count = lax.axis_size("ctx")
    ahead, behind = ring_shift(count, 1), ring_shift(count, -1)
    far = count // 2
    sums = []
    for p in range(parts):
        ups = far if p % 2 == 0 else count - 1 - far
        downs = count - 1 - ups
        up = block(count - ups, p)
        for step in range(ups - 1, 0, -1):
            up = add_low(lax.ppermute(up, "ctx", ahead), block(count - step, p))
        up = lax.ppermute(up, "ctx", ahead)
        down = block(downs, p)
        for step in range(downs - 1, 0, -1):
            down = add_low(lax.ppermute(down, "ctx", behind), block(step, p))
        down = lax.ppermute(down, "ctx", behind)
        own = block(0, p).astype(jnp.float32)
        sums.append(up.astype(jnp.float32) + down.astype(jnp.float32) + own)
    return sums


def spread(local):
    for axis in ("wsh", "ctx"):
        count = lax.axis_size(axis)
        me = lax.axis_index(axis)
        outer = lax.axis_size("ctx") if axis == "wsh" else 1
        bit = 1
        while bit < count:
            split = local.reshape(outer * (count // (2 * bit)), 2, -1, local.shape[-1])
            mine = (me // bit) % 2
            swap = [(i, i ^ bit) for i in range(count)]
            sent = lax.ppermute(lax.dynamic_index_in_dim(split, 1 - mine, 1, False), axis, swap)
            kept = lax.dynamic_index_in_dim(split, mine, 1, False)
            local = add_low(kept, sent).reshape(-1, local.shape[-1])
            bit *= 2
    return local.astype(jnp.float32)


PAIR = 2 * HEAD_DIM
def nt(left, right):
    return lax.dot_general(left, right, (((1,), (1,)), ((), ())), preferred_element_type=jnp.float32)
def tn(left, right):
    return lax.dot_general(left, right, (((0,), (0,)), ((), ())), preferred_element_type=jnp.float32)
def nn(left, right):
    return jnp.dot(left, right, preferred_element_type=jnp.float32)

def halves(ref, head):
    start = head * PAIR
    block = ref[0, :, start : start + PAIR]
    both = [block[:, :HEAD_DIM], block[:, HEAD_DIM:]]
    return (
        jnp.concatenate([one[:HALF] for one in both], 0),
        jnp.concatenate([one[HALF:] for one in both], 0),
    )

def key_parts(ref):
    whole = ref[...]
    count = whole.shape[0]
    early = whole[:, :HALF].reshape(count * HALF, -1)
    late = whole[:, HALF:].reshape(count * HALF, -1)
    return early, late

def weigh(scores):
    peak = jnp.max(scores[0], 0, keepdims=True)
    for more in scores[1:]:
        peak = jnp.maximum(peak, jnp.max(more, 0, keepdims=True))
    powers = [jnp.exp(part - peak) for part in scores]
    total = sum(jnp.sum(part, 0, keepdims=True) for part in powers)
    inverse = 1.0 / total
    return [part * inverse for part in powers]

def split_heads(stacked_early, stacked_late):
    return jnp.concatenate(
        [
            jnp.concatenate([stacked_early[:HALF], stacked_early[HALF:]], 1),
            jnp.concatenate([stacked_late[:HALF], stacked_late[HALF:]], 1),
        ],
        0,
    )

def fill_bias(owner, bias_early, bias_late):
    count = owner.shape[0] - 1

    @pl.when((pl.program_id(0) == 0) & (pl.program_id(1) == 0))
    def fill():
        lead = lax.broadcasted_iota(jnp.int32, (HALF, SEQ_TOK), 0) - (
            lax.broadcasted_iota(jnp.int32, (HALF, SEQ_TOK), 1) % HALF
        )
        for k in range(count):
            gap = (owner[count] - owner[k]) * HALF
            span = slice(k * HALF, (k + 1) * HALF)
            bias_early[span] = jnp.where(lead <= gap, 0.0, NEG)
            bias_late[span] = jnp.where(lead <= -gap, 0.0, NEG)


def attend_kernel(owner, query, keys, out, bias_early, bias_late):
    fill_bias(owner, bias_early, bias_late)
    early, late = key_parts(keys)
    for head in range(2):
        at = head * HEAD_DIM
        k_e, k_l = early[:, at : at + HEAD_DIM], late[:, at : at + HEAD_DIM]
        v_e, v_l = early[:, PAIR + at : PAIR + at + HEAD_DIM], late[:, PAIR + at : PAIR + at + HEAD_DIM]
        q_e, q_l = halves(query, head)
        (p_ee,) = weigh([nt(k_e, q_e) + bias_early[...]])
        p_el, p_ll = weigh([nt(k_e, q_l), nt(k_l, q_l) + bias_late[...]])
        o_e = tn(p_ee.astype(jnp.bfloat16), v_e)
        o_l = tn(p_el.astype(jnp.bfloat16), v_e) + tn(p_ll.astype(jnp.bfloat16), v_l)
        out[0, :, head * PAIR : (head + 1) * PAIR] = split_heads(o_e, o_l).astype(jnp.bfloat16)

def attend_back_kernel(
    owner, query, keys, grad, grad_query, grad_keys, bias_early, bias_late
):
    fill_bias(owner, bias_early, bias_late)
    early, late = key_parts(keys)
    scale = HEAD_DIM ** (-0.5)
    count = keys.shape[0]
    parts_e, parts_l = [], []
    for head in range(2):
        at = head * HEAD_DIM
        k_e, k_l = early[:, at : at + HEAD_DIM], late[:, at : at + HEAD_DIM]
        v_e, v_l = early[:, PAIR + at : PAIR + at + HEAD_DIM], late[:, PAIR + at : PAIR + at + HEAD_DIM]
        q_e, q_l = halves(query, head)
        d_e, d_l = halves(grad, head)
        (p_ee,) = weigh([nt(k_e, q_e) + bias_early[...]])
        p_el, p_ll = weigh([nt(k_e, q_l), nt(k_l, q_l) + bias_late[...]])
        g_ee, g_el, g_ll = nt(v_e, d_e), nt(v_e, d_l), nt(v_l, d_l)
        delta_e = jnp.sum(p_ee * g_ee, 0, keepdims=True)
        delta_l = jnp.sum(p_el * g_el, 0, keepdims=True) + jnp.sum(p_ll * g_ll, 0, keepdims=True)
        s_ee = (p_ee * (g_ee - delta_e)).astype(jnp.bfloat16)
        s_el = (p_el * (g_el - delta_l)).astype(jnp.bfloat16)
        s_ll = (p_ll * (g_ll - delta_l)).astype(jnp.bfloat16)
        gq_e = tn(s_ee, k_e) * scale
        gq_l = (tn(s_el, k_e) + tn(s_ll, k_l)) * scale
        grad_query[0, :, head * PAIR : (head + 1) * PAIR] = split_heads(gq_e, gq_l)
        gk_e = nn(s_ee, q_e) + nn(s_el, q_l)
        gk_l = nn(s_ll, q_l)
        gv_e = nn(p_ee.astype(jnp.bfloat16), d_e) + nn(p_el.astype(jnp.bfloat16), d_l)
        gv_l = nn(p_ll.astype(jnp.bfloat16), d_l)
        parts_e.append((gk_e, gv_e))
        parts_l.append((gk_l, gv_l))
    for parts, start in ((parts_e, 0), (parts_l, HALF)):
        for kind in range(2):
            joined = jnp.concatenate([parts[0][kind], parts[1][kind]], 1)
            grad_keys[:, start : start + HALF, kind * PAIR : (kind + 1) * PAIR] = (
                joined.astype(jnp.bfloat16).reshape(count, HALF, PAIR)
            )

def attend_specs(count):
    scalars = pl.BlockSpec(memory_space=pltpu.SMEM)
    rows = pl.BlockSpec((1, SEQ_TOK, 2 * PAIR), lambda s, j: (s, 0, j))
    keys = pl.BlockSpec((count, SEQ_TOK, 2 * PAIR), lambda s, j: (0, s, j))
    scratch = [pltpu.VMEM((count * HALF, SEQ_TOK), jnp.float32)] * 2
    return scalars, rows, keys, scratch


def attend(owner, query, keys):
    count = keys.shape[0]
    scalars, rows, key_rows, scratch = attend_specs(count)
    return pl.pallas_call(
        attend_kernel,
        out_shape=jax.ShapeDtypeStruct(query.shape, jnp.bfloat16),
        grid=(SEQ_GRP, KV_HEADS // 2),
        in_specs=[scalars, rows, key_rows],
        out_specs=rows,
        scratch_shapes=scratch,
        cost_estimate=pl.CostEstimate(
            flops=20 * query.size * count * SEQ_TOK,
            bytes_accessed=2 * keys.size + 4 * query.size,
            transcendentals=0,
        ),
    )(owner, query, keys)


def attend_back(owner, query, keys, grad):
    count = keys.shape[0]
    scalars, rows, key_rows, scratch = attend_specs(count)
    return pl.pallas_call(
        attend_back_kernel,
        out_shape=(
            jax.ShapeDtypeStruct(query.shape, jnp.float32),
            jax.ShapeDtypeStruct((count, SEQ_GRP * SEQ_TOK, keys.shape[2]), jnp.bfloat16),
        ),
        grid=(SEQ_GRP, KV_HEADS // 2),
        in_specs=[scalars, rows, key_rows, rows],
        out_specs=(rows, key_rows),
        scratch_shapes=scratch,
        cost_estimate=pl.CostEstimate(
            flops=30 * query.size * count * SEQ_TOK,
            bytes_accessed=4 * keys.size + 8 * query.size,
            transcendentals=0,
        ),
    )(owner, query, keys, grad)


STEP_BLOCKS = 16


def expert_kernel(
    arrived_ref,
    cot_ref,
    slot_gate_ref,
    gate_ref,
    up_ref,
    down_ref,
    produced_ref,
    back_ref,
    dots_ref,
    gate_grad_ref,
    up_grad_ref,
    down_grad_ref,
    *sums,
):
    rows = arrived_ref.shape[0] * MOST
    arrived = arrived_ref[:, 0].reshape(rows, D)
    cot = cot_ref[:, 0].reshape(rows, D)
    gate_w, up_w, down_w = gate_ref[0], up_ref[0], down_ref[0]
    gate_act = nn(arrived, gate_w)
    up_act = nn(arrived, up_w)
    sigma = jax.nn.sigmoid(gate_act)
    swish = gate_act * sigma
    hidden = (swish * up_act).astype(jnp.bfloat16)
    produced = nn(hidden, down_w).astype(jnp.bfloat16)
    produced_ref[:, 0] = produced.reshape(-1, MOST, D)
    wide = cot.astype(jnp.float32)
    dots = jnp.sum(produced.astype(jnp.float32) * wide, -1, keepdims=True)
    dots_ref[:, 0] = dots.reshape(-1, MOST, 1)
    grad_produced = (wide * slot_gate_ref[:, 0].reshape(rows, 1)).astype(jnp.bfloat16)
    grad_hidden = nt(grad_produced, down_w).astype(jnp.bfloat16).astype(jnp.float32)
    slope = sigma * (1.0 + gate_act * (1.0 - sigma))
    grad_gate = (grad_hidden * up_act * slope).astype(jnp.bfloat16)
    grad_up = (grad_hidden * swish).astype(jnp.bfloat16)
    back = nt(grad_gate, gate_w) + nt(grad_up, up_w)
    back_ref[:, 0] = back.astype(jnp.bfloat16).reshape(-1, MOST, D)
    grads = [tn(arrived, grad_gate), tn(arrived, grad_up), tn(hidden, grad_produced)]
    if sums:
        first = pl.program_id(1) == 0
        for held, grad in zip(sums, grads):
            held[...] = jnp.where(first, grad, held[...] + grad)
        grads = [held[...] for held in sums]
    quarter = gate_w.shape[1] // 4
    for k in range(4):
        span = slice(k * quarter, (k + 1) * quarter)
        gate_grad_ref[k, 0] = grads[0][:, span].astype(jnp.bfloat16)
        up_grad_ref[k, 0] = grads[1][:, span].astype(jnp.bfloat16)
        down_grad_ref[k, 0] = grads[2][span].astype(jnp.bfloat16)


def experts_pass(arrived, cot, slot_gates, gate_w, up_w, down_w):
    blocks, mine = arrived.shape[:2]
    steps = blocks // STEP_BLOCKS
    hidden = gate_w.shape[2]
    quarter = hidden // 4

    def slot_rows(width):
        return pl.BlockSpec((STEP_BLOCKS, 1, MOST, width), lambda e, c: (c, e, 0, 0))

    def per_expert(*shape):
        return pl.BlockSpec((1,) + shape, lambda e, c: (e, 0, 0))

    def pieces(*shape):
        return pl.BlockSpec((4, 1) + shape, lambda e, c: (0, e, 0, 0))

    low = jnp.bfloat16
    return pl.pallas_call(
        expert_kernel,
        grid=(mine, steps),
        in_specs=[
            slot_rows(D),
            slot_rows(D),
            slot_rows(1),
            per_expert(D, hidden),
            per_expert(D, hidden),
            per_expert(hidden, D),
        ],
        out_specs=(
            slot_rows(D),
            slot_rows(D),
            slot_rows(1),
            pieces(D, quarter),
            pieces(D, quarter),
            pieces(quarter, D),
        ),
        out_shape=(
            jax.ShapeDtypeStruct(arrived.shape, low),
            jax.ShapeDtypeStruct(arrived.shape, low),
            jax.ShapeDtypeStruct(slot_gates.shape, jnp.float32),
            jax.ShapeDtypeStruct((4, mine, D, quarter), low),
            jax.ShapeDtypeStruct((4, mine, D, quarter), low),
            jax.ShapeDtypeStruct((4, mine, quarter, D), low),
        ),
        scratch_shapes=[]
        if steps == 1
        else [
            pltpu.VMEM((D, hidden), jnp.float32),
            pltpu.VMEM((D, hidden), jnp.float32),
            pltpu.VMEM((hidden, D), jnp.float32),
        ],
        compiler_params=pltpu.CompilerParams(vmem_limit_bytes=63 * 1024 * 1024),
        cost_estimate=pl.CostEstimate(
            flops=18 * arrived.size * hidden,
            bytes_accessed=8 * arrived.size + 12 * mine * D * hidden,
            transcendentals=0,
        ),
    )(arrived, cot, slot_gates, gate_w, up_w, down_w)


def shards(
    tokens,
    routes,
    in_weight,
    out_weight,
    first_gain,
    second_gain,
    router_weight,
    gate_weight,
    up_weight,
    down_weight,
    cotangent,
):
    ctx_count = lax.axis_size("ctx")
    length = SEQ_TOK * ctx_count
    rows = SEQ_GRP * SEQ_TOK
    width_q = HEADS * HEAD_DIM
    width_k = KV_HEADS * HEAD_DIM
    my_index = lax.axis_index("ctx")
    order = ring_order(ctx_count)
    table = [
        [order[(order.index(c) - k) % ctx_count] for k in range(ctx_count)] + [c]
        for c in range(ctx_count)
    ]
    owner = lax.dynamic_index_in_dim(jnp.array(table, jnp.int32), my_index, 0, False)
    local_place = dealt(my_index * SEQ_TOK + jnp.arange(SEQ_TOK, dtype=jnp.int32), length)
    upstream = cotangent.reshape(rows, D)
    chosen = jnp.any(
        routes.reshape(rows, TOP).T[:, None, :] == jnp.arange(EXPERTS, dtype=jnp.int32)[:, None], 0
    )
    gate_full, up_full, down_full = (
        lax.all_gather(gate_weight, "wsh", axis=2, tiled=True),
        lax.all_gather(up_weight, "wsh", axis=2, tiled=True),
        lax.all_gather(down_weight, "wsh", axis=1, tiled=True),
    )
    inputs = tokens.astype(jnp.float32).reshape(rows, D)
    scale_one = lax.rsqrt(jnp.mean(inputs * inputs, -1, keepdims=True) + EPS)
    normed = (inputs * scale_one * first_gain).astype(jnp.bfloat16)
    mixed = jnp.dot(normed, in_weight, preferred_element_type=jnp.float32).reshape(
        SEQ_GRP, SEQ_TOK, -1
    )
    query = rotate(
        mixed[..., :width_q].reshape(SEQ_GRP, SEQ_TOK, HEADS, HEAD_DIM), local_place, 1.0
    ).astype(jnp.bfloat16)
    query = (query * jnp.bfloat16(HEAD_DIM ** (-0.5))).reshape(SEQ_GRP, SEQ_TOK, width_q)
    key = rotate(
        mixed[..., width_q : width_q + width_k].reshape(SEQ_GRP, SEQ_TOK, KV_HEADS, HEAD_DIM),
        local_place,
        1.0,
    ).astype(jnp.bfloat16)
    value = mixed[..., width_q + width_k :].astype(jnp.bfloat16)
    pairs = (SEQ_GRP, SEQ_TOK, KV_HEADS // 2, PAIR)
    key_value = jnp.concatenate([key.reshape(pairs), value.reshape(pairs)], -1).reshape(
        rows, 2 * width_k
    )
    flags = chosen.astype(jnp.bfloat16).reshape(-1, 2 * width_k)
    flag_rows = flags.shape[0]
    flags = jnp.concatenate([flags, jnp.zeros_like(flags)], 0)
    whole = jnp.stack(
        [held[0] for held in ring_gather([jnp.concatenate([key_value, flags], 0)])]
    )
    whole, cot_own = lax.optimization_barrier((whole, upstream))
    cot_ring = ring_gather([cot_own])
    attended = attend(owner, query, whole).reshape(rows, width_q)
    resid = inputs + jnp.dot(attended, out_weight, preferred_element_type=jnp.float32)
    scale_two = lax.rsqrt(jnp.mean(resid * resid, -1, keepdims=True) + EPS)
    normed_two = (resid * scale_two * second_gain).astype(jnp.bfloat16)
    blocks = SEQ_GRP * ctx_count
    mine = gate_weight.shape[0]
    chosen_all = whole[:, rows : rows + flag_rows].reshape(ctx_count, EXPERTS, rows)
    chosen_my = lax.dynamic_slice_in_dim(chosen_all, my_index * mine, mine, 1)

    def by_block(values):
        split = values.reshape(ctx_count, mine, SEQ_GRP, SEQ_TOK)
        return jnp.swapaxes(split, 1, 2).reshape(blocks, mine, SEQ_TOK)

    chosen_my = by_block(chosen_my)
    before = (
        jnp.arange(SEQ_TOK, dtype=jnp.int32)[:, None] < jnp.arange(SEQ_TOK, dtype=jnp.int32)[None, :]
    ).astype(jnp.bfloat16)
    ranks = jnp.dot(
        chosen_my.reshape(blocks * mine, SEQ_TOK), before, preferred_element_type=jnp.float32
    ).reshape(blocks, mine, SEQ_TOK)
    ranks = jnp.where(chosen_my > 0, ranks, -1.0)
    normed_all = jnp.concatenate([held[0] for held in ring_gather([normed_two])])
    cot_all = jnp.concatenate([held[0] for held in cot_ring])
    logits = lax.dot_general(
        router_weight, normed_all, (((0,), (1,)), ((), ())), preferred_element_type=jnp.float32
    )
    taken = jnp.swapaxes(chosen_all, 0, 1).reshape(EXPERTS, blocks * SEQ_TOK) > 0
    picked = jnp.where(taken, logits, NEG)
    weights = jnp.where(taken, jnp.exp(picked - jnp.max(picked, 0, keepdims=True)), 0.0)
    gates_all = weights / jnp.sum(weights, 0, keepdims=True)
    gates = gates_all[:, :rows]
    gates_my = lax.dynamic_slice_in_dim(gates_all, my_index * mine, mine, 0)
    gates_my = by_block(jnp.swapaxes(gates_my.reshape(mine, ctx_count, rows), 0, 1))
    slot_ids = jnp.arange(MOST, dtype=jnp.int32).astype(jnp.float32)
    match = ranks[:, :, None, :] == slot_ids[:, None]
    chances = jnp.where(match, gates_my[:, :, None, :], 0.0)
    dispatch = match.astype(jnp.bfloat16).reshape(blocks, mine * MOST, SEQ_TOK)
    combine = chances.astype(jnp.bfloat16).reshape(blocks, mine * MOST, SEQ_TOK)
    slot_gates = jnp.sum(chances, -1, keepdims=True).astype(jnp.bfloat16).astype(jnp.float32)
    normed_blocks = normed_all.reshape(blocks, SEQ_TOK, D)
    cot_blocks = cot_all.reshape(blocks, SEQ_TOK, D)
    slot_shape = (blocks, mine, MOST, D)
    arrived, cot_slots = (
        jnp.einsum("bst,btd->bsd", dispatch, one, preferred_element_type=jnp.float32)
        .astype(jnp.bfloat16)
        .reshape(slot_shape)
        for one in (normed_blocks, cot_blocks)
    )
    produced, grad_arrived, slot_dots, gate_local, up_local, down_local = experts_pass(
        arrived, cot_slots, slot_gates, gate_full, up_full, down_full
    )
    gate_dots = jnp.sum(jnp.where(match, slot_dots, 0.0), 2)
    gate_dots = jnp.swapaxes(gate_dots.reshape(ctx_count, SEQ_GRP, mine, SEQ_TOK), 1, 2)
    ours = jnp.arange(EXPERTS, dtype=jnp.int32)[:, None] // mine == my_index
    gate_dots = jnp.where(
        ours, jnp.tile(gate_dots.reshape(ctx_count, mine, rows), (1, EXPERTS // mine, 1)), 0.0
    ).reshape(ctx_count, flag_rows, D)
    coarse = lax.reduce_precision(gate_dots, 8, 7)

    def to_tokens(matrix, slot_values):
        return jnp.einsum(
            "bst,bsd->btd",
            matrix,
            slot_values.reshape(blocks, mine * MOST, D),
            preferred_element_type=jnp.float32,
        ).astype(jnp.bfloat16).reshape(ctx_count, rows, D)

    sent_part = jnp.concatenate(
        [
            to_tokens(dispatch, grad_arrived),
            coarse.astype(jnp.bfloat16),
            (gate_dots - coarse).astype(jnp.bfloat16),
        ],
        1,
    )
    grad_sent = ring_sum(lambda k, p: sent_part[k], 1)[0]
    grad_gates = (
        grad_sent[rows : rows + flag_rows] + grad_sent[rows + flag_rows :]
    ).reshape(EXPERTS, rows)
    grad_sent = grad_sent[:rows]
    mixed_part = to_tokens(combine, produced)
    gate_grad, up_grad, down_grad = (
        lax.psum_scatter(local, "wsh", scatter_dimension=0).astype(jnp.float32)
        for local in (gate_local, up_local, down_local)
    )
    grad_logits = (gates * (grad_gates - jnp.sum(gates * grad_gates, 0, keepdims=True))).astype(
        jnp.bfloat16
    )
    router_local = lax.dot_general(
        normed_two, grad_logits, (((0,), (1,)), ((), ())), preferred_element_type=jnp.float32
    )
    grad_normed_two = grad_sent + lax.dot_general(
        grad_logits, router_weight, (((0,), (1,)), ((), ())), preferred_element_type=jnp.float32
    )
    grad_resid_norm, second_local = norm_back(resid, scale_two, second_gain, grad_normed_two)
    grad_resid = upstream.astype(jnp.float32) + grad_resid_norm
    grad_branch = grad_resid.astype(jnp.bfloat16)
    out_local = lax.dot_general(
        attended, grad_branch, (((0,), (0,)), ((), ())), preferred_element_type=jnp.float32
    )
    grad_attended = lax.dot_general(
        grad_branch, out_weight, (((1,), (1,)), ((), ())), preferred_element_type=jnp.float32
    ).astype(jnp.bfloat16)
    grad_query, grad_whole = attend_back(
        owner,
        query,
        whole,
        grad_attended.reshape(SEQ_GRP, SEQ_TOK, width_q),
    )
    grad_query = rotate(grad_query.reshape(SEQ_GRP, SEQ_TOK, HEADS, HEAD_DIM), local_place, -1.0)
    grad_query = grad_query.astype(jnp.bfloat16).reshape(rows, width_q)
    kv_grad = ring_sum(lambda k, p: grad_whole[k], 1)[0]
    in_first = lax.dot_general(
        normed, grad_query, (((0,), (0,)), ((), ())), preferred_element_type=jnp.float32
    )
    low = jnp.bfloat16
    early = spread(
        jnp.concatenate(
            [
                in_first.astype(low),
                out_local.astype(low),
                router_local.astype(low),
                second_local[:, None].astype(low),
                jnp.zeros((D, SEQ_TOK - EXPERTS - 1), low),
            ],
            -1,
        )
    )
    kv_grad, early, mixed_part = lax.optimization_barrier((kv_grad, early, mixed_part))
    mixture = ring_sum(lambda k, p: mixed_part[k], 1)[0]
    layer_out = (resid + mixture).astype(jnp.bfloat16).reshape(SEQ_GRP, SEQ_TOK, D)
    kv_grad = kv_grad.reshape(
        SEQ_GRP, SEQ_TOK, KV_HEADS // 2, 2, PAIR
    )
    grad_key = rotate(
        kv_grad[:, :, :, 0].reshape(SEQ_GRP, SEQ_TOK, KV_HEADS, HEAD_DIM), local_place, -1.0
    )
    grad_pair = jnp.concatenate(
        [grad_key.reshape(rows, width_k), kv_grad[:, :, :, 1].reshape(rows, width_k)], -1
    ).astype(jnp.bfloat16)
    in_second = lax.dot_general(
        normed, grad_pair, (((0,), (0,)), ((), ())), preferred_element_type=jnp.float32
    )
    grad_normed = lax.dot_general(
        grad_query, in_weight[:, :width_q], (((1,), (1,)), ((), ())), preferred_element_type=jnp.float32
    ) + lax.dot_general(
        grad_pair, in_weight[:, width_q:], (((1,), (1,)), ((), ())), preferred_element_type=jnp.float32
    )
    grad_inputs_norm, first_local = norm_back(inputs, scale_one, first_gain, grad_normed)
    tokens_grad = (grad_resid + grad_inputs_norm).astype(jnp.bfloat16).reshape(SEQ_GRP, SEQ_TOK, D)
    in_second = spread(
        jnp.concatenate(
            [in_second, jnp.broadcast_to(first_local[:, None], (D, SEQ_TOK))], -1
        ).astype(jnp.bfloat16)
    )
    in_grad = jnp.concatenate([early[:, :width_q], in_second[:, : 2 * width_k]], -1)
    first_gain_grad = in_second[:, 2 * width_k]
    out_grad = early[:, width_q : width_q + D]
    small = early[:, width_q + D :]
    router_grad = small[:, :EXPERTS]
    second_gain_grad = small[:, EXPERTS]
    return (
        layer_out,
        tokens_grad,
        in_grad,
        out_grad,
        first_gain_grad,
        second_gain_grad,
        router_grad,
        gate_grad,
        up_grad,
        down_grad,
    )


def solution(mesh):
    placed = (
        P("wsh", "ctx", None),
        P("wsh", "ctx", None),
        P(),
        P(),
        P(),
        P(),
        P(),
        P("ctx", None, "wsh"),
        P("ctx", None, "wsh"),
        P("ctx", "wsh", None),
        P("wsh", "ctx", None),
    )
    return jax.shard_map(
        shards,
        mesh=mesh,
        in_specs=placed,
        out_specs=(
            P("wsh", "ctx", None),
            P("wsh", "ctx", None),
            P(("ctx", "wsh"), None),
            P(("ctx", "wsh"), None),
            P(("ctx", "wsh")),
            P(("ctx", "wsh")),
            P(("ctx", "wsh"), None),
            P("ctx", None, "wsh"),
            P("ctx", None, "wsh"),
            P("ctx", "wsh", None),
        ),
        check_vma=False,
    )
```

```python
import jax
import jax.numpy as jnp
from jax import lax
from jax.experimental import pallas as pl
from jax.experimental.pallas import tpu as pltpu
from jax.sharding import PartitionSpec as P

D = 1024
HEADS = 16
KV_HEADS = 8
HEAD_DIM = 64
EXPERTS = 32
TOP = 8
SEQ_TOK = 128
SEQ_GRP = 2
HALF = 64
MOST = 48


EPS = 1e-05
THETA = 10000.0
NEG = -1e30


def dealt(rows, length):
    owner = rows // SEQ_TOK
    offset = rows % SEQ_TOK
    early = owner * HALF + offset
    late = length - (owner + 1) * HALF + offset - HALF
    return jnp.where(offset < HALF, early, late)


def rotate(values, place, sign):
    half_dim = values.shape[-1] // 2
    freq = THETA ** (-2.0 * jnp.arange(half_dim, dtype=jnp.float32) / values.shape[-1])
    angle = place.astype(jnp.float32)[:, None] * freq[None, :]
    cosine = jnp.cos(angle)[:, None, :]
    sine = sign * jnp.sin(angle)[:, None, :]
    front = values[..., :half_dim]
    back = values[..., half_dim:]
    return jnp.concatenate([front * cosine - back * sine, back * cosine + front * sine], -1)


def norm_back(values, scale, gain, grad_out):
    weighted = grad_out * gain
    grad_in = scale * weighted - values * scale**3 * jnp.mean(weighted * values, -1, keepdims=True)
    return (grad_in, jnp.sum(grad_out * values * scale, 0))


def ring_order(count):
    return list(range(0, count, 2)) + list(reversed(range(1, count, 2)))


def ring_shift(count, step):
    order = ring_order(count)
    return [(order[i], order[(i + step) % count]) for i in range(count)]


def ring_gather(parts):
    count = lax.axis_size("ctx")
    ahead, behind = ring_shift(count, 1), ring_shift(count, -1)
    held = [list(parts)] + [[None] * len(parts) for _ in range(count - 1)]
    far = count // 2
    for p, part in enumerate(parts):
        up, down = part, part
        ups = far if p % 2 == 0 else count - 1 - far
        for step in range(1, far + 1):
            if step <= ups:
                up = lax.ppermute(up, "ctx", ahead)
                held[step][p] = up
            if step <= count - 1 - ups:
                down = lax.ppermute(down, "ctx", behind)
                held[count - step][p] = down
    return held


def add_low(left, right):
    return (left.astype(jnp.float32) + right.astype(jnp.float32)).astype(left.dtype)


def ring_sum(block, parts):
    count = lax.axis_size("ctx")
    ahead, behind = ring_shift(count, 1), ring_shift(count, -1)
    far = count // 2
    sums = []
    for p in range(parts):
        ups = far if p % 2 == 0 else count - 1 - far
        downs = count - 1 - ups
        up = block(count - ups, p)
        for step in range(ups - 1, 0, -1):
            up = lax.ppermute(up, "ctx", ahead)
            up = add_low(up, block(count - step, p))
        up = lax.ppermute(up, "ctx", ahead)
        down = block(downs, p)
        for step in range(downs - 1, 0, -1):
            down = lax.ppermute(down, "ctx", behind)
            down = add_low(down, block(step, p))
        down = lax.ppermute(down, "ctx", behind)
        own = block(0, p).astype(jnp.float32)
        sums.append(up.astype(jnp.float32) + down.astype(jnp.float32) + own)
    return sums


def spread(local):
    for axis in ("wsh", "ctx"):
        count = lax.axis_size(axis)
        me = lax.axis_index(axis)
        outer = lax.axis_size("ctx") if axis == "wsh" else 1
        bit = 1
        while bit < count:
            split = local.reshape(outer * (count // (2 * bit)), 2, -1, local.shape[-1])
            mine = (me // bit) % 2
            swap = [(i, i ^ bit) for i in range(count)]
            sent = lax.dynamic_index_in_dim(split, 1 - mine, 1, False)
            sent = lax.ppermute(sent, axis, swap)
            kept = lax.dynamic_index_in_dim(split, mine, 1, False)
            local = add_low(kept, sent).reshape(-1, local.shape[-1])
            bit *= 2
    return local.astype(jnp.float32)


PAIR = 2 * HEAD_DIM


def nt(left, right):
    return lax.dot_general(left, right, (((1,), (1,)), ((), ())), preferred_element_type=jnp.float32)


def tn(left, right):
    return lax.dot_general(left, right, (((0,), (0,)), ((), ())), preferred_element_type=jnp.float32)


def nn(left, right):
    return jnp.dot(left, right, preferred_element_type=jnp.float32)


def halves(ref, head):
    start = head * PAIR
    block = ref[0, :, start : start + PAIR]
    both = [block[:, :HEAD_DIM], block[:, HEAD_DIM:]]
    return (
        jnp.concatenate([one[:HALF] for one in both], 0),
        jnp.concatenate([one[HALF:] for one in both], 0),
    )


def key_parts(ref):
    whole = ref[...]
    count = whole.shape[0]
    early = whole[:, :HALF].reshape(count * HALF, -1)
    late = whole[:, HALF:].reshape(count * HALF, -1)
    return early, late


def weigh(scores):
    peak = jnp.max(scores[0], 0, keepdims=True)
    for more in scores[1:]:
        peak = jnp.maximum(peak, jnp.max(more, 0, keepdims=True))
    powers = [jnp.exp(part - peak) for part in scores]
    total = sum(jnp.sum(part, 0, keepdims=True) for part in powers)
    inverse = 1.0 / total
    return [part * inverse for part in powers]


def split_heads(stacked_early, stacked_late):
    return jnp.concatenate(
        [
            jnp.concatenate([stacked_early[:HALF], stacked_early[HALF:]], 1),
            jnp.concatenate([stacked_late[:HALF], stacked_late[HALF:]], 1),
        ],
        0,
    )


def fill_bias(owner, bias_early, bias_late):
    count = owner.shape[0] - 1

    @pl.when((pl.program_id(0) == 0) & (pl.program_id(1) == 0))
    def fill():
        lead = lax.broadcasted_iota(jnp.int32, (HALF, SEQ_TOK), 0) - (
            lax.broadcasted_iota(jnp.int32, (HALF, SEQ_TOK), 1) % HALF
        )
        for k in range(count):
            gap = (owner[count] - owner[k]) * HALF
            span = slice(k * HALF, (k + 1) * HALF)
            bias_early[span] = jnp.where(lead <= gap, 0.0, NEG)
            bias_late[span] = jnp.where(lead <= -gap, 0.0, NEG)


def attend_kernel(owner, query, keys, out, bias_early, bias_late):
    fill_bias(owner, bias_early, bias_late)
    early, late = key_parts(keys)
    for head in range(2):
        at = head * HEAD_DIM
        k_e, k_l = early[:, at : at + HEAD_DIM], late[:, at : at + HEAD_DIM]
        v_e, v_l = early[:, PAIR + at : PAIR + at + HEAD_DIM], late[:, PAIR + at : PAIR + at + HEAD_DIM]
        q_e, q_l = halves(query, head)
        (p_ee,) = weigh([nt(k_e, q_e) + bias_early[...]])
        p_el, p_ll = weigh([nt(k_e, q_l), nt(k_l, q_l) + bias_late[...]])
        o_e = tn(p_ee.astype(jnp.bfloat16), v_e)
        o_l = tn(p_el.astype(jnp.bfloat16), v_e) + tn(p_ll.astype(jnp.bfloat16), v_l)
        out[0, :, head * PAIR : (head + 1) * PAIR] = split_heads(o_e, o_l).astype(jnp.bfloat16)


def attend_back_kernel(
    owner, query, keys, grad, grad_query, grad_keys, bias_early, bias_late
):
    fill_bias(owner, bias_early, bias_late)
    early, late = key_parts(keys)
    scale = HEAD_DIM ** (-0.5)
    count = keys.shape[0]
    parts_e, parts_l = [], []
    for head in range(2):
        at = head * HEAD_DIM
        k_e, k_l = early[:, at : at + HEAD_DIM], late[:, at : at + HEAD_DIM]
        v_e, v_l = early[:, PAIR + at : PAIR + at + HEAD_DIM], late[:, PAIR + at : PAIR + at + HEAD_DIM]
        q_e, q_l = halves(query, head)
        d_e, d_l = halves(grad, head)
        (p_ee,) = weigh([nt(k_e, q_e) + bias_early[...]])
        p_el, p_ll = weigh([nt(k_e, q_l), nt(k_l, q_l) + bias_late[...]])
        g_ee, g_el, g_ll = nt(v_e, d_e), nt(v_e, d_l), nt(v_l, d_l)
        delta_e = jnp.sum(p_ee * g_ee, 0, keepdims=True)
        delta_l = jnp.sum(p_el * g_el, 0, keepdims=True) + jnp.sum(p_ll * g_ll, 0, keepdims=True)
        s_ee = (p_ee * (g_ee - delta_e)).astype(jnp.bfloat16)
        s_el = (p_el * (g_el - delta_l)).astype(jnp.bfloat16)
        s_ll = (p_ll * (g_ll - delta_l)).astype(jnp.bfloat16)
        gq_e = tn(s_ee, k_e) * scale
        gq_l = (tn(s_el, k_e) + tn(s_ll, k_l)) * scale
        grad_query[0, :, head * PAIR : (head + 1) * PAIR] = split_heads(gq_e, gq_l)
        gk_e = nn(s_ee, q_e) + nn(s_el, q_l)
        gk_l = nn(s_ll, q_l)
        gv_e = nn(p_ee.astype(jnp.bfloat16), d_e) + nn(p_el.astype(jnp.bfloat16), d_l)
        gv_l = nn(p_ll.astype(jnp.bfloat16), d_l)
        parts_e.append((gk_e, gv_e))
        parts_l.append((gk_l, gv_l))
    for parts, start in ((parts_e, 0), (parts_l, HALF)):
        for kind in range(2):
            joined = jnp.concatenate([parts[0][kind], parts[1][kind]], 1)
            grad_keys[:, start : start + HALF, kind * PAIR : (kind + 1) * PAIR] = (
                joined.astype(jnp.bfloat16).reshape(count, HALF, PAIR)
            )


def attend_specs(count):
    scalars = pl.BlockSpec(memory_space=pltpu.SMEM)
    rows = pl.BlockSpec((1, SEQ_TOK, 2 * PAIR), lambda s, j: (s, 0, j))
    keys = pl.BlockSpec((count, SEQ_TOK, 2 * PAIR), lambda s, j: (0, s, j))
    scratch = [pltpu.VMEM((count * HALF, SEQ_TOK), jnp.float32)] * 2
    return scalars, rows, keys, scratch


def attend(owner, query, keys):
    count = keys.shape[0]
    scalars, rows, key_rows, scratch = attend_specs(count)
    return pl.pallas_call(
        attend_kernel,
        out_shape=jax.ShapeDtypeStruct(query.shape, jnp.bfloat16),
        grid=(SEQ_GRP, KV_HEADS // 2),
        in_specs=[scalars, rows, key_rows],
        out_specs=rows,
        scratch_shapes=scratch,
        cost_estimate=pl.CostEstimate(
            flops=20 * query.size * count * SEQ_TOK,
            bytes_accessed=2 * keys.size + 4 * query.size,
            transcendentals=0,
        ),
    )(owner, query, keys)


def attend_back(owner, query, keys, grad):
    count = keys.shape[0]
    scalars, rows, key_rows, scratch = attend_specs(count)
    return pl.pallas_call(
        attend_back_kernel,
        out_shape=(
            jax.ShapeDtypeStruct(query.shape, jnp.float32),
            jax.ShapeDtypeStruct((count, SEQ_GRP * SEQ_TOK, keys.shape[2]), jnp.bfloat16),
        ),
        grid=(SEQ_GRP, KV_HEADS // 2),
        in_specs=[scalars, rows, key_rows, rows],
        out_specs=(rows, key_rows),
        scratch_shapes=scratch,
        cost_estimate=pl.CostEstimate(
            flops=30 * query.size * count * SEQ_TOK,
            bytes_accessed=4 * keys.size + 8 * query.size,
            transcendentals=0,
        ),
    )(owner, query, keys, grad)


STEP_BLOCKS = 16


def expert_kernel(
    arrived_ref,
    cot_ref,
    slot_gate_ref,
    gate_ref,
    up_ref,
    down_ref,
    produced_ref,
    back_ref,
    dots_ref,
    gate_grad_ref,
    up_grad_ref,
    down_grad_ref,
    *sums,
):
    rows = arrived_ref.shape[0] * MOST
    arrived = arrived_ref[:, 0].reshape(rows, D)
    cot = cot_ref[:, 0].reshape(rows, D)
    gate_w, up_w, down_w = gate_ref[0], up_ref[0], down_ref[0]
    gate_act = nn(arrived, gate_w)
    up_act = nn(arrived, up_w)
    sigma = jax.nn.sigmoid(gate_act)
    swish = gate_act * sigma
    hidden = (swish * up_act).astype(jnp.bfloat16)
    produced = nn(hidden, down_w).astype(jnp.bfloat16)
    produced_ref[:, 0] = produced.reshape(-1, MOST, D)
    wide = cot.astype(jnp.float32)
    dots = jnp.sum(produced.astype(jnp.float32) * wide, -1, keepdims=True)
    dots_ref[:, 0] = dots.reshape(-1, MOST, 1)
    grad_produced = (wide * slot_gate_ref[:, 0].reshape(rows, 1)).astype(jnp.bfloat16)
    grad_hidden = nt(grad_produced, down_w).astype(jnp.bfloat16).astype(jnp.float32)
    slope = sigma * (1.0 + gate_act * (1.0 - sigma))
    grad_gate = (grad_hidden * up_act * slope).astype(jnp.bfloat16)
    grad_up = (grad_hidden * swish).astype(jnp.bfloat16)
    back = nt(grad_gate, gate_w) + nt(grad_up, up_w)
    back_ref[:, 0] = back.astype(jnp.bfloat16).reshape(-1, MOST, D)
    grads = [tn(arrived, grad_gate), tn(arrived, grad_up), tn(hidden, grad_produced)]
    if sums:
        first = pl.program_id(1) == 0
        for held, grad in zip(sums, grads):
            held[...] = jnp.where(first, grad, held[...] + grad)
        grads = [held[...] for held in sums]
    quarter = gate_w.shape[1] // 4
    for k in range(4):
        span = slice(k * quarter, (k + 1) * quarter)
        gate_grad_ref[k, 0] = grads[0][:, span].astype(jnp.bfloat16)
        up_grad_ref[k, 0] = grads[1][:, span].astype(jnp.bfloat16)
        down_grad_ref[k, 0] = grads[2][span].astype(jnp.bfloat16)


def experts_pass(arrived, cot, slot_gates, gate_w, up_w, down_w):
    blocks, mine = arrived.shape[:2]
    steps = blocks // STEP_BLOCKS
    hidden = gate_w.shape[2]
    quarter = hidden // 4

    def slot_rows(width):
        return pl.BlockSpec((STEP_BLOCKS, 1, MOST, width), lambda e, c: (c, e, 0, 0))

    def per_expert(*shape):
        return pl.BlockSpec((1,) + shape, lambda e, c: (e, 0, 0))

    def pieces(*shape):
        return pl.BlockSpec((4, 1) + shape, lambda e, c: (0, e, 0, 0))

    low = jnp.bfloat16
    return pl.pallas_call(
        expert_kernel,
        grid=(mine, steps),
        in_specs=[
            slot_rows(D),
            slot_rows(D),
            slot_rows(1),
            per_expert(D, hidden),
            per_expert(D, hidden),
            per_expert(hidden, D),
        ],
        out_specs=(
            slot_rows(D),
            slot_rows(D),
            slot_rows(1),
            pieces(D, quarter),
            pieces(D, quarter),
            pieces(quarter, D),
        ),
        out_shape=(
            jax.ShapeDtypeStruct(arrived.shape, low),
            jax.ShapeDtypeStruct(arrived.shape, low),
            jax.ShapeDtypeStruct(slot_gates.shape, jnp.float32),
            jax.ShapeDtypeStruct((4, mine, D, quarter), low),
            jax.ShapeDtypeStruct((4, mine, D, quarter), low),
            jax.ShapeDtypeStruct((4, mine, quarter, D), low),
        ),
        scratch_shapes=[]
        if steps == 1
        else [
            pltpu.VMEM((D, hidden), jnp.float32),
            pltpu.VMEM((D, hidden), jnp.float32),
            pltpu.VMEM((hidden, D), jnp.float32),
        ],
        compiler_params=pltpu.CompilerParams(vmem_limit_bytes=63 * 1024 * 1024),
        cost_estimate=pl.CostEstimate(
            flops=18 * arrived.size * hidden,
            bytes_accessed=8 * arrived.size + 12 * mine * D * hidden,
            transcendentals=0,
        ),
    )(arrived, cot, slot_gates, gate_w, up_w, down_w)


def shards(
    tokens,
    routes,
    in_weight,
    out_weight,
    first_gain,
    second_gain,
    router_weight,
    gate_weight,
    up_weight,
    down_weight,
    cotangent,
):
    ctx_count = lax.axis_size("ctx")
    length = SEQ_TOK * ctx_count
    rows = SEQ_GRP * SEQ_TOK
    width_q = HEADS * HEAD_DIM
    width_k = KV_HEADS * HEAD_DIM
    my_index = lax.axis_index("ctx")
    order = ring_order(ctx_count)
    place_of = jnp.array([order.index(c) for c in range(ctx_count)], jnp.int32)
    my_place = place_of[my_index]
    table = [
        [order[(order.index(c) - k) % ctx_count] for k in range(ctx_count)] + [c]
        for c in range(ctx_count)
    ]
    owner = lax.dynamic_index_in_dim(jnp.array(table, jnp.int32), my_index, 0, False)
    local_place = dealt(my_index * SEQ_TOK + jnp.arange(SEQ_TOK, dtype=jnp.int32), length)
    upstream = cotangent.reshape(rows, D)
    chosen = jnp.any(
        routes.reshape(rows, TOP).T[:, None, :] == jnp.arange(EXPERTS, dtype=jnp.int32)[:, None], 0
    )
    gate_full, up_full, down_full = (
        lax.all_gather(gate_weight, "wsh", axis=2, tiled=True),
        lax.all_gather(up_weight, "wsh", axis=2, tiled=True),
        lax.all_gather(down_weight, "wsh", axis=1, tiled=True),
    )
    inputs = tokens.astype(jnp.float32).reshape(rows, D)
    scale_one = lax.rsqrt(jnp.mean(inputs * inputs, -1, keepdims=True) + EPS)
    normed = (inputs * scale_one * first_gain).astype(jnp.bfloat16)
    mixed = jnp.dot(normed, in_weight, preferred_element_type=jnp.float32).reshape(
        SEQ_GRP, SEQ_TOK, -1
    )
    query = rotate(
        mixed[..., :width_q].reshape(SEQ_GRP, SEQ_TOK, HEADS, HEAD_DIM), local_place, 1.0
    ).astype(jnp.bfloat16)
    query = (query * jnp.bfloat16(HEAD_DIM ** (-0.5))).reshape(SEQ_GRP, SEQ_TOK, width_q)
    key = rotate(
        mixed[..., width_q : width_q + width_k].reshape(SEQ_GRP, SEQ_TOK, KV_HEADS, HEAD_DIM),
        local_place,
        1.0,
    ).astype(jnp.bfloat16)
    value = mixed[..., width_q + width_k :].astype(jnp.bfloat16)
    pairs = (SEQ_GRP, SEQ_TOK, KV_HEADS // 2, PAIR)
    key_value = jnp.concatenate([key.reshape(pairs), value.reshape(pairs)], -1).reshape(
        rows, 2 * width_k
    )
    flags = chosen.astype(jnp.bfloat16).reshape(-1, 2 * width_k)
    flag_rows = flags.shape[0]
    flags = jnp.concatenate([flags, jnp.zeros_like(flags)], 0)
    whole = jnp.stack([held[0] for held in ring_gather([jnp.concatenate([key_value, flags], 0)])])
    whole, cot_own = lax.optimization_barrier((whole, upstream))
    cot_ring = ring_gather([cot_own])
    attended = attend(owner, query, whole)
    attended = attended.reshape(rows, width_q)
    resid = inputs + jnp.dot(attended, out_weight, preferred_element_type=jnp.float32)
    scale_two = lax.rsqrt(jnp.mean(resid * resid, -1, keepdims=True) + EPS)
    normed_two = (resid * scale_two * second_gain).astype(jnp.bfloat16)
    blocks = SEQ_GRP * ctx_count
    mine = gate_weight.shape[0]
    chosen_all = whole[:, rows : rows + flag_rows].reshape(ctx_count, EXPERTS, rows)
    chosen_my = lax.dynamic_slice_in_dim(chosen_all, my_index * mine, mine, 1)

    def by_block(values):
        split = values.reshape(ctx_count, mine, SEQ_GRP, SEQ_TOK)
        return jnp.swapaxes(split, 1, 2).reshape(blocks, mine, SEQ_TOK)

    chosen_my = by_block(chosen_my)
    before = (
        jnp.arange(SEQ_TOK, dtype=jnp.int32)[:, None] < jnp.arange(SEQ_TOK, dtype=jnp.int32)[None, :]
    ).astype(jnp.bfloat16)
    ranks = jnp.dot(
        chosen_my.reshape(blocks * mine, SEQ_TOK), before, preferred_element_type=jnp.float32
    ).reshape(blocks, mine, SEQ_TOK)
    ranks = jnp.where(chosen_my > 0, ranks, -1.0)
    normed_all = jnp.concatenate([held[0] for held in ring_gather([normed_two])])
    cot_all = jnp.concatenate([held[0] for held in cot_ring])
    logits = lax.dot_general(
        router_weight, normed_all, (((0,), (1,)), ((), ())), preferred_element_type=jnp.float32
    )
    taken = jnp.swapaxes(chosen_all, 0, 1).reshape(EXPERTS, blocks * SEQ_TOK) > 0
    picked = jnp.where(taken, logits, NEG)
    weights = jnp.where(taken, jnp.exp(picked - jnp.max(picked, 0, keepdims=True)), 0.0)
    gates_all = weights / jnp.sum(weights, 0, keepdims=True)
    gates = gates_all[:, :rows]
    gates_my = lax.dynamic_slice_in_dim(gates_all, my_index * mine, mine, 0)
    gates_my = by_block(jnp.swapaxes(gates_my.reshape(mine, ctx_count, rows), 0, 1))
    slot_ids = jnp.arange(MOST, dtype=jnp.int32).astype(jnp.float32)
    match = ranks[:, :, None, :] == slot_ids[:, None]
    chances = jnp.where(match, gates_my[:, :, None, :], 0.0)
    dispatch = match.astype(jnp.bfloat16).reshape(blocks, mine * MOST, SEQ_TOK)
    combine = chances.astype(jnp.bfloat16).reshape(blocks, mine * MOST, SEQ_TOK)
    slot_gates = jnp.sum(chances, -1, keepdims=True).astype(jnp.bfloat16).astype(jnp.float32)
    normed_blocks = normed_all.reshape(blocks, SEQ_TOK, D)
    cot_blocks = cot_all.reshape(blocks, SEQ_TOK, D)
    slot_shape = (blocks, mine, MOST, D)
    arrived, cot_slots = (
        jnp.einsum("bst,btd->bsd", dispatch, one, preferred_element_type=jnp.float32)
        .astype(jnp.bfloat16)
        .reshape(slot_shape)
        for one in (normed_blocks, cot_blocks)
    )
    produced, grad_arrived, slot_dots, gate_local, up_local, down_local = experts_pass(
        arrived, cot_slots, slot_gates, gate_full, up_full, down_full
    )
    gate_dots = jnp.sum(jnp.where(match, slot_dots, 0.0), 2)
    gate_dots = jnp.swapaxes(gate_dots.reshape(ctx_count, SEQ_GRP, mine, SEQ_TOK), 1, 2)
    ours = jnp.arange(EXPERTS, dtype=jnp.int32)[:, None] // mine == my_index
    gate_dots = jnp.where(
        ours, jnp.tile(gate_dots.reshape(ctx_count, mine, rows), (1, EXPERTS // mine, 1)), 0.0
    ).reshape(ctx_count, flag_rows, D)
    coarse = lax.reduce_precision(gate_dots, 8, 7)

    def to_tokens(matrix, slot_values):
        return jnp.einsum(
            "bst,bsd->btd",
            matrix,
            slot_values.reshape(blocks, mine * MOST, D),
            preferred_element_type=jnp.float32,
        ).astype(jnp.bfloat16).reshape(ctx_count, rows, D)

    sent_part = jnp.concatenate(
        [
            to_tokens(dispatch, grad_arrived),
            coarse.astype(jnp.bfloat16),
            (gate_dots - coarse).astype(jnp.bfloat16),
        ],
        1,
    )
    grad_sent = ring_sum(lambda k, p: sent_part[k], 1)[0]
    grad_gates = (
        grad_sent[rows : rows + flag_rows] + grad_sent[rows + flag_rows :]
    ).reshape(EXPERTS, rows)
    grad_sent = grad_sent[:rows]
    mixed_part = to_tokens(combine, produced)
    gate_grad, up_grad, down_grad = (
        lax.psum_scatter(local, "wsh", scatter_dimension=0).astype(jnp.float32)
        for local in (gate_local, up_local, down_local)
    )
    grad_logits = (gates * (grad_gates - jnp.sum(gates * grad_gates, 0, keepdims=True))).astype(
        jnp.bfloat16
    )
    router_local = lax.dot_general(
        normed_two, grad_logits, (((0,), (1,)), ((), ())), preferred_element_type=jnp.float32
    )
    grad_normed_two = grad_sent + lax.dot_general(
        grad_logits, router_weight, (((0,), (1,)), ((), ())), preferred_element_type=jnp.float32
    )
    grad_resid_norm, second_local = norm_back(resid, scale_two, second_gain, grad_normed_two)
    grad_resid = upstream.astype(jnp.float32) + grad_resid_norm
    grad_branch = grad_resid.astype(jnp.bfloat16)
    out_local = lax.dot_general(
        attended, grad_branch, (((0,), (0,)), ((), ())), preferred_element_type=jnp.float32
    )
    grad_attended = lax.dot_general(
        grad_branch, out_weight, (((1,), (1,)), ((), ())), preferred_element_type=jnp.float32
    ).astype(jnp.bfloat16)
    grad_query, grad_whole = attend_back(
        owner,
        query,
        whole,
        grad_attended.reshape(SEQ_GRP, SEQ_TOK, width_q),
    )
    grad_query = rotate(grad_query.reshape(SEQ_GRP, SEQ_TOK, HEADS, HEAD_DIM), local_place, -1.0)
    grad_query = grad_query.astype(jnp.bfloat16).reshape(rows, width_q)
    mixed_part = jnp.take(mixed_part, (my_place - place_of) % ctx_count, axis=0)
    mixed_part, grad_whole = lax.optimization_barrier((mixed_part, grad_whole))
    mixture = lax.psum_scatter(
        mixed_part.reshape(ctx_count * rows, D), "ctx", scatter_dimension=0, tiled=True
    )
    layer_out = (
        (resid + mixture.astype(jnp.float32)).astype(jnp.bfloat16).reshape(SEQ_GRP, SEQ_TOK, D)
    )
    kv_grad = ring_sum(lambda k, p: grad_whole[k], 1)[0]
    in_first = lax.dot_general(
        normed, grad_query, (((0,), (0,)), ((), ())), preferred_element_type=jnp.float32
    )
    low = jnp.bfloat16
    early = spread(
        jnp.concatenate(
            [
                in_first.astype(low),
                out_local.astype(low),
                router_local.astype(low),
                second_local[:, None].astype(low),
                jnp.zeros((D, SEQ_TOK - EXPERTS - 1), low),
            ],
            -1,
        ),
    )
    kv_grad, early = lax.optimization_barrier((kv_grad, early))
    kv_grad = kv_grad.reshape(
        SEQ_GRP, SEQ_TOK, KV_HEADS // 2, 2, PAIR
    )
    grad_key = rotate(
        kv_grad[:, :, :, 0].reshape(SEQ_GRP, SEQ_TOK, KV_HEADS, HEAD_DIM), local_place, -1.0
    )
    grad_pair = jnp.concatenate(
        [grad_key.reshape(rows, width_k), kv_grad[:, :, :, 1].reshape(rows, width_k)], -1
    ).astype(jnp.bfloat16)
    in_second = lax.dot_general(
        normed, grad_pair, (((0,), (0,)), ((), ())), preferred_element_type=jnp.float32
    )
    grad_normed = lax.dot_general(
        grad_query, in_weight[:, :width_q], (((1,), (1,)), ((), ())), preferred_element_type=jnp.float32
    ) + lax.dot_general(
        grad_pair, in_weight[:, width_q:], (((1,), (1,)), ((), ())), preferred_element_type=jnp.float32
    )
    grad_inputs_norm, first_local = norm_back(inputs, scale_one, first_gain, grad_normed)
    tokens_grad = (grad_resid + grad_inputs_norm).astype(jnp.bfloat16).reshape(SEQ_GRP, SEQ_TOK, D)
    in_second = spread(
        jnp.concatenate(
            [in_second, jnp.broadcast_to(first_local[:, None], (D, SEQ_TOK))], -1
        ).astype(jnp.bfloat16),
    )
    in_grad = jnp.concatenate([early[:, :width_q], in_second[:, : 2 * width_k]], -1)
    first_gain_grad = in_second[:, 2 * width_k]
    out_grad = early[:, width_q : width_q + D]
    small = early[:, width_q + D :]
    router_grad = small[:, :EXPERTS]
    second_gain_grad = small[:, EXPERTS]
    return (
        layer_out,
        tokens_grad,
        in_grad,
        out_grad,
        first_gain_grad,
        second_gain_grad,
        router_grad,
        gate_grad,
        up_grad,
        down_grad,
    )


def solution(mesh):
    placed = (
        P("wsh", "ctx", None),
        P("wsh", "ctx", None),
        P(),
        P(),
        P(),
        P(),
        P(),
        P("ctx", None, "wsh"),
        P("ctx", None, "wsh"),
        P("ctx", "wsh", None),
        P("wsh", "ctx", None),
    )
    return jax.shard_map(
        shards,
        mesh=mesh,
        in_specs=placed,
        out_specs=(
            P("wsh", "ctx", None),
            P("wsh", "ctx", None),
            P(("ctx", "wsh"), None),
            P(("ctx", "wsh"), None),
            P(("ctx", "wsh")),
            P(("ctx", "wsh")),
            P(("ctx", "wsh"), None),
            P("ctx", None, "wsh"),
            P("ctx", None, "wsh"),
            P("ctx", "wsh", None),
        ),
        check_vma=False,
    )
```

```python
import jax
import jax.numpy as jnp
from jax import lax
from jax.experimental import pallas as pl
from jax.experimental.pallas import tpu as pltpu
from jax.sharding import PartitionSpec as P

D = 1024
HEADS = 16
KV_HEADS = 8
HEAD_DIM = 64
EXPERTS = 32
TOP = 8
SEQ_TOK = 128
SEQ_GRP = 2
HALF = 64
MOST = 48


EPS = 1e-05
THETA = 10000.0
NEG = -1e30


def dealt(rows, length):
    owner = rows // SEQ_TOK
    offset = rows % SEQ_TOK
    early = owner * HALF + offset
    late = length - (owner + 1) * HALF + offset - HALF
    return jnp.where(offset < HALF, early, late)


def rotate(values, place, sign):
    half_dim = values.shape[-1] // 2
    freq = THETA ** (-2.0 * jnp.arange(half_dim, dtype=jnp.float32) / values.shape[-1])
    angle = place.astype(jnp.float32)[:, None] * freq[None, :]
    cosine = jnp.cos(angle)[:, None, :]
    sine = sign * jnp.sin(angle)[:, None, :]
    front = values[..., :half_dim]
    back = values[..., half_dim:]
    return jnp.concatenate([front * cosine - back * sine, back * cosine + front * sine], -1)


def norm_back(values, scale, gain, grad_out):
    weighted = grad_out * gain
    grad_in = scale * weighted - values * scale**3 * jnp.mean(weighted * values, -1, keepdims=True)
    return (grad_in, jnp.sum(grad_out * values * scale, 0))


def ring_order(count):
    return list(range(0, count, 2)) + list(reversed(range(1, count, 2)))


def ring_shift(count, step):
    order = ring_order(count)
    return [(order[i], order[(i + step) % count]) for i in range(count)]


def ring_gather(parts):
    count = lax.axis_size("ctx")
    ahead, behind = ring_shift(count, 1), ring_shift(count, -1)
    held = [list(parts)] + [[None] * len(parts) for _ in range(count - 1)]
    far = count // 2
    for p, part in enumerate(parts):
        up, down = part, part
        ups = far if p % 2 == 0 else count - 1 - far
        for step in range(1, far + 1):
            if step <= ups:
                up = lax.ppermute(up, "ctx", ahead)
                held[step][p] = up
            if step <= count - 1 - ups:
                down = lax.ppermute(down, "ctx", behind)
                held[count - step][p] = down
    return held


def add_low(left, right):
    return (left.astype(jnp.float32) + right.astype(jnp.float32)).astype(left.dtype)


def ring_sum(block, parts):
    count = lax.axis_size("ctx")
    ahead, behind = ring_shift(count, 1), ring_shift(count, -1)
    far = count // 2
    sums = []
    for p in range(parts):
        ups = far if p % 2 == 0 else count - 1 - far
        downs = count - 1 - ups
        up = block(count - ups, p)
        for step in range(ups - 1, 0, -1):
            up = lax.ppermute(up, "ctx", ahead)
            up = add_low(up, block(count - step, p))
        up = lax.ppermute(up, "ctx", ahead)
        down = block(downs, p)
        for step in range(downs - 1, 0, -1):
            down = lax.ppermute(down, "ctx", behind)
            down = add_low(down, block(step, p))
        down = lax.ppermute(down, "ctx", behind)
        own = block(0, p).astype(jnp.float32)
        sums.append(up.astype(jnp.float32) + down.astype(jnp.float32) + own)
    return sums


def spread(local):
    for axis in ("wsh", "ctx"):
        count = lax.axis_size(axis)
        me = lax.axis_index(axis)
        outer = lax.axis_size("ctx") if axis == "wsh" else 1
        bit = 1
        while bit < count:
            split = local.reshape(outer * (count // (2 * bit)), 2, -1, local.shape[-1])
            mine = (me // bit) % 2
            swap = [(i, i ^ bit) for i in range(count)]
            sent = lax.dynamic_index_in_dim(split, 1 - mine, 1, False)
            sent = lax.ppermute(sent, axis, swap)
            kept = lax.dynamic_index_in_dim(split, mine, 1, False)
            local = add_low(kept, sent).reshape(-1, local.shape[-1])
            bit *= 2
    return local.astype(jnp.float32)


PAIR = 2 * HEAD_DIM


def nt(left, right):
    return lax.dot_general(left, right, (((1,), (1,)), ((), ())), preferred_element_type=jnp.float32)


def tn(left, right):
    return lax.dot_general(left, right, (((0,), (0,)), ((), ())), preferred_element_type=jnp.float32)


def nn(left, right):
    return jnp.dot(left, right, preferred_element_type=jnp.float32)


def halves(ref, head):
    start = head * PAIR
    block = ref[0, :, start : start + PAIR]
    both = [block[:, :HEAD_DIM], block[:, HEAD_DIM:]]
    return (
        jnp.concatenate([one[:HALF] for one in both], 0),
        jnp.concatenate([one[HALF:] for one in both], 0),
    )


def key_parts(ref):
    whole = ref[...]
    count = whole.shape[0]
    early = whole[:, :HALF].reshape(count * HALF, -1)
    late = whole[:, HALF:].reshape(count * HALF, -1)
    return early, late


def weigh(scores):
    peak = jnp.max(scores[0], 0, keepdims=True)
    for more in scores[1:]:
        peak = jnp.maximum(peak, jnp.max(more, 0, keepdims=True))
    powers = [jnp.exp(part - peak) for part in scores]
    total = sum(jnp.sum(part, 0, keepdims=True) for part in powers)
    inverse = 1.0 / total
    return [part * inverse for part in powers]


def split_heads(stacked_early, stacked_late):
    return jnp.concatenate(
        [
            jnp.concatenate([stacked_early[:HALF], stacked_early[HALF:]], 1),
            jnp.concatenate([stacked_late[:HALF], stacked_late[HALF:]], 1),
        ],
        0,
    )


def fill_bias(owner, bias_early, bias_late):
    count = owner.shape[0] - 1

    @pl.when((pl.program_id(0) == 0) & (pl.program_id(1) == 0))
    def fill():
        lead = lax.broadcasted_iota(jnp.int32, (HALF, SEQ_TOK), 0) - (
            lax.broadcasted_iota(jnp.int32, (HALF, SEQ_TOK), 1) % HALF
        )
        for k in range(count):
            gap = (owner[count] - owner[k]) * HALF
            span = slice(k * HALF, (k + 1) * HALF)
            bias_early[span] = jnp.where(lead <= gap, 0.0, NEG)
            bias_late[span] = jnp.where(lead <= -gap, 0.0, NEG)


def attend_kernel(owner, query, keys, out, bias_early, bias_late):
    fill_bias(owner, bias_early, bias_late)
    early, late = key_parts(keys)
    for head in range(2):
        at = head * HEAD_DIM
        k_e, k_l = early[:, at : at + HEAD_DIM], late[:, at : at + HEAD_DIM]
        v_e, v_l = early[:, PAIR + at : PAIR + at + HEAD_DIM], late[:, PAIR + at : PAIR + at + HEAD_DIM]
        q_e, q_l = halves(query, head)
        (p_ee,) = weigh([nt(k_e, q_e) + bias_early[...]])
        p_el, p_ll = weigh([nt(k_e, q_l), nt(k_l, q_l) + bias_late[...]])
        o_e = tn(p_ee.astype(jnp.bfloat16), v_e)
        o_l = tn(p_el.astype(jnp.bfloat16), v_e) + tn(p_ll.astype(jnp.bfloat16), v_l)
        out[0, :, head * PAIR : (head + 1) * PAIR] = split_heads(o_e, o_l).astype(jnp.bfloat16)


def attend_back_kernel(
    owner, query, keys, grad, grad_query, grad_keys, bias_early, bias_late
):
    fill_bias(owner, bias_early, bias_late)
    early, late = key_parts(keys)
    scale = HEAD_DIM ** (-0.5)
    count = keys.shape[0]
    parts_e, parts_l = [], []
    for head in range(2):
        at = head * HEAD_DIM
        k_e, k_l = early[:, at : at + HEAD_DIM], late[:, at : at + HEAD_DIM]
        v_e, v_l = early[:, PAIR + at : PAIR + at + HEAD_DIM], late[:, PAIR + at : PAIR + at + HEAD_DIM]
        q_e, q_l = halves(query, head)
        d_e, d_l = halves(grad, head)
        (p_ee,) = weigh([nt(k_e, q_e) + bias_early[...]])
        p_el, p_ll = weigh([nt(k_e, q_l), nt(k_l, q_l) + bias_late[...]])
        g_ee, g_el, g_ll = nt(v_e, d_e), nt(v_e, d_l), nt(v_l, d_l)
        delta_e = jnp.sum(p_ee * g_ee, 0, keepdims=True)
        delta_l = jnp.sum(p_el * g_el, 0, keepdims=True) + jnp.sum(p_ll * g_ll, 0, keepdims=True)
        s_ee = (p_ee * (g_ee - delta_e)).astype(jnp.bfloat16)
        s_el = (p_el * (g_el - delta_l)).astype(jnp.bfloat16)
        s_ll = (p_ll * (g_ll - delta_l)).astype(jnp.bfloat16)
        gq_e = tn(s_ee, k_e) * scale
        gq_l = (tn(s_el, k_e) + tn(s_ll, k_l)) * scale
        grad_query[0, :, head * PAIR : (head + 1) * PAIR] = split_heads(gq_e, gq_l)
        gk_e = nn(s_ee, q_e) + nn(s_el, q_l)
        gk_l = nn(s_ll, q_l)
        gv_e = nn(p_ee.astype(jnp.bfloat16), d_e) + nn(p_el.astype(jnp.bfloat16), d_l)
        gv_l = nn(p_ll.astype(jnp.bfloat16), d_l)
        parts_e.append((gk_e, gv_e))
        parts_l.append((gk_l, gv_l))
    for parts, start in ((parts_e, 0), (parts_l, HALF)):
        for kind in range(2):
            joined = jnp.concatenate([parts[0][kind], parts[1][kind]], 1)
            grad_keys[:, start : start + HALF, kind * PAIR : (kind + 1) * PAIR] = (
                joined.astype(jnp.bfloat16).reshape(count, HALF, PAIR)
            )


def attend_specs(count):
    scalars = pl.BlockSpec(memory_space=pltpu.SMEM)
    rows = pl.BlockSpec((1, SEQ_TOK, 2 * PAIR), lambda s, j: (s, 0, j))
    keys = pl.BlockSpec((count, SEQ_TOK, 2 * PAIR), lambda s, j: (0, s, j))
    scratch = [pltpu.VMEM((count * HALF, SEQ_TOK), jnp.float32)] * 2
    return scalars, rows, keys, scratch


def attend(owner, query, keys):
    count = keys.shape[0]
    scalars, rows, key_rows, scratch = attend_specs(count)
    return pl.pallas_call(
        attend_kernel,
        out_shape=jax.ShapeDtypeStruct(query.shape, jnp.bfloat16),
        grid=(SEQ_GRP, KV_HEADS // 2),
        in_specs=[scalars, rows, key_rows],
        out_specs=rows,
        scratch_shapes=scratch,
        cost_estimate=pl.CostEstimate(
            flops=20 * query.size * count * SEQ_TOK,
            bytes_accessed=2 * keys.size + 4 * query.size,
            transcendentals=0,
        ),
    )(owner, query, keys)


def attend_back(owner, query, keys, grad):
    count = keys.shape[0]
    scalars, rows, key_rows, scratch = attend_specs(count)
    return pl.pallas_call(
        attend_back_kernel,
        out_shape=(
            jax.ShapeDtypeStruct(query.shape, jnp.float32),
            jax.ShapeDtypeStruct((count, SEQ_GRP * SEQ_TOK, keys.shape[2]), jnp.bfloat16),
        ),
        grid=(SEQ_GRP, KV_HEADS // 2),
        in_specs=[scalars, rows, key_rows, rows],
        out_specs=(rows, key_rows),
        scratch_shapes=scratch,
        cost_estimate=pl.CostEstimate(
            flops=30 * query.size * count * SEQ_TOK,
            bytes_accessed=4 * keys.size + 8 * query.size,
            transcendentals=0,
        ),
    )(owner, query, keys, grad)


STEP_BLOCKS = 16


def expert_kernel(
    arrived_ref,
    cot_ref,
    slot_gate_ref,
    gate_ref,
    up_ref,
    down_ref,
    produced_ref,
    back_ref,
    dots_ref,
    gate_grad_ref,
    up_grad_ref,
    down_grad_ref,
    *sums,
):
    rows = arrived_ref.shape[0] * MOST
    arrived = arrived_ref[:, 0].reshape(rows, D)
    cot = cot_ref[:, 0].reshape(rows, D)
    gate_w, up_w, down_w = gate_ref[0], up_ref[0], down_ref[0]
    gate_act = nn(arrived, gate_w)
    up_act = nn(arrived, up_w)
    sigma = jax.nn.sigmoid(gate_act)
    swish = gate_act * sigma
    hidden = (swish * up_act).astype(jnp.bfloat16)
    produced = nn(hidden, down_w).astype(jnp.bfloat16)
    produced_ref[:, 0] = produced.reshape(-1, MOST, D)
    wide = cot.astype(jnp.float32)
    dots = jnp.sum(produced.astype(jnp.float32) * wide, -1, keepdims=True)
    dots_ref[:, 0] = dots.reshape(-1, MOST, 1)
    grad_produced = (wide * slot_gate_ref[:, 0].reshape(rows, 1)).astype(jnp.bfloat16)
    grad_hidden = nt(grad_produced, down_w).astype(jnp.bfloat16).astype(jnp.float32)
    slope = sigma * (1.0 + gate_act * (1.0 - sigma))
    grad_gate = (grad_hidden * up_act * slope).astype(jnp.bfloat16)
    grad_up = (grad_hidden * swish).astype(jnp.bfloat16)
    back = nt(grad_gate, gate_w) + nt(grad_up, up_w)
    back_ref[:, 0] = back.astype(jnp.bfloat16).reshape(-1, MOST, D)
    grads = [tn(arrived, grad_gate), tn(arrived, grad_up), tn(hidden, grad_produced)]
    if sums:
        first = pl.program_id(1) == 0
        for held, grad in zip(sums, grads):
            held[...] = jnp.where(first, grad, held[...] + grad)
        grads = [held[...] for held in sums]
    quarter = gate_w.shape[1] // 4
    for k in range(4):
        span = slice(k * quarter, (k + 1) * quarter)
        gate_grad_ref[k, 0] = grads[0][:, span].astype(jnp.bfloat16)
        up_grad_ref[k, 0] = grads[1][:, span].astype(jnp.bfloat16)
        down_grad_ref[k, 0] = grads[2][span].astype(jnp.bfloat16)


def experts_pass(arrived, cot, slot_gates, gate_w, up_w, down_w):
    blocks, mine = arrived.shape[:2]
    steps = blocks // STEP_BLOCKS
    hidden = gate_w.shape[2]
    quarter = hidden // 4

    def slot_rows(width):
        return pl.BlockSpec((STEP_BLOCKS, 1, MOST, width), lambda e, c: (c, e, 0, 0))

    def per_expert(*shape):
        return pl.BlockSpec((1,) + shape, lambda e, c: (e, 0, 0))

    def pieces(*shape):
        return pl.BlockSpec((4, 1) + shape, lambda e, c: (0, e, 0, 0))

    low = jnp.bfloat16
    return pl.pallas_call(
        expert_kernel,
        grid=(mine, steps),
        in_specs=[
            slot_rows(D),
            slot_rows(D),
            slot_rows(1),
            per_expert(D, hidden),
            per_expert(D, hidden),
            per_expert(hidden, D),
        ],
        out_specs=(
            slot_rows(D),
            slot_rows(D),
            slot_rows(1),
            pieces(D, quarter),
            pieces(D, quarter),
            pieces(quarter, D),
        ),
        out_shape=(
            jax.ShapeDtypeStruct(arrived.shape, low),
            jax.ShapeDtypeStruct(arrived.shape, low),
            jax.ShapeDtypeStruct(slot_gates.shape, jnp.float32),
            jax.ShapeDtypeStruct((4, mine, D, quarter), low),
            jax.ShapeDtypeStruct((4, mine, D, quarter), low),
            jax.ShapeDtypeStruct((4, mine, quarter, D), low),
        ),
        scratch_shapes=[]
        if steps == 1
        else [
            pltpu.VMEM((D, hidden), jnp.float32),
            pltpu.VMEM((D, hidden), jnp.float32),
            pltpu.VMEM((hidden, D), jnp.float32),
        ],
        compiler_params=pltpu.CompilerParams(vmem_limit_bytes=63 * 1024 * 1024),
        cost_estimate=pl.CostEstimate(
            flops=18 * arrived.size * hidden,
            bytes_accessed=8 * arrived.size + 12 * mine * D * hidden,
            transcendentals=0,
        ),
    )(arrived, cot, slot_gates, gate_w, up_w, down_w)


def shards(
    tokens,
    routes,
    in_weight,
    out_weight,
    first_gain,
    second_gain,
    router_weight,
    gate_weight,
    up_weight,
    down_weight,
    cotangent,
):
    ctx_count = lax.axis_size("ctx")
    length = SEQ_TOK * ctx_count
    rows = SEQ_GRP * SEQ_TOK
    width_q = HEADS * HEAD_DIM
    width_k = KV_HEADS * HEAD_DIM
    my_index = lax.axis_index("ctx")
    order = ring_order(ctx_count)
    place_of = jnp.array([order.index(c) for c in range(ctx_count)], jnp.int32)
    my_place = place_of[my_index]
    table = [
        [order[(order.index(c) - k) % ctx_count] for k in range(ctx_count)] + [c]
        for c in range(ctx_count)
    ]
    owner = lax.dynamic_index_in_dim(jnp.array(table, jnp.int32), my_index, 0, False)
    local_place = dealt(my_index * SEQ_TOK + jnp.arange(SEQ_TOK, dtype=jnp.int32), length)
    upstream = cotangent.reshape(rows, D)
    chosen = jnp.any(
        routes.reshape(rows, TOP).T[:, None, :] == jnp.arange(EXPERTS, dtype=jnp.int32)[:, None], 0
    )
    gate_full, up_full, down_full = (
        lax.all_gather(gate_weight, "wsh", axis=2, tiled=True),
        lax.all_gather(up_weight, "wsh", axis=2, tiled=True),
        lax.all_gather(down_weight, "wsh", axis=1, tiled=True),
    )
    inputs = tokens.astype(jnp.float32).reshape(rows, D)
    scale_one = lax.rsqrt(jnp.mean(inputs * inputs, -1, keepdims=True) + EPS)
    normed = (inputs * scale_one * first_gain).astype(jnp.bfloat16)
    mixed = jnp.dot(normed, in_weight, preferred_element_type=jnp.float32).reshape(
        SEQ_GRP, SEQ_TOK, -1
    )
    query = rotate(
        mixed[..., :width_q].reshape(SEQ_GRP, SEQ_TOK, HEADS, HEAD_DIM), local_place, 1.0
    ).astype(jnp.bfloat16)
    query = (query * jnp.bfloat16(HEAD_DIM ** (-0.5))).reshape(SEQ_GRP, SEQ_TOK, width_q)
    key = rotate(
        mixed[..., width_q : width_q + width_k].reshape(SEQ_GRP, SEQ_TOK, KV_HEADS, HEAD_DIM),
        local_place,
        1.0,
    ).astype(jnp.bfloat16)
    value = mixed[..., width_q + width_k :].astype(jnp.bfloat16)
    pairs = (SEQ_GRP, SEQ_TOK, KV_HEADS // 2, PAIR)
    key_value = jnp.concatenate([key.reshape(pairs), value.reshape(pairs)], -1).reshape(
        rows, 2 * width_k
    )
    flags = chosen.astype(jnp.bfloat16).reshape(-1, 2 * width_k)
    flag_rows = flags.shape[0]
    flags = jnp.concatenate([flags, jnp.zeros_like(flags)], 0)
    whole = jnp.stack([held[0] for held in ring_gather([jnp.concatenate([key_value, flags], 0)])])
    whole, cot_own = lax.optimization_barrier((whole, upstream))
    cot_ring = ring_gather([cot_own])
    attended = attend(owner, query, whole)
    attended = attended.reshape(rows, width_q)
    resid = inputs + jnp.dot(attended, out_weight, preferred_element_type=jnp.float32)
    scale_two = lax.rsqrt(jnp.mean(resid * resid, -1, keepdims=True) + EPS)
    normed_two = (resid * scale_two * second_gain).astype(jnp.bfloat16)
    blocks = SEQ_GRP * ctx_count
    mine = gate_weight.shape[0]
    chosen_all = whole[:, rows : rows + flag_rows].reshape(ctx_count, EXPERTS, rows)
    chosen_my = lax.dynamic_slice_in_dim(chosen_all, my_index * mine, mine, 1)

    def by_block(values):
        split = values.reshape(ctx_count, mine, SEQ_GRP, SEQ_TOK)
        return jnp.swapaxes(split, 1, 2).reshape(blocks, mine, SEQ_TOK)

    chosen_my = by_block(chosen_my)
    before = (
        jnp.arange(SEQ_TOK, dtype=jnp.int32)[:, None] < jnp.arange(SEQ_TOK, dtype=jnp.int32)[None, :]
    ).astype(jnp.bfloat16)
    ranks = jnp.dot(
        chosen_my.reshape(blocks * mine, SEQ_TOK), before, preferred_element_type=jnp.float32
    ).reshape(blocks, mine, SEQ_TOK)
    ranks = jnp.where(chosen_my > 0, ranks, -1.0)
    normed_all = jnp.concatenate([held[0] for held in ring_gather([normed_two])])
    cot_all = jnp.concatenate([held[0] for held in cot_ring])
    logits = lax.dot_general(
        router_weight, normed_all, (((0,), (1,)), ((), ())), preferred_element_type=jnp.float32
    )
    taken = jnp.swapaxes(chosen_all, 0, 1).reshape(EXPERTS, blocks * SEQ_TOK) > 0
    picked = jnp.where(taken, logits, NEG)
    weights = jnp.where(taken, jnp.exp(picked - jnp.max(picked, 0, keepdims=True)), 0.0)
    gates_all = weights / jnp.sum(weights, 0, keepdims=True)
    gates = gates_all[:, :rows]
    gates_my = lax.dynamic_slice_in_dim(gates_all, my_index * mine, mine, 0)
    gates_my = by_block(jnp.swapaxes(gates_my.reshape(mine, ctx_count, rows), 0, 1))
    slot_ids = jnp.arange(MOST, dtype=jnp.int32).astype(jnp.float32)
    match = ranks[:, :, None, :] == slot_ids[:, None]
    chances = jnp.where(match, gates_my[:, :, None, :], 0.0)
    dispatch = match.astype(jnp.bfloat16).reshape(blocks, mine * MOST, SEQ_TOK)
    combine = chances.astype(jnp.bfloat16).reshape(blocks, mine * MOST, SEQ_TOK)
    slot_gates = jnp.sum(chances, -1, keepdims=True).astype(jnp.bfloat16).astype(jnp.float32)
    normed_blocks = normed_all.reshape(blocks, SEQ_TOK, D)
    cot_blocks = cot_all.reshape(blocks, SEQ_TOK, D)
    slot_shape = (blocks, mine, MOST, D)
    arrived, cot_slots = (
        jnp.einsum("bst,btd->bsd", dispatch, one, preferred_element_type=jnp.float32)
        .astype(jnp.bfloat16)
        .reshape(slot_shape)
        for one in (normed_blocks, cot_blocks)
    )
    produced, grad_arrived, slot_dots, gate_local, up_local, down_local = experts_pass(
        arrived, cot_slots, slot_gates, gate_full, up_full, down_full
    )
    gate_dots = jnp.sum(jnp.where(match, slot_dots, 0.0), 2)
    gate_dots = jnp.swapaxes(gate_dots.reshape(ctx_count, SEQ_GRP, mine, SEQ_TOK), 1, 2)
    ours = jnp.arange(EXPERTS, dtype=jnp.int32)[:, None] // mine == my_index
    gate_dots = jnp.where(
        ours, jnp.tile(gate_dots.reshape(ctx_count, mine, rows), (1, EXPERTS // mine, 1)), 0.0
    ).reshape(ctx_count, flag_rows, D)
    coarse = lax.reduce_precision(gate_dots, 8, 7)

    def to_tokens(matrix, slot_values):
        return jnp.einsum(
            "bst,bsd->btd",
            matrix,
            slot_values.reshape(blocks, mine * MOST, D),
            preferred_element_type=jnp.float32,
        ).astype(jnp.bfloat16).reshape(ctx_count, rows, D)

    sent_part = jnp.concatenate(
        [
            to_tokens(dispatch, grad_arrived),
            coarse.astype(jnp.bfloat16),
            (gate_dots - coarse).astype(jnp.bfloat16),
        ],
        1,
    )
    grad_sent = ring_sum(lambda k, p: sent_part[k], 1)[0]
    grad_gates = (
        grad_sent[rows : rows + flag_rows] + grad_sent[rows + flag_rows :]
    ).reshape(EXPERTS, rows)
    grad_sent = grad_sent[:rows]
    mixed_part = to_tokens(combine, produced)
    gate_grad, up_grad, down_grad = (
        lax.psum_scatter(local, "wsh", scatter_dimension=0).astype(jnp.float32)
        for local in (gate_local, up_local, down_local)
    )
    grad_logits = (gates * (grad_gates - jnp.sum(gates * grad_gates, 0, keepdims=True))).astype(
        jnp.bfloat16
    )
    router_local = lax.dot_general(
        normed_two, grad_logits, (((0,), (1,)), ((), ())), preferred_element_type=jnp.float32
    )
    grad_normed_two = grad_sent + lax.dot_general(
        grad_logits, router_weight, (((0,), (1,)), ((), ())), preferred_element_type=jnp.float32
    )
    grad_resid_norm, second_local = norm_back(resid, scale_two, second_gain, grad_normed_two)
    grad_resid = upstream.astype(jnp.float32) + grad_resid_norm
    grad_branch = grad_resid.astype(jnp.bfloat16)
    out_local = lax.dot_general(
        attended, grad_branch, (((0,), (0,)), ((), ())), preferred_element_type=jnp.float32
    )
    grad_attended = lax.dot_general(
        grad_branch, out_weight, (((1,), (1,)), ((), ())), preferred_element_type=jnp.float32
    ).astype(jnp.bfloat16)
    grad_query, grad_whole = attend_back(
        owner,
        query,
        whole,
        grad_attended.reshape(SEQ_GRP, SEQ_TOK, width_q),
    )
    grad_query = rotate(grad_query.reshape(SEQ_GRP, SEQ_TOK, HEADS, HEAD_DIM), local_place, -1.0)
    grad_query = grad_query.astype(jnp.bfloat16).reshape(rows, width_q)
    kv_grad = ring_sum(lambda k, p: grad_whole[k], 1)[0]
    in_first = lax.dot_general(
        normed, grad_query, (((0,), (0,)), ((), ())), preferred_element_type=jnp.float32
    )
    low = jnp.bfloat16
    early = spread(
        jnp.concatenate(
            [
                in_first.astype(low),
                out_local.astype(low),
                router_local.astype(low),
                second_local[:, None].astype(low),
                jnp.zeros((D, SEQ_TOK - EXPERTS - 1), low),
            ],
            -1,
        ),
    )
    mixed_part = jnp.take(mixed_part, (my_place - place_of) % ctx_count, axis=0, mode="clip")
    kv_grad, early, mixed_part = lax.optimization_barrier((kv_grad, early, mixed_part))
    mixture = lax.psum_scatter(
        mixed_part.reshape(ctx_count * rows, D), "ctx", scatter_dimension=0, tiled=True
    )
    layer_out = (
        (resid + mixture.astype(jnp.float32)).astype(jnp.bfloat16).reshape(SEQ_GRP, SEQ_TOK, D)
    )
    kv_grad = kv_grad.reshape(
        SEQ_GRP, SEQ_TOK, KV_HEADS // 2, 2, PAIR
    )
    grad_key = rotate(
        kv_grad[:, :, :, 0].reshape(SEQ_GRP, SEQ_TOK, KV_HEADS, HEAD_DIM), local_place, -1.0
    )
    grad_pair = jnp.concatenate(
        [grad_key.reshape(rows, width_k), kv_grad[:, :, :, 1].reshape(rows, width_k)], -1
    ).astype(jnp.bfloat16)
    in_second = lax.dot_general(
        normed, grad_pair, (((0,), (0,)), ((), ())), preferred_element_type=jnp.float32
    )
    grad_normed = lax.dot_general(
        grad_query, in_weight[:, :width_q], (((1,), (1,)), ((), ())), preferred_element_type=jnp.float32
    ) + lax.dot_general(
        grad_pair, in_weight[:, width_q:], (((1,), (1,)), ((), ())), preferred_element_type=jnp.float32
    )
    grad_inputs_norm, first_local = norm_back(inputs, scale_one, first_gain, grad_normed)
    tokens_grad = (grad_resid + grad_inputs_norm).astype(jnp.bfloat16).reshape(SEQ_GRP, SEQ_TOK, D)
    in_second = spread(
        jnp.concatenate(
            [in_second, jnp.broadcast_to(first_local[:, None], (D, SEQ_TOK))], -1
        ).astype(jnp.bfloat16),
    )
    in_grad = jnp.concatenate([early[:, :width_q], in_second[:, : 2 * width_k]], -1)
    first_gain_grad = in_second[:, 2 * width_k]
    out_grad = early[:, width_q : width_q + D]
    small = early[:, width_q + D :]
    router_grad = small[:, :EXPERTS]
    second_gain_grad = small[:, EXPERTS]
    return (
        layer_out,
        tokens_grad,
        in_grad,
        out_grad,
        first_gain_grad,
        second_gain_grad,
        router_grad,
        gate_grad,
        up_grad,
        down_grad,
    )


def solution(mesh):
    placed = (
        P("wsh", "ctx", None),
        P("wsh", "ctx", None),
        P(),
        P(),
        P(),
        P(),
        P(),
        P("ctx", None, "wsh"),
        P("ctx", None, "wsh"),
        P("ctx", "wsh", None),
        P("wsh", "ctx", None),
    )
    return jax.shard_map(
        shards,
        mesh=mesh,
        in_specs=placed,
        out_specs=(
            P("wsh", "ctx", None),
            P("wsh", "ctx", None),
            P(("ctx", "wsh"), None),
            P(("ctx", "wsh"), None),
            P(("ctx", "wsh")),
            P(("ctx", "wsh")),
            P(("ctx", "wsh"), None),
            P("ctx", None, "wsh"),
            P("ctx", None, "wsh"),
            P("ctx", "wsh", None),
        ),
        check_vma=False,
    )
```

```python
import jax
import jax.numpy as jnp
from jax import lax
from jax.experimental import pallas as pl
from jax.experimental.pallas import tpu as pltpu
from jax.sharding import PartitionSpec as P

D = 1024
HEADS = 16
KV_HEADS = 8
HEAD_DIM = 64
EXPERTS = 32
TOP = 8
SEQ_TOK = 128
SEQ_GRP = 2
HALF = 64
MOST = 48


EPS = 1e-05
THETA = 10000.0
NEG = -1e30


def dealt(rows, length):
    owner = rows // SEQ_TOK
    offset = rows % SEQ_TOK
    early = owner * HALF + offset
    late = length - (owner + 1) * HALF + offset - HALF
    return jnp.where(offset < HALF, early, late)


def rotate(values, place, sign):
    half_dim = values.shape[-1] // 2
    freq = THETA ** (-2.0 * jnp.arange(half_dim, dtype=jnp.float32) / values.shape[-1])
    angle = place.astype(jnp.float32)[:, None] * freq[None, :]
    cosine = jnp.cos(angle)[:, None, :]
    sine = sign * jnp.sin(angle)[:, None, :]
    front = values[..., :half_dim]
    back = values[..., half_dim:]
    return jnp.concatenate([front * cosine - back * sine, back * cosine + front * sine], -1)


def norm_back(values, scale, gain, grad_out):
    weighted = grad_out * gain
    grad_in = scale * weighted - values * scale**3 * jnp.mean(weighted * values, -1, keepdims=True)
    return (grad_in, jnp.sum(grad_out * values * scale, 0))


def ring_order(count):
    return list(range(0, count, 2)) + list(reversed(range(1, count, 2)))


def ring_shift(count, step):
    order = ring_order(count)
    return [(order[i], order[(i + step) % count]) for i in range(count)]


def ring_gather(parts):
    count = lax.axis_size("ctx")
    ahead, behind = ring_shift(count, 1), ring_shift(count, -1)
    held = [list(parts)] + [[None] * len(parts) for _ in range(count - 1)]
    far = count // 2
    for p, part in enumerate(parts):
        up, down = part, part
        ups = far if p % 2 == 0 else count - 1 - far
        for step in range(1, far + 1):
            if step <= ups:
                up = lax.ppermute(up, "ctx", ahead)
                held[step][p] = up
            if step <= count - 1 - ups:
                down = lax.ppermute(down, "ctx", behind)
                held[count - step][p] = down
    return held


def add_low(left, right):
    return (left.astype(jnp.float32) + right.astype(jnp.float32)).astype(left.dtype)


def ring_sum(block, parts):
    count = lax.axis_size("ctx")
    ahead, behind = ring_shift(count, 1), ring_shift(count, -1)
    far = count // 2
    sums = []
    for p in range(parts):
        ups = far if p % 2 == 0 else count - 1 - far
        downs = count - 1 - ups
        up = block(count - ups, p)
        for step in range(ups - 1, 0, -1):
            up = lax.ppermute(up, "ctx", ahead)
            up = add_low(up, block(count - step, p))
        up = lax.ppermute(up, "ctx", ahead)
        down = block(downs, p)
        for step in range(downs - 1, 0, -1):
            down = lax.ppermute(down, "ctx", behind)
            down = add_low(down, block(step, p))
        down = lax.ppermute(down, "ctx", behind)
        own = block(0, p).astype(jnp.float32)
        sums.append(up.astype(jnp.float32) + down.astype(jnp.float32) + own)
    return sums


def spread(local):
    for axis in ("wsh", "ctx"):
        count = lax.axis_size(axis)
        me = lax.axis_index(axis)
        outer = lax.axis_size("ctx") if axis == "wsh" else 1
        bit = 1
        while bit < count:
            split = local.reshape(outer * (count // (2 * bit)), 2, -1, local.shape[-1])
            mine = (me // bit) % 2
            swap = [(i, i ^ bit) for i in range(count)]
            sent = lax.dynamic_index_in_dim(split, 1 - mine, 1, False)
            sent = lax.ppermute(sent, axis, swap)
            kept = lax.dynamic_index_in_dim(split, mine, 1, False)
            local = add_low(kept, sent).reshape(-1, local.shape[-1])
            bit *= 2
    return local.astype(jnp.float32)


PAIR = 2 * HEAD_DIM


def nt(left, right):
    return lax.dot_general(left, right, (((1,), (1,)), ((), ())), preferred_element_type=jnp.float32)


def tn(left, right):
    return lax.dot_general(left, right, (((0,), (0,)), ((), ())), preferred_element_type=jnp.float32)


def nn(left, right):
    return jnp.dot(left, right, preferred_element_type=jnp.float32)


def halves(ref, head):
    start = head * PAIR
    block = ref[0, :, start : start + PAIR]
    both = [block[:, :HEAD_DIM], block[:, HEAD_DIM:]]
    return (
        jnp.concatenate([one[:HALF] for one in both], 0),
        jnp.concatenate([one[HALF:] for one in both], 0),
    )


def key_parts(ref):
    whole = ref[...]
    count = whole.shape[0]
    early = whole[:, :HALF].reshape(count * HALF, -1)
    late = whole[:, HALF:].reshape(count * HALF, -1)
    return early, late


def weigh(scores):
    peak = jnp.max(scores[0], 0, keepdims=True)
    for more in scores[1:]:
        peak = jnp.maximum(peak, jnp.max(more, 0, keepdims=True))
    powers = [jnp.exp(part - peak) for part in scores]
    total = sum(jnp.sum(part, 0, keepdims=True) for part in powers)
    inverse = 1.0 / total
    return [part * inverse for part in powers]


def split_heads(stacked_early, stacked_late):
    return jnp.concatenate(
        [
            jnp.concatenate([stacked_early[:HALF], stacked_early[HALF:]], 1),
            jnp.concatenate([stacked_late[:HALF], stacked_late[HALF:]], 1),
        ],
        0,
    )


def fill_bias(owner, bias_early, bias_late):
    count = owner.shape[0] - 1

    @pl.when((pl.program_id(0) == 0) & (pl.program_id(1) == 0))
    def fill():
        lead = lax.broadcasted_iota(jnp.int32, (HALF, SEQ_TOK), 0) - (
            lax.broadcasted_iota(jnp.int32, (HALF, SEQ_TOK), 1) % HALF
        )
        for k in range(count):
            gap = (owner[count] - owner[k]) * HALF
            span = slice(k * HALF, (k + 1) * HALF)
            bias_early[span] = jnp.where(lead <= gap, 0.0, NEG)
            bias_late[span] = jnp.where(lead <= -gap, 0.0, NEG)


def attend_kernel(owner, query, keys, out, bias_early, bias_late):
    fill_bias(owner, bias_early, bias_late)
    early, late = key_parts(keys)
    for head in range(2):
        at = head * HEAD_DIM
        k_e, k_l = early[:, at : at + HEAD_DIM], late[:, at : at + HEAD_DIM]
        v_e, v_l = early[:, PAIR + at : PAIR + at + HEAD_DIM], late[:, PAIR + at : PAIR + at + HEAD_DIM]
        q_e, q_l = halves(query, head)
        (p_ee,) = weigh([nt(k_e, q_e) + bias_early[...]])
        p_el, p_ll = weigh([nt(k_e, q_l), nt(k_l, q_l) + bias_late[...]])
        o_e = tn(p_ee.astype(jnp.bfloat16), v_e)
        o_l = tn(p_el.astype(jnp.bfloat16), v_e) + tn(p_ll.astype(jnp.bfloat16), v_l)
        out[0, :, head * PAIR : (head + 1) * PAIR] = split_heads(o_e, o_l).astype(jnp.bfloat16)


def attend_back_kernel(
    owner, query, keys, grad, grad_query, grad_keys, bias_early, bias_late
):
    fill_bias(owner, bias_early, bias_late)
    early, late = key_parts(keys)
    scale = HEAD_DIM ** (-0.5)
    count = keys.shape[0]
    parts_e, parts_l = [], []
    for head in range(2):
        at = head * HEAD_DIM
        k_e, k_l = early[:, at : at + HEAD_DIM], late[:, at : at + HEAD_DIM]
        v_e, v_l = early[:, PAIR + at : PAIR + at + HEAD_DIM], late[:, PAIR + at : PAIR + at + HEAD_DIM]
        q_e, q_l = halves(query, head)
        d_e, d_l = halves(grad, head)
        (p_ee,) = weigh([nt(k_e, q_e) + bias_early[...]])
        p_el, p_ll = weigh([nt(k_e, q_l), nt(k_l, q_l) + bias_late[...]])
        g_ee, g_el, g_ll = nt(v_e, d_e), nt(v_e, d_l), nt(v_l, d_l)
        delta_e = jnp.sum(p_ee * g_ee, 0, keepdims=True)
        delta_l = jnp.sum(p_el * g_el, 0, keepdims=True) + jnp.sum(p_ll * g_ll, 0, keepdims=True)
        s_ee = (p_ee * (g_ee - delta_e)).astype(jnp.bfloat16)
        s_el = (p_el * (g_el - delta_l)).astype(jnp.bfloat16)
        s_ll = (p_ll * (g_ll - delta_l)).astype(jnp.bfloat16)
        gq_e = tn(s_ee, k_e) * scale
        gq_l = (tn(s_el, k_e) + tn(s_ll, k_l)) * scale
        grad_query[0, :, head * PAIR : (head + 1) * PAIR] = split_heads(gq_e, gq_l)
        gk_e = nn(s_ee, q_e) + nn(s_el, q_l)
        gk_l = nn(s_ll, q_l)
        gv_e = nn(p_ee.astype(jnp.bfloat16), d_e) + nn(p_el.astype(jnp.bfloat16), d_l)
        gv_l = nn(p_ll.astype(jnp.bfloat16), d_l)
        parts_e.append((gk_e, gv_e))
        parts_l.append((gk_l, gv_l))
    for parts, start in ((parts_e, 0), (parts_l, HALF)):
        for kind in range(2):
            joined = jnp.concatenate([parts[0][kind], parts[1][kind]], 1)
            grad_keys[:, start : start + HALF, kind * PAIR : (kind + 1) * PAIR] = (
                joined.astype(jnp.bfloat16).reshape(count, HALF, PAIR)
            )


def attend_specs(count):
    scalars = pl.BlockSpec(memory_space=pltpu.SMEM)
    rows = pl.BlockSpec((1, SEQ_TOK, 2 * PAIR), lambda s, j: (s, 0, j))
    keys = pl.BlockSpec((count, SEQ_TOK, 2 * PAIR), lambda s, j: (0, s, j))
    scratch = [pltpu.VMEM((count * HALF, SEQ_TOK), jnp.float32)] * 2
    return scalars, rows, keys, scratch


def attend(owner, query, keys):
    count = keys.shape[0]
    scalars, rows, key_rows, scratch = attend_specs(count)
    return pl.pallas_call(
        attend_kernel,
        out_shape=jax.ShapeDtypeStruct(query.shape, jnp.bfloat16),
        grid=(SEQ_GRP, KV_HEADS // 2),
        in_specs=[scalars, rows, key_rows],
        out_specs=rows,
        scratch_shapes=scratch,
        cost_estimate=pl.CostEstimate(
            flops=20 * query.size * count * SEQ_TOK,
            bytes_accessed=2 * keys.size + 4 * query.size,
            transcendentals=0,
        ),
    )(owner, query, keys)


def attend_back(owner, query, keys, grad):
    count = keys.shape[0]
    scalars, rows, key_rows, scratch = attend_specs(count)
    return pl.pallas_call(
        attend_back_kernel,
        out_shape=(
            jax.ShapeDtypeStruct(query.shape, jnp.float32),
            jax.ShapeDtypeStruct((count, SEQ_GRP * SEQ_TOK, keys.shape[2]), jnp.bfloat16),
        ),
        grid=(SEQ_GRP, KV_HEADS // 2),
        in_specs=[scalars, rows, key_rows, rows],
        out_specs=(rows, key_rows),
        scratch_shapes=scratch,
        cost_estimate=pl.CostEstimate(
            flops=30 * query.size * count * SEQ_TOK,
            bytes_accessed=4 * keys.size + 8 * query.size,
            transcendentals=0,
        ),
    )(owner, query, keys, grad)


STEP_BLOCKS = 16


def expert_kernel(
    arrived_ref,
    cot_ref,
    slot_gate_ref,
    gate_ref,
    up_ref,
    down_ref,
    produced_ref,
    back_ref,
    dots_ref,
    gate_grad_ref,
    up_grad_ref,
    down_grad_ref,
    *sums,
):
    rows = arrived_ref.shape[0] * MOST
    arrived = arrived_ref[:, 0].reshape(rows, D)
    cot = cot_ref[:, 0].reshape(rows, D)
    gate_w, up_w, down_w = gate_ref[0], up_ref[0], down_ref[0]
    gate_act = nn(arrived, gate_w)
    up_act = nn(arrived, up_w)
    sigma = jax.nn.sigmoid(gate_act)
    swish = gate_act * sigma
    hidden = (swish * up_act).astype(jnp.bfloat16)
    produced = nn(hidden, down_w).astype(jnp.bfloat16)
    produced_ref[:, 0] = produced.reshape(-1, MOST, D)
    wide = cot.astype(jnp.float32)
    dots = jnp.sum(produced.astype(jnp.float32) * wide, -1, keepdims=True)
    dots_ref[:, 0] = dots.reshape(-1, MOST, 1)
    grad_produced = (wide * slot_gate_ref[:, 0].reshape(rows, 1)).astype(jnp.bfloat16)
    grad_hidden = nt(grad_produced, down_w).astype(jnp.bfloat16).astype(jnp.float32)
    slope = sigma * (1.0 + gate_act * (1.0 - sigma))
    grad_gate = (grad_hidden * up_act * slope).astype(jnp.bfloat16)
    grad_up = (grad_hidden * swish).astype(jnp.bfloat16)
    back = nt(grad_gate, gate_w) + nt(grad_up, up_w)
    back_ref[:, 0] = back.astype(jnp.bfloat16).reshape(-1, MOST, D)
    grads = [tn(arrived, grad_gate), tn(arrived, grad_up), tn(hidden, grad_produced)]
    if sums:
        first = pl.program_id(1) == 0
        for held, grad in zip(sums, grads):
            held[...] = jnp.where(first, grad, held[...] + grad)
        grads = [held[...] for held in sums]
    quarter = gate_w.shape[1] // 4
    for k in range(4):
        span = slice(k * quarter, (k + 1) * quarter)
        gate_grad_ref[k, 0] = grads[0][:, span].astype(jnp.bfloat16)
        up_grad_ref[k, 0] = grads[1][:, span].astype(jnp.bfloat16)
        down_grad_ref[k, 0] = grads[2][span].astype(jnp.bfloat16)


def experts_pass(arrived, cot, slot_gates, gate_w, up_w, down_w):
    blocks, mine = arrived.shape[:2]
    steps = blocks // STEP_BLOCKS
    hidden = gate_w.shape[2]
    quarter = hidden // 4

    def slot_rows(width):
        return pl.BlockSpec((STEP_BLOCKS, 1, MOST, width), lambda e, c: (c, e, 0, 0))

    def per_expert(*shape):
        return pl.BlockSpec((1,) + shape, lambda e, c: (e, 0, 0))

    def pieces(*shape):
        return pl.BlockSpec((4, 1) + shape, lambda e, c: (0, e, 0, 0))

    low = jnp.bfloat16
    return pl.pallas_call(
        expert_kernel,
        grid=(mine, steps),
        in_specs=[
            slot_rows(D),
            slot_rows(D),
            slot_rows(1),
            per_expert(D, hidden),
            per_expert(D, hidden),
            per_expert(hidden, D),
        ],
        out_specs=(
            slot_rows(D),
            slot_rows(D),
            slot_rows(1),
            pieces(D, quarter),
            pieces(D, quarter),
            pieces(quarter, D),
        ),
        out_shape=(
            jax.ShapeDtypeStruct(arrived.shape, low),
            jax.ShapeDtypeStruct(arrived.shape, low),
            jax.ShapeDtypeStruct(slot_gates.shape, jnp.float32),
            jax.ShapeDtypeStruct((4, mine, D, quarter), low),
            jax.ShapeDtypeStruct((4, mine, D, quarter), low),
            jax.ShapeDtypeStruct((4, mine, quarter, D), low),
        ),
        scratch_shapes=[]
        if steps == 1
        else [
            pltpu.VMEM((D, hidden), jnp.float32),
            pltpu.VMEM((D, hidden), jnp.float32),
            pltpu.VMEM((hidden, D), jnp.float32),
        ],
        compiler_params=pltpu.CompilerParams(vmem_limit_bytes=63 * 1024 * 1024),
        cost_estimate=pl.CostEstimate(
            flops=18 * arrived.size * hidden,
            bytes_accessed=8 * arrived.size + 12 * mine * D * hidden,
            transcendentals=0,
        ),
    )(arrived, cot, slot_gates, gate_w, up_w, down_w)


def shards(
    tokens,
    routes,
    in_weight,
    out_weight,
    first_gain,
    second_gain,
    router_weight,
    gate_weight,
    up_weight,
    down_weight,
    cotangent,
):
    ctx_count = lax.axis_size("ctx")
    length = SEQ_TOK * ctx_count
    rows = SEQ_GRP * SEQ_TOK
    width_q = HEADS * HEAD_DIM
    width_k = KV_HEADS * HEAD_DIM
    my_index = lax.axis_index("ctx")
    order = ring_order(ctx_count)
    place_of = jnp.array([order.index(c) for c in range(ctx_count)], jnp.int32)
    table = [
        [order[(order.index(c) - k) % ctx_count] for k in range(ctx_count)] + [c]
        for c in range(ctx_count)
    ]
    owner = lax.dynamic_index_in_dim(jnp.array(table, jnp.int32), my_index, 0, False)
    local_place = dealt(my_index * SEQ_TOK + jnp.arange(SEQ_TOK, dtype=jnp.int32), length)
    upstream = cotangent.reshape(rows, D)
    chosen = jnp.any(
        routes.reshape(rows, TOP).T[:, None, :] == jnp.arange(EXPERTS, dtype=jnp.int32)[:, None], 0
    )
    gate_full, up_full, down_full = (
        lax.all_gather(gate_weight, "wsh", axis=2, tiled=True),
        lax.all_gather(up_weight, "wsh", axis=2, tiled=True),
        lax.all_gather(down_weight, "wsh", axis=1, tiled=True),
    )
    inputs = tokens.astype(jnp.float32).reshape(rows, D)
    scale_one = lax.rsqrt(jnp.mean(inputs * inputs, -1, keepdims=True) + EPS)
    normed = (inputs * scale_one * first_gain).astype(jnp.bfloat16)
    mixed = jnp.dot(normed, in_weight, preferred_element_type=jnp.float32).reshape(
        SEQ_GRP, SEQ_TOK, -1
    )
    query = rotate(
        mixed[..., :width_q].reshape(SEQ_GRP, SEQ_TOK, HEADS, HEAD_DIM), local_place, 1.0
    ).astype(jnp.bfloat16)
    query = (query * jnp.bfloat16(HEAD_DIM ** (-0.5))).reshape(SEQ_GRP, SEQ_TOK, width_q)
    key = rotate(
        mixed[..., width_q : width_q + width_k].reshape(SEQ_GRP, SEQ_TOK, KV_HEADS, HEAD_DIM),
        local_place,
        1.0,
    ).astype(jnp.bfloat16)
    value = mixed[..., width_q + width_k :].astype(jnp.bfloat16)
    pairs = (SEQ_GRP, SEQ_TOK, KV_HEADS // 2, PAIR)
    key_value = jnp.concatenate([key.reshape(pairs), value.reshape(pairs)], -1).reshape(
        rows, 2 * width_k
    )
    flags = chosen.astype(jnp.bfloat16).reshape(-1, 2 * width_k)
    flag_rows = flags.shape[0]
    flags = jnp.concatenate([flags, jnp.zeros_like(flags)], 0)
    whole = jnp.stack([held[0] for held in ring_gather([jnp.concatenate([key_value, flags], 0)])])
    whole, cot_own = lax.optimization_barrier((whole, upstream))
    cot_ring = ring_gather([cot_own])
    attended = attend(owner, query, whole)
    attended = attended.reshape(rows, width_q)
    resid = inputs + jnp.dot(attended, out_weight, preferred_element_type=jnp.float32)
    scale_two = lax.rsqrt(jnp.mean(resid * resid, -1, keepdims=True) + EPS)
    normed_two = (resid * scale_two * second_gain).astype(jnp.bfloat16)
    blocks = SEQ_GRP * ctx_count
    mine = gate_weight.shape[0]
    chosen_all = whole[:, rows : rows + flag_rows].reshape(ctx_count, EXPERTS, rows)
    chosen_my = lax.dynamic_slice_in_dim(chosen_all, my_index * mine, mine, 1)

    def by_block(values):
        split = values.reshape(ctx_count, mine, SEQ_GRP, SEQ_TOK)
        return jnp.swapaxes(split, 1, 2).reshape(blocks, mine, SEQ_TOK)

    chosen_my = by_block(chosen_my)
    before = (
        jnp.arange(SEQ_TOK, dtype=jnp.int32)[:, None] < jnp.arange(SEQ_TOK, dtype=jnp.int32)[None, :]
    ).astype(jnp.bfloat16)
    ranks = jnp.dot(
        chosen_my.reshape(blocks * mine, SEQ_TOK), before, preferred_element_type=jnp.float32
    ).reshape(blocks, mine, SEQ_TOK)
    ranks = jnp.where(chosen_my > 0, ranks, -1.0)
    normed_all = jnp.concatenate([held[0] for held in ring_gather([normed_two])])
    cot_all = jnp.concatenate([held[0] for held in cot_ring])
    logits = lax.dot_general(
        router_weight, normed_all, (((0,), (1,)), ((), ())), preferred_element_type=jnp.float32
    )
    taken = jnp.swapaxes(chosen_all, 0, 1).reshape(EXPERTS, blocks * SEQ_TOK) > 0
    picked = jnp.where(taken, logits, NEG)
    weights = jnp.where(taken, jnp.exp(picked - jnp.max(picked, 0, keepdims=True)), 0.0)
    gates_all = weights / jnp.sum(weights, 0, keepdims=True)
    gates = gates_all[:, :rows]
    gates_my = lax.dynamic_slice_in_dim(gates_all, my_index * mine, mine, 0)
    gates_my = by_block(jnp.swapaxes(gates_my.reshape(mine, ctx_count, rows), 0, 1))
    slot_ids = jnp.arange(MOST, dtype=jnp.int32).astype(jnp.float32)
    match = ranks[:, :, None, :] == slot_ids[:, None]
    chances = jnp.where(match, gates_my[:, :, None, :], 0.0)
    dispatch = match.astype(jnp.bfloat16).reshape(blocks, mine * MOST, SEQ_TOK)
    combine = chances.astype(jnp.bfloat16).reshape(blocks, mine * MOST, SEQ_TOK)
    slot_gates = jnp.sum(chances, -1, keepdims=True).astype(jnp.bfloat16).astype(jnp.float32)
    normed_blocks = normed_all.reshape(blocks, SEQ_TOK, D)
    cot_blocks = cot_all.reshape(blocks, SEQ_TOK, D)
    slot_shape = (blocks, mine, MOST, D)
    arrived, cot_slots = (
        jnp.einsum("bst,btd->bsd", dispatch, one, preferred_element_type=jnp.float32)
        .astype(jnp.bfloat16)
        .reshape(slot_shape)
        for one in (normed_blocks, cot_blocks)
    )
    produced, grad_arrived, slot_dots, gate_local, up_local, down_local = experts_pass(
        arrived, cot_slots, slot_gates, gate_full, up_full, down_full
    )
    gate_dots = jnp.sum(jnp.where(match, slot_dots, 0.0), 2)
    gate_dots = jnp.swapaxes(gate_dots.reshape(ctx_count, SEQ_GRP, mine, SEQ_TOK), 1, 2)
    ours = jnp.arange(EXPERTS, dtype=jnp.int32)[:, None] // mine == my_index
    gate_dots = jnp.where(
        ours, jnp.tile(gate_dots.reshape(ctx_count, mine, rows), (1, EXPERTS // mine, 1)), 0.0
    ).reshape(ctx_count, flag_rows, D)
    coarse = lax.reduce_precision(gate_dots, 8, 7)

    def to_tokens(matrix, slot_values):
        return jnp.einsum(
            "bst,bsd->btd",
            matrix,
            slot_values.reshape(blocks, mine * MOST, D),
            preferred_element_type=jnp.float32,
        ).astype(jnp.bfloat16).reshape(ctx_count, rows, D)

    sent_part = jnp.concatenate(
        [
            to_tokens(dispatch, grad_arrived),
            coarse.astype(jnp.bfloat16),
            (gate_dots - coarse).astype(jnp.bfloat16),
        ],
        1,
    )
    grad_sent = ring_sum(lambda k, p: sent_part[k], 1)[0]
    grad_gates = (
        grad_sent[rows : rows + flag_rows] + grad_sent[rows + flag_rows :]
    ).reshape(EXPERTS, rows)
    grad_sent = grad_sent[:rows]
    mixed_part = to_tokens(combine, produced)
    mixture = ring_sum(lambda k, p: mixed_part[k], 1)[0]
    grad_sent, mixture = lax.optimization_barrier((grad_sent, mixture))
    layer_out = (resid + mixture).astype(jnp.bfloat16).reshape(SEQ_GRP, SEQ_TOK, D)
    gate_grad, up_grad, down_grad = (
        lax.psum_scatter(local, "wsh", scatter_dimension=0).astype(jnp.float32)
        for local in (gate_local, up_local, down_local)
    )
    grad_logits = (gates * (grad_gates - jnp.sum(gates * grad_gates, 0, keepdims=True))).astype(
        jnp.bfloat16
    )
    router_local = lax.dot_general(
        normed_two, grad_logits, (((0,), (1,)), ((), ())), preferred_element_type=jnp.float32
    )
    grad_normed_two = grad_sent + lax.dot_general(
        grad_logits, router_weight, (((0,), (1,)), ((), ())), preferred_element_type=jnp.float32
    )
    grad_resid_norm, second_local = norm_back(resid, scale_two, second_gain, grad_normed_two)
    grad_resid = upstream.astype(jnp.float32) + grad_resid_norm
    grad_branch = grad_resid.astype(jnp.bfloat16)
    out_local = lax.dot_general(
        attended, grad_branch, (((0,), (0,)), ((), ())), preferred_element_type=jnp.float32
    )
    grad_attended = lax.dot_general(
        grad_branch, out_weight, (((1,), (1,)), ((), ())), preferred_element_type=jnp.float32
    ).astype(jnp.bfloat16)
    grad_query, grad_whole = attend_back(
        owner,
        query,
        whole,
        grad_attended.reshape(SEQ_GRP, SEQ_TOK, width_q),
    )
    grad_query = rotate(grad_query.reshape(SEQ_GRP, SEQ_TOK, HEADS, HEAD_DIM), local_place, -1.0)
    grad_query = grad_query.astype(jnp.bfloat16).reshape(rows, width_q)
    kv_grad = ring_sum(lambda k, p: grad_whole[k], 1)[0]
    in_first = lax.dot_general(
        normed, grad_query, (((0,), (0,)), ((), ())), preferred_element_type=jnp.float32
    )
    low = jnp.bfloat16
    early = spread(
        jnp.concatenate(
            [
                in_first.astype(low),
                out_local.astype(low),
                router_local.astype(low),
                second_local[:, None].astype(low),
                jnp.zeros((D, SEQ_TOK - EXPERTS - 1), low),
            ],
            -1,
        ),
    )
    kv_grad, early = lax.optimization_barrier((kv_grad, early))
    kv_grad = kv_grad.reshape(
        SEQ_GRP, SEQ_TOK, KV_HEADS // 2, 2, PAIR
    )
    grad_key = rotate(
        kv_grad[:, :, :, 0].reshape(SEQ_GRP, SEQ_TOK, KV_HEADS, HEAD_DIM), local_place, -1.0
    )
    grad_pair = jnp.concatenate(
        [grad_key.reshape(rows, width_k), kv_grad[:, :, :, 1].reshape(rows, width_k)], -1
    ).astype(jnp.bfloat16)
    in_second = lax.dot_general(
        normed, grad_pair, (((0,), (0,)), ((), ())), preferred_element_type=jnp.float32
    )
    grad_normed = lax.dot_general(
        grad_query, in_weight[:, :width_q], (((1,), (1,)), ((), ())), preferred_element_type=jnp.float32
    ) + lax.dot_general(
        grad_pair, in_weight[:, width_q:], (((1,), (1,)), ((), ())), preferred_element_type=jnp.float32
    )
    grad_inputs_norm, first_local = norm_back(inputs, scale_one, first_gain, grad_normed)
    tokens_grad = (grad_resid + grad_inputs_norm).astype(jnp.bfloat16).reshape(SEQ_GRP, SEQ_TOK, D)
    in_second = spread(
        jnp.concatenate(
            [in_second, jnp.broadcast_to(first_local[:, None], (D, SEQ_TOK))], -1
        ).astype(jnp.bfloat16),
    )
    in_grad = jnp.concatenate([early[:, :width_q], in_second[:, : 2 * width_k]], -1)
    first_gain_grad = in_second[:, 2 * width_k]
    out_grad = early[:, width_q : width_q + D]
    small = early[:, width_q + D :]
    router_grad = small[:, :EXPERTS]
    second_gain_grad = small[:, EXPERTS]
    return (
        layer_out,
        tokens_grad,
        in_grad,
        out_grad,
        first_gain_grad,
        second_gain_grad,
        router_grad,
        gate_grad,
        up_grad,
        down_grad,
    )


def solution(mesh):
    placed = (
        P("wsh", "ctx", None),
        P("wsh", "ctx", None),
        P(),
        P(),
        P(),
        P(),
        P(),
        P("ctx", None, "wsh"),
        P("ctx", None, "wsh"),
        P("ctx", "wsh", None),
        P("wsh", "ctx", None),
    )
    return jax.shard_map(
        shards,
        mesh=mesh,
        in_specs=placed,
        out_specs=(
            P("wsh", "ctx", None),
            P("wsh", "ctx", None),
            P(("ctx", "wsh"), None),
            P(("ctx", "wsh"), None),
            P(("ctx", "wsh")),
            P(("ctx", "wsh")),
            P(("ctx", "wsh"), None),
            P("ctx", None, "wsh"),
            P("ctx", None, "wsh"),
            P("ctx", "wsh", None),
        ),
        check_vma=False,
    )
```
